32 devices in a mesh: dev: 32 (over z, y, x, core).
Axes of the slice: x: 2, y: 2, z: 4, core: 2. Of those that a mesh axis runs over, the one named last changes fastest.
Arguments:
- runs_field: float32 [512, 256, 256], P('dev'), may hold values from -6 to 6
- spectral_filter: float32 [256, 129], replicated, may hold values from 0.3 to 3, as said below
- block_inverses: float32 [2, 256, 256], replicated, may hold values from -1.5 to 1.5, as said below
- factor_panels: float32 [2, 512, 256], P(None, 'dev'), may hold values from -0.375 to 0.375
Outputs:
- solved: float32 [512, 65536], P(None, 'dev')
The draws below stay inside these ranges and needn't reach their ends.
Inputs may be any that keep to these rules, and one draw needn't show every extreme that they name: `spectral_filter`: symmetric under the first frequency index k -> (256 - k) mod 256 in columns 0 and 128. `block_inverses`: each block is lower triangular with diagonal entries from 0.7 to 1.4.
All inputs are finite; a program needn't handle non-finite values.
Results may differ from the reference program's by a relative error of at most 0.000076.
Values sent between devices are 32-bit elements; how exact they have to be, the bound alone decides.
No kernel may reach another device: no remote copies, remote signals or barrier semaphores. Data moves between devices by JAX's collectives and lax.ppermute only.
A program may use at most 64 MiB of HBM per device.

```python
import jax
import jax.numpy as jnp
from jax import lax

GRID = 256
PANEL = 256
RUNS = 512
HALF = 129


def draw_spectral_filter(key, part):
    logs = jax.random.uniform(key, (GRID, HALF), jnp.float32, jnp.log(0.3), jnp.log(3.0))
    mirrored = jnp.roll(jnp.flip(logs, 0), 1, 0)
    column = jnp.arange(HALF, dtype=jnp.int32)[None, :]
    edges = (column == 0) | (column == HALF - 1)
    logs = jnp.where(edges, 0.5 * (logs + mirrored), logs)
    return jnp.exp(logs).astype(jnp.float32)


def draw_block_inverses(key, part):
    key_low, key_diag = jax.random.split(key)
    rows = jnp.arange(PANEL, dtype=jnp.int32)[:, None]
    cols = jnp.arange(PANEL, dtype=jnp.int32)[None, :]
    lower = (rows > cols).astype(jnp.float32)
    below = jax.random.truncated_normal(key_low, -3.0, 3.0, (2, PANEL, PANEL), jnp.float32)
    diagonal = jax.random.uniform(key_diag, (2, PANEL), jnp.float32, 0.7, 1.4)
    eye = (rows == cols).astype(jnp.float32)
    blocks = below * lower * (0.6 / PANEL ** 0.5) + diagonal[:, :, None] * eye
    return blocks.astype(jnp.float32)


def level_of(rng, extent, cuts, smallest, largest):
    factor_of = 1.0
    for dim, shards_of in cuts:
        steps = jax.random.uniform(jax.random.fold_in(jax.random.fold_in(rng, 6), dim), (shards_of,), jnp.float32, smallest / len(cuts), largest / len(cuts))
        factor_of = factor_of * jnp.repeat(jnp.exp(steps), extent[dim] // shards_of).reshape((-1,) + (1,) * (len(extent) - 1 - dim))
    return factor_of


def centred(own_key, extent, scale, limit, shards=(), kind=jnp.bfloat16):
    gain = level_of(own_key, extent, shards, -0.22, 0.18) if shards else 1.0
    result = jax.random.normal(own_key, extent, jnp.float32) * scale * gain
    return jnp.minimum(jnp.maximum(result, -limit), limit).astype(kind)


def setup_inputs(seed: int = 0) -> dict:
    streams_of = jax.random.split(jax.random.key(seed), 5)
    return {
        "runs_field": centred(streams_of[0], (RUNS, GRID, GRID), 1.0, 6.0, ((0, 32),), jnp.float32),
        "spectral_filter": draw_spectral_filter(jax.random.fold_in(streams_of[4], 71), 0),
        "block_inverses": draw_block_inverses(jax.random.fold_in(streams_of[4], 71), 0),
        "factor_panels": centred(streams_of[3], (2, RUNS, PANEL), PANEL ** -0.5, 0.375, ((1, 32),), jnp.float32),
    }


def reference(runs_field, spectral_filter, block_inverses, factor_panels):
    precise = lax.Precision.HIGHEST

    def whiten_one(one_run):
        spectrum = jnp.fft.rfft2(one_run) * spectral_filter
        return jnp.fft.irfft2(spectrum, s=(GRID, GRID)).astype(jnp.float32)

    whitened = lax.map(whiten_one, runs_field).reshape(RUNS, GRID * GRID)
    first = jnp.dot(block_inverses[0], whitened[:PANEL], precision=precise, preferred_element_type=jnp.float32)
    remain_one = whitened[PANEL:] - jnp.dot(factor_panels[0, PANEL:], first, precision=precise, preferred_element_type=jnp.float32)
    second = jnp.dot(block_inverses[1], remain_one[:PANEL], precision=precise, preferred_element_type=jnp.float32)
    remain_two = remain_one[PANEL:] - jnp.dot(factor_panels[1, 2 * PANEL:], second, precision=precise, preferred_element_type=jnp.float32)
    return jnp.concatenate([first, second, remain_two], axis=0)
```

```python
import functools, math
LANES = 128
import numpy as np
import jax, jax.numpy as jnp
from jax import lax
from jax.experimental import pallas as pl
from jax.experimental.pallas import tpu as pltpu
from jax.sharding import PartitionSpec as P

def basis(length):
    half = length // 2
    slot = np.arange(length)
    freq = np.where(slot <= half, slot, slot - half)
    phase = np.outer(np.arange(length), freq) % length
    angle = phase * (2.0 * math.pi / length)
    table = np.where(slot[None, :] <= half, np.cos(angle), np.sin(angle))
    hi = table.astype(jnp.bfloat16)
    lo = (table - hi.astype(np.float64)).astype(jnp.bfloat16)
    return hi, lo

def split(x):
    hi = x.astype(jnp.bfloat16)
    lo = (x - hi.astype(jnp.float32)).astype(jnp.bfloat16)
    return hi, lo

def mm(a, b):
    return lax.dot_general(a, b, (((1,), (0,)), ((), ())), preferred_element_type=jnp.float32)

def gains(filter_t, length):
    half = length // 2
    row = lax.broadcasted_iota(jnp.int32, (length, length), 0)
    col = lax.broadcasted_iota(jnp.int32, (length, length), 1)
    freq = jnp.where(row <= half, row, row - half)
    edge = (freq == 0) | (freq == half)
    plus = (col == freq).astype(jnp.float32)
    minus = (col == length - freq).astype(jnp.float32)
    minus = jnp.where(edge, 0.0, minus)
    plus_only = jnp.where(edge, 0.0, plus)
    sums = (plus + minus).astype(jnp.bfloat16)
    diffs = (plus_only - minus).astype(jnp.bfloat16)
    low = filter_t[:half]
    k = lax.broadcasted_iota(jnp.int32, (half, length), 0)
    high = jnp.where(k == 0, jnp.broadcast_to(filter_t[half:half + 1], (half, length)), low)
    def pick(sel, table):
        out = None
        rest = table
        for _ in range(3):
            piece = rest.astype(jnp.bfloat16)
            rest = rest - piece.astype(jnp.float32)
            part = lax.dot_general(sel, piece, (((1,), (1,)), ((), ())), preferred_element_type=jnp.float32)
            out = part if out is None else out + part
        return out
    tab = jnp.concatenate([low, high], axis=0)
    s = pick(sums, tab)
    d = pick(diffs, tab)
    kk = jnp.where(col <= half, col, col - half)
    kedge = (kk == 0) | (kk == half)
    scale = 1.0 / float(length * length)
    s = s * jnp.where(kedge, scale, 2.0 * scale)
    same = (row < half) == (col < half)
    d = d * jnp.where(kedge, 0.0, jnp.where(same, -2.0 * scale, 2.0 * scale))
    return s, d

def whiten_kernel(x_ref, ft_ref, fh_ref, fl_ref, th_ref, tl_ref, o_ref, g1_ref, g2_ref, *, rb, groups):
    length = x_ref.shape[1]
    half = length // 2
    @pl.when(pl.program_id(0) == 0)
    def _():
        s, d = gains(ft_ref[...], length)
        g1_ref[...] = s
        g2_ref[...] = d
    fh = fh_ref[...]; fl = fl_ref[...]; th = th_ref[...]; tl = tl_ref[...]
    def right(x, h, l):
        xh, xl = split(x)
        return mm(xh, h) + mm(xh, l) + mm(xl, h)
    def left(h, l, x):
        xh, xl = split(x)
        return mm(h, xh) + mm(l, xh) + mm(h, xl)
    z = right(x_ref[...].reshape(rb * length, length), fh, fl)
    vs = []
    for r in range(rb):
        t = left(th, tl, z[r * length:(r + 1) * length])
        sw = jnp.concatenate([
            jnp.concatenate([t[half:, half:], t[half:, :half]], axis=1),
            jnp.concatenate([t[:half, half:], t[:half, :half]], axis=1)], axis=0)
        t = g1_ref[...] * t + g2_ref[...] * sw
        vs.append(left(fh, fl, t))
    y = right(jnp.concatenate(vs, axis=0), th, tl)
    rows = length // groups
    for r in range(rb):
        for part in range(o_ref.shape[2]):
            o_ref[:, r, part] = y[r * length:(r + 1) * length, part * LANES:(part + 1) * LANES].reshape(groups, rows, LANES)

def whiten(x, spectral_filter, groups, start=0, count=None, rb=2):
    runs, length, _ = x.shape
    count = runs if count is None else count
    rows = length // groups
    fh, fl = basis(length)
    const = lambda shape: pl.BlockSpec(shape, lambda i: (0,) * len(shape), pipeline_mode=pl.Buffered(1))
    off = start // rb
    return pl.pallas_call(
        functools.partial(whiten_kernel, rb=rb, groups=groups),
        grid=(count // rb,),
        in_specs=[pl.BlockSpec((rb, length, length), lambda i: (i + off, 0, 0)),
                  const((spectral_filter.shape[1], length))] + [const((length, length))] * 4,
        out_specs=pl.BlockSpec((groups, rb, length // LANES, rows, LANES), lambda i: (0, i, 0, 0, 0)),
        out_shape=jax.ShapeDtypeStruct((groups, count, length // LANES, rows, LANES), jnp.float32),
        scratch_shapes=[pltpu.VMEM((length, length), jnp.float32)] * 2,
        name="whiten",
    )(x, spectral_filter.T, fh, fl, fh.T, fl.T)

def solve_kernel(w_ref, mh_ref, ml_ref, *rest, rows, acc):
    a_ref, o_ref = rest if acc else (None, rest[0])
    k = mh_ref.shape[1]
    i = pl.program_id(0)
    parts = w_ref.shape[0] // (k * rows)
    w = jnp.concatenate([w_ref[pl.ds(i + p * rows, k, stride=rows * parts), :] for p in range(parts)], axis=1)
    wh, wl = split(w)
    mh = mh_ref[...]; ml = ml_ref[...]
    out = mm(mh, wh) + mm(mh, wl) + mm(ml, wh)
    o_ref[...] = out + a_ref[...] if acc else out

def solve(w, mh, ml, acc=None):
    src, runs, parts, rows, lanes = w.shape
    length = parts * lanes
    q, k = mh.shape
    const = lambda shape: pl.BlockSpec(shape, lambda i: (0,) * len(shape), pipeline_mode=pl.Buffered(1))
    tile = pl.BlockSpec((q, length), lambda i: (0, i))
    w = w.reshape(src * runs * parts * rows, lanes)
    args = (w, mh, ml) + (() if acc is None else (acc,))
    return pl.pallas_call(
        functools.partial(solve_kernel, rows=rows, acc=acc is not None),
        grid=(rows,),
        in_specs=[const(w.shape), const((q, k)), const((q, k))] + ([] if acc is None else [tile]),
        out_specs=tile,
        out_shape=jax.ShapeDtypeStruct((q, rows * length), jnp.float32),
        input_output_aliases={} if acc is None else {3: 0},
        name="solve",
    )(*args)


def precise_dot(a, b):
    return jnp.dot(a, b, precision=lax.Precision.HIGHEST, preferred_element_type=jnp.float32)


def split_outside(x):
    hi = lax.reduce_precision(x, 8, 7)
    return hi.astype(jnp.bfloat16), (x - hi).astype(jnp.bfloat16)


def gather_panels(mine):
    groups = lax.axis_size("dev")
    me = lax.axis_index("dev")
    held = mine[None]
    bit = groups // 2
    while bit:
        pairs = [(i, i ^ bit) for i in range(groups)]
        held = jnp.concatenate([held, lax.ppermute(held, "dev", pairs)], axis=0)
        bit //= 2
    order = np.zeros(1, np.int32)
    bit = groups // 2
    while bit:
        order = np.concatenate([order, order ^ bit])
        bit //= 2
    place = np.argsort(order).astype(np.int32)
    held = jnp.take(held, jnp.asarray(place)[jnp.arange(groups) ^ me], axis=0)
    return jnp.moveaxis(held, 0, 1).reshape(mine.shape[0], -1, mine.shape[2])


def mixing(block_inverses, panels, total):
    width = block_inverses.shape[1]
    first, second = block_inverses[0], block_inverses[1]
    below = -precise_dot(second, precise_dot(panels[0, width : 2 * width], first))
    top = jnp.concatenate([first, jnp.zeros_like(first)], axis=1)
    rows = [top, jnp.concatenate([below, second], axis=1)]
    if total > 2 * width:
        left, right = panels[0, 2 * width :], panels[1, 2 * width :]
        rows.append(
            -jnp.concatenate(
                [precise_dot(left, first) + precise_dot(right, below), precise_dot(right, second)],
                axis=1,
            )
        )
    return jnp.concatenate(rows, axis=0)


def per_device(runs_field, spectral_filter, block_inverses, factor_panels):
    groups = lax.axis_size("dev")
    local, length, _ = runs_field.shape
    total = local * groups
    width = block_inverses.shape[1]
    pieces = whiten(runs_field, spectral_filter, groups, rb=4)
    arrived = lax.all_to_all(pieces, "dev", 0, 0, tiled=True)
    needed = 1 if total == 2 * width else 2
    panels = gather_panels(factor_panels[:needed])
    high, low = split_outside(mixing(block_inverses, panels, total))
    used = 2 * width // local
    out = solve(arrived[:used], high, low)
    if total > 2 * width:
        rest = jnp.moveaxis(arrived[used:], 2, 3).reshape(total - 2 * width, -1)
        out = jnp.concatenate([out[: 2 * width], out[2 * width :] + rest], axis=0)
    return out


def solution(mesh):
    return jax.shard_map(
        per_device,
        mesh=mesh,
        in_specs=(P("dev", None, None), P(), P(), P(None, "dev", None)),
        out_specs=P(None, "dev"),
        check_vma=False,
    )
```

```python
import functools, math
LANES = 128
import numpy as np
import jax, jax.numpy as jnp
from jax import lax
from jax.experimental import pallas as pl
from jax.experimental.pallas import tpu as pltpu
from jax.sharding import PartitionSpec as P


def basis(length):
    half = length // 2
    slot = np.arange(length)
    freq = np.where(slot <= half, slot, slot - half)
    phase = np.outer(np.arange(length), freq) % length
    angle = phase * (2.0 * math.pi / length)
    table = np.where(slot[None, :] <= half, np.cos(angle), np.sin(angle))
    hi = table.astype(jnp.bfloat16)
    lo = (table - hi.astype(np.float64)).astype(jnp.bfloat16)
    return hi, lo


def split(x):
    hi = x.astype(jnp.bfloat16)
    lo = (x - hi.astype(jnp.float32)).astype(jnp.bfloat16)
    return hi, lo


def mm(a, b):
    return lax.dot_general(a, b, (((1,), (0,)), ((), ())), preferred_element_type=jnp.float32)


def gains(filter_t, length):
    half = length // 2
    row = lax.broadcasted_iota(jnp.int32, (length, length), 0)
    col = lax.broadcasted_iota(jnp.int32, (length, length), 1)
    freq = jnp.where(row <= half, row, row - half)
    edge = (freq == 0) | (freq == half)
    plus = (col == freq).astype(jnp.float32)
    minus = (col == length - freq).astype(jnp.float32)
    minus = jnp.where(edge, 0.0, minus)
    plus_only = jnp.where(edge, 0.0, plus)
    sums = (plus + minus).astype(jnp.bfloat16)
    diffs = (plus_only - minus).astype(jnp.bfloat16)
    low = filter_t[:half]
    k = lax.broadcasted_iota(jnp.int32, (half, length), 0)
    high = jnp.where(k == 0, jnp.broadcast_to(filter_t[half:half + 1], (half, length)), low)

    def pick(sel, table):
        out = None
        rest = table
        for _ in range(3):
            piece = rest.astype(jnp.bfloat16)
            rest = rest - piece.astype(jnp.float32)
            part = lax.dot_general(sel, piece, (((1,), (1,)), ((), ())), preferred_element_type=jnp.float32)
            out = part if out is None else out + part
        return out

    tab = jnp.concatenate([low, high], axis=0)
    s = pick(sums, tab)
    d = pick(diffs, tab)
    kk = jnp.where(col <= half, col, col - half)
    kedge = (kk == 0) | (kk == half)
    scale = 1.0 / float(length * length)
    s = s * jnp.where(kedge, scale, 2.0 * scale)
    same = (row < half) == (col < half)
    d = d * jnp.where(kedge, 0.0, jnp.where(same, -2.0 * scale, 2.0 * scale))
    return s, d


def whiten_kernel(me_ref, x_ref, ft_ref, fh_ref, fl_ref, th_ref, tl_ref, *rest, rb, groups, outs):
    o_refs, (g1_ref, g2_ref), stage = rest[:outs], rest[outs:outs + 2], rest[outs + 2:]
    length = x_ref.shape[1]
    half = length // 2

    @pl.when(pl.program_id(0) == 0)
    def _():
        s, d = gains(ft_ref[...], length)
        g1_ref[...] = s
        g2_ref[...] = d

    fh, fl, th, tl = fh_ref[...], fl_ref[...], th_ref[...], tl_ref[...]

    def right(x, h, l):
        xh, xl = split(x)
        return mm(xh, h) + mm(xh, l) + mm(xl, h)

    def left(h, l, x):
        xh, xl = split(x)
        return mm(h, xh) + mm(l, xh) + mm(h, xl)

    z = right(x_ref[...].reshape(rb * length, length), fh, fl)
    vs = []
    for r in range(rb):
        t = left(th, tl, z[r * length:(r + 1) * length])
        sw = jnp.concatenate([
            jnp.concatenate([t[half:, half:], t[half:, :half]], axis=1),
            jnp.concatenate([t[:half, half:], t[:half, :half]], axis=1)], axis=0)
        t = g1_ref[...] * t + g2_ref[...] * sw
        vs.append(left(fh, fl, t))
    y = right(jnp.concatenate(vs, axis=0), th, tl)
    rows = length // groups
    target = stage[0] if stage else o_refs[0]
    for r in range(rb):
        for part in range(length // LANES):
            target[:, r, part] = y[r * length:(r + 1) * length, part * LANES:(part + 1) * LANES].reshape(groups, rows, LANES)
    if stage:
        chip = me_ref[0] // 2
        for k, o_ref in enumerate(o_refs):
            o_ref[...] = target[pl.ds(2 * (chip ^ k), 2)]


def whiten(me, x, spectral_filter, groups, start, count, rb, spread):
    length = x.shape[1]
    rows, parts = length // groups, length // LANES
    fh, fl = basis(length)
    const = lambda shape: pl.BlockSpec(shape, lambda i, me: (0,) * len(shape), pipeline_mode=pl.Buffered(1))
    off = start // rb
    outs, lead = (groups // 2, 2) if spread else (1, groups)
    scratch = [pltpu.VMEM((length, length), jnp.float32)] * 2
    if spread:
        scratch.append(pltpu.VMEM((groups, rb, parts, rows, LANES), jnp.float32))
    return pl.pallas_call(
        functools.partial(whiten_kernel, rb=rb, groups=groups, outs=outs),
        grid_spec=pltpu.PrefetchScalarGridSpec(
            num_scalar_prefetch=1,
            grid=(count // rb,),
            in_specs=[pl.BlockSpec((rb, length, length), lambda i, me: (i + off, 0, 0)),
                      const((spectral_filter.shape[1], length))] + [const((length, length))] * 4,
            out_specs=[pl.BlockSpec((lead, rb, parts, rows, LANES), lambda i, me: (0, i, 0, 0, 0))] * outs,
            scratch_shapes=scratch,
        ),
        out_shape=[jax.ShapeDtypeStruct((lead, count, parts, rows, LANES), jnp.float32)] * outs,
        name="whiten",
    )(me, x, spectral_filter.T, fh, fl, fh.T, fl.T)


def solve_kernel(me_ref, *refs, rows, parts, sizes, acc):
    n = len(sizes)
    w_refs, (mh_ref, ml_ref) = refs[:n], refs[n:n + 2]
    o_ref = refs[-1]
    i = pl.program_id(0)
    pieces = [
        jnp.concatenate([w_ref[pl.ds(p * rows + i, k, stride=rows * parts), :] for p in range(parts)], axis=1)
        for w_ref, k in zip(w_refs, sizes)
    ]
    wh, wl = split(jnp.concatenate(pieces, axis=0) if n > 1 else pieces[0])
    mh, ml = mh_ref[...], ml_ref[...]
    out = mm(mh, wh) + mm(mh, wl) + mm(ml, wh)
    o_ref[...] = out + refs[n + 2][...] if acc else out


def solve(me, pieces, mh, ml, rows, parts, acc=None):
    q = mh.shape[0]
    const = lambda shape: pl.BlockSpec(shape, lambda i, me: (0,) * len(shape), pipeline_mode=pl.Buffered(1))
    each = rows * parts
    specs, args, sizes = [], [], []
    for array, runs, paired in pieces:
        sizes.append(runs)
        args.append(array)
        if paired:
            specs.append(pl.BlockSpec((None, runs * each, LANES), lambda i, me: (me[0] % 2, 0, 0), pipeline_mode=pl.Buffered(1)))
        else:
            specs.append(const((runs * each, LANES)))
    tile = pl.BlockSpec((q, parts * LANES), lambda i, me: (0, i))
    specs += [const(mh.shape), const(ml.shape)]
    args += [mh, ml]
    if acc is not None:
        specs.append(tile)
        args.append(acc)
    return pl.pallas_call(
        functools.partial(solve_kernel, rows=rows, parts=parts, sizes=tuple(sizes), acc=acc is not None),
        grid_spec=pltpu.PrefetchScalarGridSpec(
            num_scalar_prefetch=1, grid=(rows,), in_specs=specs, out_specs=tile),
        out_shape=jax.ShapeDtypeStruct((q, each * LANES), jnp.float32),
        input_output_aliases={} if acc is None else {len(args): 0},
        name="solve",
    )(me, *args)


def precise_dot(a, b):
    return jnp.dot(a, b, precision=lax.Precision.HIGHEST, preferred_element_type=jnp.float32)


def split_outside(x):
    hi = lax.reduce_precision(x, 8, 7)
    return hi.astype(jnp.bfloat16), (x - hi).astype(jnp.bfloat16)


def mixing(block_inverses, panels, total):
    width = block_inverses.shape[1]
    first, second = block_inverses[0], block_inverses[1]
    below = -precise_dot(second, precise_dot(panels[0, width : 2 * width], first))
    top = jnp.concatenate([first, jnp.zeros_like(first)], axis=1)
    rows = [top, jnp.concatenate([below, second], axis=1)]
    if total > 2 * width:
        left, right = panels[0, 2 * width :], panels[1, 2 * width :]
        rows.append(
            -jnp.concatenate(
                [precise_dot(left, first) + precise_dot(right, below), precise_dot(right, second)],
                axis=1,
            )
        )
    return jnp.concatenate(rows, axis=0)


HEAD = 4
LATE = 3


def exchange(x, offset):
    pairs = [(i, i ^ offset) for i in range(lax.axis_size("dev"))]
    return lax.ppermute(x, "dev", pairs)


def whole_order(me, head, got, early, late, load, final, ways, mix, rows, parts, front):
    groups, _ = head.shape[:2]
    each = rows * parts
    rest = final.shape[0] // (len(late) * each)
    core = me[0] % 2

    def mine(k):
        return lax.dynamic_slice_in_dim(got[k], core, 1, 0)[0, : rest * each]

    tail = [mine(k) for k in early] + [load[: len(early) * rest * each]] + [mine(k) for k in late] + [final]
    tail = jnp.concatenate(tail, axis=0).reshape(groups, rest, parts, rows, LANES)
    spot = jnp.asarray(np.argsort(ways).astype(np.int32))
    tail = jnp.take(tail, spot[jnp.arange(groups) ^ me[0]], axis=0)
    runs = jnp.concatenate([head, tail], axis=1).reshape(-1, parts, rows, LANES)
    out = solve(me, [(runs[:front].reshape(-1, LANES), front, False)], *split_outside(mix), rows, parts)
    below = jnp.moveaxis(runs[front:], 1, 2).reshape(out.shape[0] - front, -1)
    return jnp.concatenate([out[:front], out[front:] + below], axis=0)


def per_device(runs_field, spectral_filter, block_inverses, factor_panels):
    groups = lax.axis_size("dev")
    place = lax.axis_index("dev")
    local, length, _ = runs_field.shape
    total = local * groups
    width = block_inverses.shape[1]
    rows, parts = length // groups, length // LANES
    each = rows * parts
    chips, top = groups // 2, groups // 2
    rest = local - HEAD
    core = place % 2
    me = place.astype(jnp.int32).reshape(1)
    needed = 1 if total == 2 * width else 2

    def other(x):
        return lax.dynamic_slice_in_dim(x, 1 - core, 1, 0)

    mine = factor_panels[:needed]
    held = jnp.stack([mine, exchange(mine, top)])
    (head,) = whiten(me, runs_field, spectral_filter, groups, 0, HEAD, HEAD, False)
    head = lax.all_to_all(head, "dev", 0, 0, tiled=True)
    outs = whiten(me, runs_field, spectral_filter, groups, HEAD, rest, HEAD, True)
    outs = [o.reshape(2, rest * each, LANES) for o in outs]
    carried = held.reshape(2, -1, LANES)
    got = {0: outs[0]}
    papers = {0: carried}
    near = list(range(1, chips // 2))
    far = list(range(chips // 2, chips))
    for k in far:
        got[k] = exchange(outs[k], 2 * k)
    for k in near:
        got[k] = exchange(jnp.concatenate([outs[k], carried], axis=1), 2 * k)
        papers[k] = got[k][:, rest * each:]
    early = [0] + near + far[:-LATE]
    late = far[-LATE:]
    book = jnp.concatenate([papers[k].reshape(1, -1, LANES) for k in [0] + near], axis=1)
    load = jnp.concatenate([other(got[k])[:, : rest * each] for k in early] + [book], axis=1)
    load = exchange(load[0], 1)
    first_count = len(early) * rest
    theirs = load[first_count * each :]
    pages = jnp.concatenate([book[0], theirs], axis=0)
    pages = pages.reshape(2, chips // 2, 2, needed, local, width)
    pages = jnp.transpose(pages, (2, 1, 0, 3, 4, 5)).reshape(groups, needed, local, width)
    ways = np.array([[h * top + 2 * k + c for k in [0] + near for c in range(2)] for h in range(2)]).reshape(-1)
    spot = np.argsort(ways).astype(np.int32)
    pages = jnp.take(pages, jnp.asarray(spot)[jnp.arange(groups) ^ place], axis=0)
    panels = jnp.moveaxis(pages, 0, 1).reshape(needed, total, width)
    mix = mixing(block_inverses, panels, total)
    ways = [2 * k for k in early] + [2 * k + 1 for k in early] + [2 * k for k in late] + [2 * k + 1 for k in late]
    cut = 2 * first_count

    if total == 2 * width:
        table = mix.T.reshape(groups, local, total)
        tail = jnp.take(table[:, HEAD:], jnp.asarray(np.array(ways, np.int32)) ^ place, axis=0)
        tail = tail.reshape(-1, total)
        soon = split_outside(jnp.concatenate([table[:, :HEAD].reshape(-1, total), tail[:cut]], axis=0).T)
        last = split_outside(tail[cut:].T)
    final = exchange(jnp.concatenate([other(got[k])[0] for k in late], axis=0), 1)
    if total > 2 * width:
        return whole_order(me, head, got, early, late, load, final, ways, mix, rows, parts, 2 * width)
    pieces = [(head.reshape(-1, LANES), groups * HEAD, False)]
    pieces += [(got[k], rest, True) for k in early]
    pieces.append((load, first_count, False))
    out = solve(me, pieces, *soon, rows, parts)
    pieces = [(got[k], rest, True) for k in late] + [(final, len(late) * rest, False)]
    out = solve(me, pieces, *last, rows, parts, out)
    return out


def solution(mesh):
    return jax.shard_map(
        per_device,
        mesh=mesh,
        in_specs=(P("dev", None, None), P(), P(), P(None, "dev", None)),
        out_specs=P(None, "dev"),
        check_vma=False,
    )
```

```python
import functools, math
LANES = 128
import numpy as np
import jax, jax.numpy as jnp
from jax import lax
from jax.experimental import pallas as pl
from jax.experimental.pallas import tpu as pltpu
from jax.sharding import PartitionSpec as P


def basis(length):
    half = length // 2
    slot = np.arange(length)
    freq = np.where(slot <= half, slot, slot - half)
    phase = np.outer(np.arange(length), freq) % length
    angle = phase * (2.0 * math.pi / length)
    table = np.where(slot[None, :] <= half, np.cos(angle), np.sin(angle))
    hi = table.astype(jnp.bfloat16)
    lo = (table - hi.astype(np.float64)).astype(jnp.bfloat16)
    return hi, lo


def split(x):
    hi = x.astype(jnp.bfloat16)
    lo = (x - hi.astype(jnp.float32)).astype(jnp.bfloat16)
    return hi, lo


def mm(a, b):
    return lax.dot_general(a, b, (((1,), (0,)), ((), ())), preferred_element_type=jnp.float32)


def gains(filter_t, length):
    half = length // 2
    row = lax.broadcasted_iota(jnp.int32, (length, length), 0)
    col = lax.broadcasted_iota(jnp.int32, (length, length), 1)
    freq = jnp.where(row <= half, row, row - half)
    edge = (freq == 0) | (freq == half)
    plus = (col == freq).astype(jnp.float32)
    minus = (col == length - freq).astype(jnp.float32)
    minus = jnp.where(edge, 0.0, minus)
    plus_only = jnp.where(edge, 0.0, plus)
    sums = (plus + minus).astype(jnp.bfloat16)
    diffs = (plus_only - minus).astype(jnp.bfloat16)
    low = filter_t[:half]
    k = lax.broadcasted_iota(jnp.int32, (half, length), 0)
    high = jnp.where(k == 0, jnp.broadcast_to(filter_t[half:half + 1], (half, length)), low)

    def pick(sel, table):
        out = None
        rest = table
        for _ in range(3):
            piece = rest.astype(jnp.bfloat16)
            rest = rest - piece.astype(jnp.float32)
            part = lax.dot_general(sel, piece, (((1,), (1,)), ((), ())), preferred_element_type=jnp.float32)
            out = part if out is None else out + part
        return out

    tab = jnp.concatenate([low, high], axis=0)
    s = pick(sums, tab)
    d = pick(diffs, tab)
    kk = jnp.where(col <= half, col, col - half)
    kedge = (kk == 0) | (kk == half)
    scale = 1.0 / float(length * length)
    s = s * jnp.where(kedge, scale, 2.0 * scale)
    same = (row < half) == (col < half)
    d = d * jnp.where(kedge, 0.0, jnp.where(same, -2.0 * scale, 2.0 * scale))
    return s, d


def whiten_kernel(me_ref, x_ref, ft_ref, fh_ref, fl_ref, th_ref, tl_ref, *rest, rb, groups, outs):
    o_refs, (g1_ref, g2_ref), stage = rest[:outs], rest[outs:outs + 2], rest[outs + 2:]
    length = x_ref.shape[1]
    half = length // 2

    @pl.when(pl.program_id(0) == 0)
    def _():
        s, d = gains(ft_ref[...], length)
        g1_ref[...] = s
        g2_ref[...] = d

    fh, fl, th, tl = fh_ref[...], fl_ref[...], th_ref[...], tl_ref[...]

    def right(x, h, l):
        xh, xl = split(x)
        return mm(xh, h) + mm(xh, l) + mm(xl, h)

    def left(h, l, x):
        xh, xl = split(x)
        return mm(h, xh) + mm(l, xh) + mm(h, xl)

    z = right(x_ref[...].reshape(rb * length, length), fh, fl)
    vs = []
    for r in range(rb):
        t = left(th, tl, z[r * length:(r + 1) * length])
        sw = jnp.concatenate([
            jnp.concatenate([t[half:, half:], t[half:, :half]], axis=1),
            jnp.concatenate([t[:half, half:], t[:half, :half]], axis=1)], axis=0)
        t = g1_ref[...] * t + g2_ref[...] * sw
        vs.append(left(fh, fl, t))
    y = right(jnp.concatenate(vs, axis=0), th, tl)
    rows = length // groups
    target = stage[0] if stage else o_refs[0]
    for r in range(rb):
        for part in range(length // LANES):
            target[:, r, part] = y[r * length:(r + 1) * length, part * LANES:(part + 1) * LANES].reshape(groups, rows, LANES)
    if stage:
        chip = me_ref[0] // 2
        for k, o_ref in enumerate(o_refs):
            o_ref[...] = target[pl.ds(2 * (chip ^ k), 2)]


def whiten(me, x, spectral_filter, groups, start, count, rb, spread):
    length = x.shape[1]
    rows, parts = length // groups, length // LANES
    fh, fl = basis(length)
    const = lambda shape: pl.BlockSpec(shape, lambda i, me: (0,) * len(shape), pipeline_mode=pl.Buffered(1))
    off = start // rb
    outs, lead = (groups // 2, 2) if spread else (1, groups)
    scratch = [pltpu.VMEM((length, length), jnp.float32)] * 2
    if spread:
        scratch.append(pltpu.VMEM((groups, rb, parts, rows, LANES), jnp.float32))
    return pl.pallas_call(
        functools.partial(whiten_kernel, rb=rb, groups=groups, outs=outs),
        grid_spec=pltpu.PrefetchScalarGridSpec(
            num_scalar_prefetch=1,
            grid=(count // rb,),
            in_specs=[pl.BlockSpec((rb, length, length), lambda i, me: (i + off, 0, 0)),
                      const((spectral_filter.shape[1], length))] + [const((length, length))] * 4,
            out_specs=[pl.BlockSpec((lead, rb, parts, rows, LANES), lambda i, me: (0, i, 0, 0, 0))] * outs,
            scratch_shapes=scratch,
        ),
        out_shape=[jax.ShapeDtypeStruct((lead, count, parts, rows, LANES), jnp.float32)] * outs,
        name="whiten",
    )(me, x, spectral_filter.T, fh, fl, fh.T, fl.T)


def plain_kernel(w_ref, mh_ref, ml_ref, o_ref, *, rows, parts):
    k = mh_ref.shape[1]
    i = pl.program_id(0)
    w = jnp.concatenate([w_ref[pl.ds(p * rows + i, k, stride=rows * parts), :] for p in range(parts)], axis=1)
    wh, wl = split(w)
    o_ref[...] = mm(mh_ref[...], wh) + mm(mh_ref[...], wl) + mm(ml_ref[...], wh)


def plain_solve(w, mh, ml, rows, parts):
    q = mh.shape[0]
    const = lambda a: pl.BlockSpec(a.shape, lambda i: (0,) * a.ndim, pipeline_mode=pl.Buffered(1))
    return pl.pallas_call(
        functools.partial(plain_kernel, rows=rows, parts=parts),
        grid=(rows,),
        in_specs=[const(w), const(mh), const(ml)],
        out_specs=pl.BlockSpec((q, parts * LANES), lambda i: (0, i)),
        out_shape=jax.ShapeDtypeStruct((q, rows * parts * LANES), jnp.float32),
        name="plain",
    )(w, mh, ml)


def whole(shape):
    return pl.BlockSpec(shape, lambda i, me: (0,) * len(shape), pipeline_mode=pl.Buffered(1))


def here():
    return pl.BlockSpec(memory_space=pltpu.VMEM)


def bundle_kernel(me_ref, *refs):
    size = refs[0].shape[1]
    for j, ref in enumerate(refs[:-1]):
        refs[-1][j * size:(j + 1) * size] = ref[1 - me_ref[0] % 2]


def bundle(me, arrays):
    size = arrays[0].shape[1]
    shape = (len(arrays) * size, LANES)
    return pl.pallas_call(
        bundle_kernel,
        grid_spec=pltpu.PrefetchScalarGridSpec(
            num_scalar_prefetch=1, grid=(1,), in_specs=[here() for a in arrays], out_specs=here()),
        out_shape=jax.ShapeDtypeStruct(shape, jnp.float32),
        name="bundle",
    )(me, *arrays)


def mix_kernel(me_ref, spot_ref, mask_ref, inverse_ref, *refs, top, local):
    papers, theirs_ref = refs[:-6], refs[-6]
    th_ref, tl_ref, bh_ref, bl_ref, panel_ref = refs[-5:]
    me = me_ref[0]
    for k, ref in enumerate(papers):
        for c in range(2):
            at = pl.multiple_of(((me ^ (2 * k + c)) & (top - 1)) * local, local)
            panel_ref[pl.ds(at, local), :] = theirs_ref[k * local:(k + 1) * local] if c else ref[...]
    exact = functools.partial(jnp.dot, precision=lax.Precision.HIGHEST, preferred_element_type=jnp.float32)
    first, second = inverse_ref[0], inverse_ref[1]
    below = -exact(second, exact(panel_ref[...], first))
    width = first.shape[0]
    table = jnp.concatenate([
        jnp.concatenate([first, jnp.zeros_like(first)], axis=1),
        jnp.concatenate([below, second], axis=1)], axis=0)
    run = spot_ref[...] ^ ((me * local) & mask_ref[...])
    order = lax.broadcasted_iota(jnp.int32, table.shape, 0) == jnp.broadcast_to(run, table.shape)
    order = order.astype(jnp.float32).astype(jnp.bfloat16)
    left = me < top
    for piece, t_ref, b_ref in zip(split(table), (th_ref, tl_ref), (bh_ref, bl_ref)):
        moved = mm(piece, order)
        b_ref[...] = moved[width:].astype(jnp.bfloat16)
        t_ref[...] = jnp.where(left, moved[:width, :width], moved[:width, width:]).astype(jnp.bfloat16)


def mix(me, spots, masks, inverses, papers, theirs, top, local):
    width = inverses.shape[1]
    shapes = [(width, width)] * 2 + [(width, 2 * width)] * 2
    args = [spots, masks, inverses, *papers, theirs]
    return pl.pallas_call(
        functools.partial(mix_kernel, top=top, local=local),
        grid_spec=pltpu.PrefetchScalarGridSpec(
            num_scalar_prefetch=1, grid=(1,),
            in_specs=[whole(spots.shape), whole(masks.shape), whole(inverses.shape)] + [here()] * (len(papers) + 1),
            out_specs=[here()] * len(shapes),
            scratch_shapes=[pltpu.VMEM((width, width), jnp.float32)]),
        out_shape=[jax.ShapeDtypeStruct(shape, jnp.bfloat16) for shape in shapes],
        name="mix",
    )(me, *args)


def solve_kernel(me_ref, *refs, rows, parts, per, near, far, top):
    count = len(refs) - 6
    w_refs = refs[:count]
    th_ref, tl_ref, bh_ref, bl_ref, o_ref, held_ref = refs[count:]
    stride = rows * parts
    width = th_ref.shape[0]
    left = me_ref[0] // top
    for block, picks in enumerate((near, far)):
        columns = []
        for g in range(per):
            i = pl.program_id(0) * per + g
            for p in range(parts):
                at = p * rows + i
                column = []
                for n, start, size in picks:
                    if start is None:
                        start = (left ^ block) * (size * stride)
                    ref = w_refs[n]
                    if len(ref.shape) == 3:
                        ref = ref.at[me_ref[0] % 2]
                    column.append(ref[pl.ds(start + at, size, stride=stride), :])
                columns.append(jnp.concatenate(column, axis=0))
        high, low = split(jnp.concatenate(columns, axis=1))
        held_ref[block, 0] = high
        held_ref[block, 1] = low
    th, tl = th_ref[...], tl_ref[...]
    o_ref[:width] = mm(th, held_ref[left, 0]) + mm(th, held_ref[left, 1]) + mm(tl, held_ref[left, 0])
    out = None
    for block in range(2):
        bh = bh_ref[:, block * width:(block + 1) * width]
        bl = bl_ref[:, block * width:(block + 1) * width]
        part = mm(bh, held_ref[block, 0]) + mm(bh, held_ref[block, 1]) + mm(bl, held_ref[block, 0])
        out = part if out is None else out + part
    o_ref[width:] = out


def solve(me, head, got, load, final, late, rest, tables, rows, parts, top):
    chips = len(got)
    each = rows * parts
    early = chips - late
    per = 2 if rows % 2 == 0 else 1
    args = [head, *got, load, final, *tables]
    half_rows = head.shape[0] // each // 2
    pair = lambda n, start, size: (n, start * each, size)
    near = [(0, None, half_rows)] + [pair(1 + k, 0, rest) for k in range(chips // 2)]
    near += [pair(1 + chips, 0, chips // 2 * rest)]
    far = [(0, None, half_rows)] + [pair(1 + k, 0, rest) for k in range(chips // 2, chips)]
    far += [pair(1 + chips, chips // 2 * rest, (early - chips // 2) * rest), pair(2 + chips, 0, late * rest)]
    specs = [here()] * len(args)
    width = tables[0].shape[0]
    return pl.pallas_call(
        functools.partial(solve_kernel, rows=rows, parts=parts, per=per, near=tuple(near), far=tuple(far), top=top),
        grid_spec=pltpu.PrefetchScalarGridSpec(
            num_scalar_prefetch=1, grid=(rows // per,), in_specs=specs,
            out_specs=pl.BlockSpec((2 * width, per * parts * LANES), lambda i, me: (0, i)),
            scratch_shapes=[pltpu.VMEM((2, 2, width, per * parts * LANES), jnp.bfloat16)]),
        out_shape=jax.ShapeDtypeStruct((2 * width, each * LANES), jnp.float32),
        name="solve",
    )(me, *args)


def precise_dot(a, b):
    return jnp.dot(a, b, precision=lax.Precision.HIGHEST, preferred_element_type=jnp.float32)


def split_outside(x):
    hi = lax.reduce_precision(x, 8, 7)
    return hi.astype(jnp.bfloat16), (x - hi).astype(jnp.bfloat16)


def mixing(block_inverses, panels, total):
    width = block_inverses.shape[1]
    first, second = block_inverses[0], block_inverses[1]
    below = -precise_dot(second, precise_dot(panels[0, width : 2 * width], first))
    top = jnp.concatenate([first, jnp.zeros_like(first)], axis=1)
    rows = [top, jnp.concatenate([below, second], axis=1)]
    if total > 2 * width:
        left, right = panels[0, 2 * width :], panels[1, 2 * width :]
        rows.append(
            -jnp.concatenate(
                [precise_dot(left, first) + precise_dot(right, below), precise_dot(right, second)],
                axis=1,
            )
        )
    return jnp.concatenate(rows, axis=0)


HEAD = 4
LATE = 3


def exchange(x, offset):
    pairs = [(i, i ^ offset) for i in range(lax.axis_size("dev"))]
    return lax.ppermute(x, "dev", pairs)


def general(me, runs_field, spectral_filter, block_inverses, factor_panels):
    groups = lax.axis_size("dev")
    local, length, _ = runs_field.shape
    total = local * groups
    front = 2 * block_inverses.shape[1]
    rows, parts = length // groups, length // LANES
    (pieces,) = whiten(me, runs_field, spectral_filter, groups, 0, local, HEAD, False)
    runs = lax.all_to_all(pieces, "dev", 0, 0, tiled=True).reshape(total, parts, rows, LANES)
    panels = lax.all_gather(factor_panels, "dev", axis=1, tiled=True)
    tables = split_outside(mixing(block_inverses, panels, total))
    out = plain_solve(runs[:front].reshape(-1, LANES), *tables, rows, parts)
    if total > front:
        below = jnp.moveaxis(runs[front:], 1, 2).reshape(total - front, -1)
        out = jnp.concatenate([out[:front], out[front:] + below], axis=0)
    return out


def places(groups, local, early, late):
    top = groups // 2
    rest = range(HEAD, local)
    spots, masks = [], []
    for far in range(2):
        for source in range(top):
            spots += [(source + far * top) * local + r for r in range(HEAD)]
            masks += [top * local] * HEAD
        mine = [k for k in early + late if (2 * k >= top) == bool(far)]
        ways = [2 * k for k in mine]
        ways += [2 * k + 1 for k in mine]
        for way in ways:
            spots += [way * local + r for r in rest]
            masks += [-1] * len(rest)
    return np.array([spots], np.int32), np.array([masks], np.int32)


def per_device(runs_field, spectral_filter, block_inverses, factor_panels):
    groups = lax.axis_size("dev")
    place = lax.axis_index("dev")
    local, length, _ = runs_field.shape
    width = block_inverses.shape[1]
    rows, parts = length // groups, length // LANES
    chips, top = groups // 2, groups // 2
    me = place.astype(jnp.int32).reshape(1)
    if local * groups != 2 * width:
        return general(me, runs_field, spectral_filter, block_inverses, factor_panels)
    rest = local - HEAD
    near = list(range(1, chips // 2))
    far = list(range(chips // 2, chips))
    early, late = [0] + near + far[:-LATE], far[-LATE:]
    mine = factor_panels[0]
    mine = jnp.where(place < top, exchange(mine, top), mine)
    (head,) = whiten(me, runs_field, spectral_filter, groups, 0, HEAD, HEAD, False)
    head = lax.all_to_all(head, "dev", 0, 0, tiled=True)
    outs = whiten(me, runs_field, spectral_filter, groups, HEAD, rest, HEAD, True)
    outs = [o.reshape(2, -1, LANES) for o in outs]
    got = [outs[0]] + [None] * (chips - 1)
    papers = [mine]
    for k in near:
        papers.append(exchange(mine, 2 * k))
    for k in near + far:
        got[k] = exchange(outs[k], 2 * k)
    theirs = exchange(jnp.concatenate(papers, axis=0), 1)
    spots, masks = places(groups, local, early, late)
    tables = mix(me, spots, masks, block_inverses, papers, theirs, top, local)
    load = bundle(me, [got[k] for k in early])
    load = exchange(load, 1)
    final = bundle(me, [got[k] for k in late])
    final = exchange(final, 1)
    return solve(me, head.reshape(-1, LANES), got, load, final, LATE, rest, tables, rows, parts, top)


def solution(mesh):
    return jax.shard_map(
        per_device,
        mesh=mesh,
        in_specs=(P("dev", None, None), P(), P(), P(None, "dev", None)),
        out_specs=P(None, "dev"),
        check_vma=False,
    )
```

```python
import functools, math
LANES = 128
import numpy as np
import jax, jax.numpy as jnp
from jax import lax
from jax.experimental import pallas as pl
from jax.experimental.pallas import tpu as pltpu
from jax.sharding import PartitionSpec as P

LIMIT = pltpu.CompilerParams(vmem_limit_bytes=32 << 20)


def basis(length):
    half = length // 2
    slot = np.arange(length)
    freq = np.where(slot <= half, slot, slot - half)
    phase = np.outer(np.arange(length), freq) % length
    angle = phase * (2.0 * math.pi / length)
    table = np.where(slot[None, :] <= half, np.cos(angle), np.sin(angle))
    hi = table.astype(jnp.bfloat16)
    lo = (table - hi.astype(np.float64)).astype(jnp.bfloat16)
    return hi, lo


def split(x):
    hi = x.astype(jnp.bfloat16)
    lo = (x - hi.astype(jnp.float32)).astype(jnp.bfloat16)
    return hi, lo


def mm(a, b):
    return lax.dot_general(a, b, (((1,), (0,)), ((), ())), preferred_element_type=jnp.float32)


def gains(filter_t, length):
    half = length // 2
    row = lax.broadcasted_iota(jnp.int32, (length, length), 0)
    col = lax.broadcasted_iota(jnp.int32, (length, length), 1)
    freq = jnp.where(row <= half, row, row - half)
    edge = (freq == 0) | (freq == half)
    plus = (col == freq).astype(jnp.float32)
    minus = (col == length - freq).astype(jnp.float32)
    minus = jnp.where(edge, 0.0, minus)
    plus_only = jnp.where(edge, 0.0, plus)
    sums = (plus + minus).astype(jnp.bfloat16)
    diffs = (plus_only - minus).astype(jnp.bfloat16)
    low = filter_t[:half]
    k = lax.broadcasted_iota(jnp.int32, (half, length), 0)
    high = jnp.where(k == 0, jnp.broadcast_to(filter_t[half:half + 1], (half, length)), low)

    def pick(sel, table):
        out = None
        rest = table
        for _ in range(3):
            piece = rest.astype(jnp.bfloat16)
            rest = rest - piece.astype(jnp.float32)
            part = lax.dot_general(sel, piece, (((1,), (1,)), ((), ())), preferred_element_type=jnp.float32)
            out = part if out is None else out + part
        return out

    tab = jnp.concatenate([low, high], axis=0)
    s = pick(sums, tab)
    d = pick(diffs, tab)
    kk = jnp.where(col <= half, col, col - half)
    kedge = (kk == 0) | (kk == half)
    scale = 1.0 / float(length * length)
    s = s * jnp.where(kedge, scale, 2.0 * scale)
    same = (row < half) == (col < half)
    d = d * jnp.where(kedge, 0.0, jnp.where(same, -2.0 * scale, 2.0 * scale))
    return s, d


def whiten_kernel(me_ref, x_ref, ft_ref, fh_ref, fl_ref, th_ref, tl_ref, *rest, rb, groups, outs):
    o_refs, (g1_ref, g2_ref), stage = rest[:outs], rest[outs:outs + 2], rest[outs + 2:]
    length = x_ref.shape[1]
    half = length // 2

    @pl.when(pl.program_id(0) == 0)
    def _():
        s, d = gains(ft_ref[...], length)
        g1_ref[...] = s
        g2_ref[...] = d

    fh, fl, th, tl = fh_ref[...], fl_ref[...], th_ref[...], tl_ref[...]

    def right(x, h, l):
        xh, xl = split(x)
        return mm(xh, h) + mm(xh, l) + mm(xl, h)

    def left(h, l, x):
        xh, xl = split(x)
        return mm(h, xh) + mm(l, xh) + mm(h, xl)

    z = right(x_ref[...].reshape(rb * length, length), fh, fl)
    vs = []
    for r in range(rb):
        t = left(th, tl, z[r * length:(r + 1) * length])
        sw = jnp.concatenate([
            jnp.concatenate([t[half:, half:], t[half:, :half]], axis=1),
            jnp.concatenate([t[:half, half:], t[:half, :half]], axis=1)], axis=0)
        t = g1_ref[...] * t + g2_ref[...] * sw
        vs.append(left(fh, fl, t))
    y = right(jnp.concatenate(vs, axis=0), th, tl)
    rows = length // groups
    target = stage[0] if stage else o_refs[0]
    for r in range(rb):
        for part in range(length // LANES):
            target[:, r, part] = y[r * length:(r + 1) * length, part * LANES:(part + 1) * LANES].reshape(groups, rows, LANES)
    if stage:
        chip = me_ref[0] // 2
        for k, o_ref in enumerate(o_refs[:groups // 4]):
            o_ref[...] = target[pl.ds(2 * (chip ^ k), 2)]
        for way, o_ref in enumerate(o_refs[groups // 4:], groups // 2):
            o_ref[...] = target[pl.ds(me_ref[0] ^ way, 1)]


def whiten(me, x, spectral_filter, groups, start, count, rb, spread):
    length = x.shape[1]
    rows, parts = length // groups, length // LANES
    fh, fl = basis(length)
    const = lambda shape: pl.BlockSpec(shape, lambda i, me: (0,) * len(shape), pipeline_mode=pl.Buffered(1))
    off = start // rb
    leads = [2] * (groups // 4) + [1] * (groups // 2) if spread else [groups]
    scratch = [pltpu.VMEM((length, length), jnp.float32)] * 2
    if spread:
        scratch.append(pltpu.VMEM((groups, rb, parts, rows, LANES), jnp.float32))
    return pl.pallas_call(
        functools.partial(whiten_kernel, rb=rb, groups=groups, outs=len(leads)),
        grid_spec=pltpu.PrefetchScalarGridSpec(
            num_scalar_prefetch=1,
            grid=(count // rb,),
            in_specs=[pl.BlockSpec((rb, length, length), lambda i, me: (i + off, 0, 0)),
                      const((spectral_filter.shape[1], length))] + [const((length, length))] * 4,
            out_specs=[pl.BlockSpec((lead, rb, parts, rows, LANES), lambda i, me: (0, i, 0, 0, 0)) for lead in leads],
            scratch_shapes=scratch,
        ),
        out_shape=[jax.ShapeDtypeStruct((lead, count, parts, rows, LANES), jnp.float32) for lead in leads],
        compiler_params=LIMIT,
        name="whiten",
    )(me, x, spectral_filter.T, fh, fl, fh.T, fl.T)


def plain_kernel(w_ref, mh_ref, ml_ref, o_ref, *, rows, parts):
    k = mh_ref.shape[1]
    i = pl.program_id(0)
    w = jnp.concatenate([w_ref[pl.ds(p * rows + i, k, stride=rows * parts), :] for p in range(parts)], axis=1)
    wh, wl = split(w)
    o_ref[...] = mm(mh_ref[...], wh) + mm(mh_ref[...], wl) + mm(ml_ref[...], wh)


def plain_solve(w, mh, ml, rows, parts):
    q = mh.shape[0]
    const = lambda a: pl.BlockSpec(a.shape, lambda i: (0,) * a.ndim, pipeline_mode=pl.Buffered(1))
    return pl.pallas_call(
        functools.partial(plain_kernel, rows=rows, parts=parts),
        grid=(rows,),
        in_specs=[const(w), const(mh), const(ml)],
        out_specs=pl.BlockSpec((q, parts * LANES), lambda i: (0, i)),
        out_shape=jax.ShapeDtypeStruct((q, rows * parts * LANES), jnp.float32),
        name="plain",
    )(w, mh, ml)


def whole(shape):
    return pl.BlockSpec(shape, lambda i, me: (0,) * len(shape), pipeline_mode=pl.Buffered(1))


def outside(arrays):
    return [pltpu.with_memory_space_constraint(a, pltpu.HBM) for a in arrays]


def parity(array, flip):
    pick = (lambda i, me: (1 - me[0] % 2, 0, 0)) if flip else (lambda i, me: (me[0] % 2, 0, 0))
    return pl.BlockSpec((None,) + array.shape[1:], pick, pipeline_mode=pl.Buffered(1))


def bundle_kernel(me_ref, *refs):
    size = refs[0].shape[0]
    for j, ref in enumerate(refs[:-1]):
        refs[-1][j * size:(j + 1) * size] = ref[...]


def bundle(me, arrays):
    size = arrays[0].shape[1]
    shape = (len(arrays) * size, LANES)
    return pl.pallas_call(
        bundle_kernel,
        grid_spec=pltpu.PrefetchScalarGridSpec(
            num_scalar_prefetch=1, grid=(1,), in_specs=[parity(a, True) for a in arrays], out_specs=whole(shape)),
        out_shape=jax.ShapeDtypeStruct(shape, jnp.float32),
        compiler_params=LIMIT,
        name="bundle",
    )(me, *arrays)


def stack(me, arrays):
    rows, lanes = arrays[0].shape
    shape = (len(arrays) * rows, lanes)
    return pl.pallas_call(
        bundle_kernel,
        grid_spec=pltpu.PrefetchScalarGridSpec(
            num_scalar_prefetch=1, grid=(1,), in_specs=[whole(a.shape) for a in arrays], out_specs=whole(shape)),
        out_shape=jax.ShapeDtypeStruct(shape, jnp.float32),
        compiler_params=LIMIT,
        name="stack",
    )(me, *arrays)


def mix_kernel(me_ref, spot_ref, mask_ref, inverse_ref, *refs, top, local):
    papers, theirs_ref = refs[:-6], refs[-6]
    th_ref, tl_ref, bh_ref, bl_ref, panel_ref = refs[-5:]
    me = me_ref[0]
    for k, ref in enumerate(papers):
        for c in range(2):
            at = pl.multiple_of(((me ^ (2 * k + c)) & (top - 1)) * local, local)
            panel_ref[pl.ds(at, local), :] = theirs_ref[k * local:(k + 1) * local] if c else ref[...]
    exact = functools.partial(jnp.dot, precision=lax.Precision.HIGHEST, preferred_element_type=jnp.float32)
    first, second = inverse_ref[0], inverse_ref[1]
    below = -exact(second, exact(panel_ref[...], first))
    width = first.shape[0]
    table = jnp.concatenate([
        jnp.concatenate([first, jnp.zeros_like(first)], axis=1),
        jnp.concatenate([below, second], axis=1)], axis=0)
    run = spot_ref[...] ^ ((me * local) & mask_ref[...])
    order = lax.broadcasted_iota(jnp.int32, table.shape, 0) == jnp.broadcast_to(run, table.shape)
    order = order.astype(jnp.float32).astype(jnp.bfloat16)
    left = me < top
    for piece, t_ref, b_ref in zip(split(table), (th_ref, tl_ref), (bh_ref, bl_ref)):
        moved = mm(piece, order)
        b_ref[...] = moved[width:].astype(jnp.bfloat16)
        t_ref[...] = jnp.where(left, moved[:width, :width], moved[:width, width:]).astype(jnp.bfloat16)


def mix(me, spots, masks, inverses, papers, theirs, top, local):
    width = inverses.shape[1]
    shapes = [(width, width)] * 2 + [(width, 2 * width)] * 2
    args = [spots, masks, inverses, *papers, theirs]
    return pl.pallas_call(
        functools.partial(mix_kernel, top=top, local=local),
        grid_spec=pltpu.PrefetchScalarGridSpec(
            num_scalar_prefetch=1, grid=(1,),
            in_specs=[whole(a.shape) for a in args],
            out_specs=[whole(shape) for shape in shapes],
            scratch_shapes=[pltpu.VMEM((width, width), jnp.float32)]),
        out_shape=[jax.ShapeDtypeStruct(shape, jnp.bfloat16) for shape in shapes],
        compiler_params=LIMIT,
        name="mix",
    )(me, *args)


def solve_kernel(me_ref, *refs, rows, parts, per, near, far, top):
    count = len(refs) - 6
    w_refs = refs[:count]
    th_ref, tl_ref, bh_ref, bl_ref, o_ref, held_ref = refs[count:]
    stride = rows * parts
    width = th_ref.shape[0]
    left = me_ref[0] // top
    for block, picks in enumerate((near, far)):
        columns = []
        for g in range(per):
            i = pl.program_id(0) * per + g
            for p in range(parts):
                at = p * rows + i
                column = []
                for n, start, size in picks:
                    if start is None:
                        start = (left ^ block) * (size * stride)
                    column.append(w_refs[n][pl.ds(start + at, size, stride=stride), :])
                columns.append(jnp.concatenate(column, axis=0))
        high, low = split(jnp.concatenate(columns, axis=1))
        held_ref[block, 0] = high
        held_ref[block, 1] = low
    th, tl = th_ref[...], tl_ref[...]
    o_ref[:width] = mm(th, held_ref[left, 0]) + mm(th, held_ref[left, 1]) + mm(tl, held_ref[left, 0])
    out = None
    for block in range(2):
        bh = bh_ref[:, block * width:(block + 1) * width]
        bl = bl_ref[:, block * width:(block + 1) * width]
        part = mm(bh, held_ref[block, 0]) + mm(bh, held_ref[block, 1]) + mm(bl, held_ref[block, 0])
        out = part if out is None else out + part
    o_ref[width:] = out


def solve(me, head, got, load, direct, rest, tables, rows, parts, top):
    each = rows * parts
    per = 2 if rows % 2 == 0 else 1
    args = [*outside([head]), *got, load, *outside([*direct, *tables])]
    specs = [parity(a, False) if a.ndim == 3 else whole(a.shape) for a in args]
    pair = lambda n, size: (n, 0, size)
    half_rows = head.shape[0] // each // 2
    near = [(0, None, half_rows)] + [pair(1 + k, rest) for k in range(len(got))]
    near += [pair(1 + len(got), len(got) * rest)]
    far = [(0, None, half_rows)] + [pair(2 + len(got) + k, rest) for k in range(len(direct))]
    width = tables[0].shape[0]
    return pl.pallas_call(
        functools.partial(solve_kernel, rows=rows, parts=parts, per=per, near=tuple(near), far=tuple(far), top=top),
        grid_spec=pltpu.PrefetchScalarGridSpec(
            num_scalar_prefetch=1, grid=(rows // per,), in_specs=specs,
            out_specs=pl.BlockSpec((2 * width, per * parts * LANES), lambda i, me: (0, i)),
            scratch_shapes=[pltpu.VMEM((2, 2, width, per * parts * LANES), jnp.bfloat16)]),
        out_shape=jax.ShapeDtypeStruct((2 * width, each * LANES), jnp.float32),
        compiler_params=LIMIT,
        name="solve",
    )(me, *args)


def precise_dot(a, b):
    return jnp.dot(a, b, precision=lax.Precision.HIGHEST, preferred_element_type=jnp.float32)


def split_outside(x):
    hi = lax.reduce_precision(x, 8, 7)
    return hi.astype(jnp.bfloat16), (x - hi).astype(jnp.bfloat16)


def mixing(block_inverses, panels, total):
    width = block_inverses.shape[1]
    first, second = block_inverses[0], block_inverses[1]
    below = -precise_dot(second, precise_dot(panels[0, width : 2 * width], first))
    top = jnp.concatenate([first, jnp.zeros_like(first)], axis=1)
    rows = [top, jnp.concatenate([below, second], axis=1)]
    if total > 2 * width:
        left, right = panels[0, 2 * width :], panels[1, 2 * width :]
        rows.append(
            -jnp.concatenate(
                [precise_dot(left, first) + precise_dot(right, below), precise_dot(right, second)],
                axis=1,
            )
        )
    return jnp.concatenate(rows, axis=0)


HEAD = 4


def exchange(x, offset):
    pairs = [(i, i ^ offset) for i in range(lax.axis_size("dev"))]
    return lax.ppermute(x, "dev", pairs)


def general(me, runs_field, spectral_filter, block_inverses, factor_panels):
    groups = lax.axis_size("dev")
    local, length, _ = runs_field.shape
    total = local * groups
    front = 2 * block_inverses.shape[1]
    rows, parts = length // groups, length // LANES
    (pieces,) = whiten(me, runs_field, spectral_filter, groups, 0, local, HEAD, False)
    runs = lax.all_to_all(pieces, "dev", 0, 0, tiled=True).reshape(total, parts, rows, LANES)
    panels = lax.all_gather(factor_panels, "dev", axis=1, tiled=True)
    tables = split_outside(mixing(block_inverses, panels, total))
    out = plain_solve(runs[:front].reshape(-1, LANES), *tables, rows, parts)
    if total > front:
        below = jnp.moveaxis(runs[front:], 1, 2).reshape(total - front, -1)
        out = jnp.concatenate([out[:front], out[front:] + below], axis=0)
    return out


def places(groups, local):
    top = groups // 2
    rest = range(HEAD, local)
    ways = list(range(0, top, 2)) + list(range(1, top, 2)) + list(range(top, groups))
    spots, masks = [], []
    for far in range(2):
        for source in range(top):
            spots += [(source + far * top) * local + r for r in range(HEAD)]
            masks += [top * local] * HEAD
        for way in ways[far * top : (far + 1) * top]:
            spots += [way * local + r for r in rest]
            masks += [-1] * len(rest)
    return np.array([spots], np.int32), np.array([masks], np.int32)


def per_device(runs_field, spectral_filter, block_inverses, factor_panels):
    groups = lax.axis_size("dev")
    place = lax.axis_index("dev")
    local, length, _ = runs_field.shape
    width = block_inverses.shape[1]
    rows, parts = length // groups, length // LANES
    chips, top = groups // 2, groups // 2
    me = place.astype(jnp.int32).reshape(1)
    if local * groups != 2 * width:
        return general(me, runs_field, spectral_filter, block_inverses, factor_panels)
    rest = local - HEAD
    near = list(range(1, chips // 2))
    mine = factor_panels[0]
    mine = jnp.where(place < top, exchange(mine, top), mine)
    (head,) = whiten(me, runs_field, spectral_filter, groups, 0, HEAD, HEAD, False)
    head = lax.all_to_all(head, "dev", 0, 0, tiled=True)
    outs = whiten(me, runs_field, spectral_filter, groups, HEAD, rest, HEAD, True)
    got = [outs[0].reshape(2, -1, LANES)]
    papers = [mine]
    for k in near:
        papers.append(exchange(mine, 2 * k))
    for k in near:
        got.append(exchange(outs[k].reshape(2, -1, LANES), 2 * k))
    direct = []
    for way in range(top, groups):
        direct.append(exchange(outs[way - chips // 2].reshape(-1, LANES), way))
    theirs = exchange(stack(me, papers), 1)
    tables = mix(me, *places(groups, local), block_inverses, papers, theirs, top, local)
    load = bundle(me, got)
    load = exchange(load, 1)
    return solve(me, head.reshape(-1, LANES), got, load, direct, rest, tables, rows, parts, top)


def solution(mesh):
    return jax.shard_map(
        per_device,
        mesh=mesh,
        in_specs=(P("dev", None, None), P(), P(), P(None, "dev", None)),
        out_specs=P(None, "dev"),
        check_vma=False,
    )
```

```python
import functools, math
LANES = 128
import numpy as np
import jax, jax.numpy as jnp
from jax import lax
from jax.experimental import pallas as pl
from jax.experimental.pallas import tpu as pltpu
from jax.sharding import PartitionSpec as P


def basis(length):
    half = length // 2
    slot = np.arange(length)
    freq = np.where(slot <= half, slot, slot - half)
    phase = np.outer(np.arange(length), freq) % length
    angle = phase * (2.0 * math.pi / length)
    table = np.where(slot[None, :] <= half, np.cos(angle), np.sin(angle))
    hi = table.astype(jnp.bfloat16)
    lo = (table - hi.astype(np.float64)).astype(jnp.bfloat16)
    return hi, lo


def split(x):
    hi = x.astype(jnp.bfloat16)
    lo = (x - hi.astype(jnp.float32)).astype(jnp.bfloat16)
    return hi, lo


def mm(a, b):
    return lax.dot_general(a, b, (((1,), (0,)), ((), ())), preferred_element_type=jnp.float32)


def gains(filter_t, length):
    half = length // 2
    row = lax.broadcasted_iota(jnp.int32, (length, length), 0)
    col = lax.broadcasted_iota(jnp.int32, (length, length), 1)
    freq = jnp.where(row <= half, row, row - half)
    edge = (freq == 0) | (freq == half)
    plus = (col == freq).astype(jnp.float32)
    minus = (col == length - freq).astype(jnp.float32)
    minus = jnp.where(edge, 0.0, minus)
    plus_only = jnp.where(edge, 0.0, plus)
    sums = (plus + minus).astype(jnp.bfloat16)
    diffs = (plus_only - minus).astype(jnp.bfloat16)
    low = filter_t[:half]
    k = lax.broadcasted_iota(jnp.int32, (half, length), 0)
    high = jnp.where(k == 0, jnp.broadcast_to(filter_t[half:half + 1], (half, length)), low)

    def pick(sel, table):
        out = None
        rest = table
        for _ in range(3):
            piece = rest.astype(jnp.bfloat16)
            rest = rest - piece.astype(jnp.float32)
            part = lax.dot_general(sel, piece, (((1,), (1,)), ((), ())), preferred_element_type=jnp.float32)
            out = part if out is None else out + part
        return out

    tab = jnp.concatenate([low, high], axis=0)
    s = pick(sums, tab)
    d = pick(diffs, tab)
    kk = jnp.where(col <= half, col, col - half)
    kedge = (kk == 0) | (kk == half)
    scale = 1.0 / float(length * length)
    s = s * jnp.where(kedge, scale, 2.0 * scale)
    same = (row < half) == (col < half)
    d = d * jnp.where(kedge, 0.0, jnp.where(same, -2.0 * scale, 2.0 * scale))
    return s, d


def whiten_kernel(me_ref, x_ref, ft_ref, fh_ref, fl_ref, th_ref, tl_ref, *rest, rb, groups, outs):
    o_refs, (g1_ref, g2_ref), stage = rest[:outs], rest[outs:outs + 2], rest[outs + 2:]
    length = x_ref.shape[1]
    half = length // 2

    @pl.when(pl.program_id(0) == 0)
    def _():
        s, d = gains(ft_ref[...], length)
        g1_ref[...] = s
        g2_ref[...] = d

    fh, fl, th, tl = fh_ref[...], fl_ref[...], th_ref[...], tl_ref[...]

    def right(x, h, l):
        xh, xl = split(x)
        return mm(xh, h) + mm(xh, l) + mm(xl, h)

    def left(h, l, x):
        xh, xl = split(x)
        return mm(h, xh) + mm(l, xh) + mm(h, xl)

    z = right(x_ref[...].reshape(rb * length, length), fh, fl)
    vs = []
    for r in range(rb):
        t = left(th, tl, z[r * length:(r + 1) * length])
        sw = jnp.concatenate([
            jnp.concatenate([t[half:, half:], t[half:, :half]], axis=1),
            jnp.concatenate([t[:half, half:], t[:half, :half]], axis=1)], axis=0)
        t = g1_ref[...] * t + g2_ref[...] * sw
        vs.append(left(fh, fl, t))
    y = right(jnp.concatenate(vs, axis=0), th, tl)
    rows = length // groups
    target = stage[0] if stage else o_refs[0]
    for r in range(rb):
        for part in range(length // LANES):
            target[:, r, part] = y[r * length:(r + 1) * length, part * LANES:(part + 1) * LANES].reshape(groups, rows, LANES)
    if stage:
        chip = me_ref[0] // 2
        for k, o_ref in enumerate(o_refs):
            o_ref[...] = target[pl.ds(2 * (chip ^ k), 2)]


def whiten(me, x, spectral_filter, groups, start, count, rb, spread):
    length = x.shape[1]
    rows, parts = length // groups, length // LANES
    fh, fl = basis(length)
    const = lambda shape: pl.BlockSpec(shape, lambda i, me: (0,) * len(shape), pipeline_mode=pl.Buffered(1))
    off = start // rb
    outs, lead = (groups // 2, 2) if spread else (1, groups)
    scratch = [pltpu.VMEM((length, length), jnp.float32)] * 2
    if spread:
        scratch.append(pltpu.VMEM((groups, rb, parts, rows, LANES), jnp.float32))
    return pl.pallas_call(
        functools.partial(whiten_kernel, rb=rb, groups=groups, outs=outs),
        grid_spec=pltpu.PrefetchScalarGridSpec(
            num_scalar_prefetch=1,
            grid=(count // rb,),
            in_specs=[pl.BlockSpec((rb, length, length), lambda i, me: (i + off, 0, 0)),
                      const((spectral_filter.shape[1], length))] + [const((length, length))] * 4,
            out_specs=[pl.BlockSpec((lead, rb, parts, rows, LANES), lambda i, me: (0, i, 0, 0, 0))] * outs,
            scratch_shapes=scratch,
        ),
        out_shape=[jax.ShapeDtypeStruct((lead, count, parts, rows, LANES), jnp.float32)] * outs,
        name="whiten",
    )(me, x, spectral_filter.T, fh, fl, fh.T, fl.T)


def plain_kernel(w_ref, mh_ref, ml_ref, o_ref, *, rows, parts):
    k = mh_ref.shape[1]
    i = pl.program_id(0)
    w = jnp.concatenate([w_ref[pl.ds(p * rows + i, k, stride=rows * parts), :] for p in range(parts)], axis=1)
    wh, wl = split(w)
    o_ref[...] = mm(mh_ref[...], wh) + mm(mh_ref[...], wl) + mm(ml_ref[...], wh)


def plain_solve(w, mh, ml, rows, parts):
    q = mh.shape[0]
    const = lambda a: pl.BlockSpec(a.shape, lambda i: (0,) * a.ndim, pipeline_mode=pl.Buffered(1))
    return pl.pallas_call(
        functools.partial(plain_kernel, rows=rows, parts=parts),
        grid=(rows,),
        in_specs=[const(w), const(mh), const(ml)],
        out_specs=pl.BlockSpec((q, parts * LANES), lambda i: (0, i)),
        out_shape=jax.ShapeDtypeStruct((q, rows * parts * LANES), jnp.float32),
        name="plain",
    )(w, mh, ml)


def whole(shape):
    return pl.BlockSpec(shape, lambda i, me: (0,) * len(shape), pipeline_mode=pl.Buffered(1))


def parity(array, flip):
    pick = (lambda i, me: (1 - me[0] % 2, 0, 0)) if flip else (lambda i, me: (me[0] % 2, 0, 0))
    return pl.BlockSpec((None,) + array.shape[1:], pick, pipeline_mode=pl.Buffered(1))


def bundle_kernel(me_ref, *refs):
    size = refs[0].shape[0]
    for j, ref in enumerate(refs[:-1]):
        refs[-1][j * size:(j + 1) * size] = ref[...]


def bundle(me, arrays):
    size = arrays[0].shape[1]
    shape = (len(arrays) * size, LANES)
    return pl.pallas_call(
        bundle_kernel,
        grid_spec=pltpu.PrefetchScalarGridSpec(
            num_scalar_prefetch=1, grid=(1,), in_specs=[parity(a, True) for a in arrays], out_specs=whole(shape)),
        out_shape=jax.ShapeDtypeStruct(shape, jnp.float32),
        name="bundle",
    )(me, *arrays)


def stack(me, arrays):
    rows, lanes = arrays[0].shape
    shape = (len(arrays) * rows, lanes)
    return pl.pallas_call(
        bundle_kernel,
        grid_spec=pltpu.PrefetchScalarGridSpec(
            num_scalar_prefetch=1, grid=(1,), in_specs=[whole(a.shape) for a in arrays], out_specs=whole(shape)),
        out_shape=jax.ShapeDtypeStruct(shape, jnp.float32),
        name="stack",
    )(me, *arrays)


def mix_kernel(me_ref, spot_ref, mask_ref, inverse_ref, *refs, top, local):
    papers, theirs_ref = refs[:-6], refs[-6]
    th_ref, tl_ref, bh_ref, bl_ref, panel_ref = refs[-5:]
    me = me_ref[0]
    for k, ref in enumerate(papers):
        for c in range(2):
            at = pl.multiple_of(((me ^ (2 * k + c)) & (top - 1)) * local, local)
            panel_ref[pl.ds(at, local), :] = theirs_ref[k * local:(k + 1) * local] if c else ref[...]
    exact = functools.partial(jnp.dot, precision=lax.Precision.HIGHEST, preferred_element_type=jnp.float32)
    first, second = inverse_ref[0], inverse_ref[1]
    below = -exact(second, exact(panel_ref[...], first))
    width = first.shape[0]
    table = jnp.concatenate([
        jnp.concatenate([first, jnp.zeros_like(first)], axis=1),
        jnp.concatenate([below, second], axis=1)], axis=0)
    run = spot_ref[...] ^ ((me * local) & mask_ref[...])
    order = lax.broadcasted_iota(jnp.int32, table.shape, 0) == jnp.broadcast_to(run, table.shape)
    order = order.astype(jnp.float32).astype(jnp.bfloat16)
    left = me < top
    for piece, t_ref, b_ref in zip(split(table), (th_ref, tl_ref), (bh_ref, bl_ref)):
        moved = mm(piece, order)
        b_ref[...] = moved[width:].astype(jnp.bfloat16)
        t_ref[...] = jnp.where(left, moved[:width, :width], moved[:width, width:]).astype(jnp.bfloat16)


def mix(me, spots, masks, inverses, papers, theirs, top, local):
    width = inverses.shape[1]
    shapes = [(width, width)] * 2 + [(width, 2 * width)] * 2
    args = [spots, masks, inverses, *papers, theirs]
    return pl.pallas_call(
        functools.partial(mix_kernel, top=top, local=local),
        grid_spec=pltpu.PrefetchScalarGridSpec(
            num_scalar_prefetch=1, grid=(1,),
            in_specs=[whole(a.shape) for a in args],
            out_specs=[whole(shape) for shape in shapes],
            scratch_shapes=[pltpu.VMEM((width, width), jnp.float32)]),
        out_shape=[jax.ShapeDtypeStruct(shape, jnp.bfloat16) for shape in shapes],
        name="mix",
    )(me, *args)


def solve_kernel(me_ref, *refs, rows, parts, per, near, far, top):
    count = len(refs) - 6
    w_refs = refs[:count]
    th_ref, tl_ref, bh_ref, bl_ref, o_ref, held_ref = refs[count:]
    stride = rows * parts
    width = th_ref.shape[0]
    left = me_ref[0] // top
    for block, picks in enumerate((near, far)):
        columns = []
        for g in range(per):
            i = pl.program_id(0) * per + g
            for p in range(parts):
                at = p * rows + i
                column = []
                for n, start, size in picks:
                    if start is None:
                        start = (left ^ block) * (size * stride)
                    column.append(w_refs[n][pl.ds(start + at, size, stride=stride), :])
                columns.append(jnp.concatenate(column, axis=0))
        high, low = split(jnp.concatenate(columns, axis=1))
        held_ref[block, 0] = high
        held_ref[block, 1] = low
    th, tl = th_ref[...], tl_ref[...]
    o_ref[:width] = mm(th, held_ref[left, 0]) + mm(th, held_ref[left, 1]) + mm(tl, held_ref[left, 0])
    out = None
    for block in range(2):
        bh = bh_ref[:, block * width:(block + 1) * width]
        bl = bl_ref[:, block * width:(block + 1) * width]
        part = mm(bh, held_ref[block, 0]) + mm(bh, held_ref[block, 1]) + mm(bl, held_ref[block, 0])
        out = part if out is None else out + part
    o_ref[width:] = out


def solve(me, head, got, load, final, late, rest, tables, rows, parts, top):
    chips = len(got)
    each = rows * parts
    early = chips - late
    per = 2 if rows % 2 == 0 else 1
    args = [head, *got, load, final, *tables]
    half_rows = head.shape[0] // each // 2
    pair = lambda n, start, size: (n, start * each, size)
    near = [(0, None, half_rows)] + [pair(1 + k, 0, rest) for k in range(chips // 2)]
    near += [pair(1 + chips, 0, chips // 2 * rest)]
    far = [(0, None, half_rows)] + [pair(1 + k, 0, rest) for k in range(chips // 2, chips)]
    far += [pair(1 + chips, chips // 2 * rest, (early - chips // 2) * rest), pair(2 + chips, 0, late * rest)]
    specs = [parity(a, False) if a.ndim == 3 else whole(a.shape) for a in args]
    width = tables[0].shape[0]
    return pl.pallas_call(
        functools.partial(solve_kernel, rows=rows, parts=parts, per=per, near=tuple(near), far=tuple(far), top=top),
        grid_spec=pltpu.PrefetchScalarGridSpec(
            num_scalar_prefetch=1, grid=(rows // per,), in_specs=specs,
            out_specs=pl.BlockSpec((2 * width, per * parts * LANES), lambda i, me: (0, i)),
            scratch_shapes=[pltpu.VMEM((2, 2, width, per * parts * LANES), jnp.bfloat16)]),
        out_shape=jax.ShapeDtypeStruct((2 * width, each * LANES), jnp.float32),
        name="solve",
    )(me, *args)


def precise_dot(a, b):
    return jnp.dot(a, b, precision=lax.Precision.HIGHEST, preferred_element_type=jnp.float32)


def split_outside(x):
    hi = lax.reduce_precision(x, 8, 7)
    return hi.astype(jnp.bfloat16), (x - hi).astype(jnp.bfloat16)


def mixing(block_inverses, panels, total):
    width = block_inverses.shape[1]
    first, second = block_inverses[0], block_inverses[1]
    below = -precise_dot(second, precise_dot(panels[0, width : 2 * width], first))
    top = jnp.concatenate([first, jnp.zeros_like(first)], axis=1)
    rows = [top, jnp.concatenate([below, second], axis=1)]
    if total > 2 * width:
        left, right = panels[0, 2 * width :], panels[1, 2 * width :]
        rows.append(
            -jnp.concatenate(
                [precise_dot(left, first) + precise_dot(right, below), precise_dot(right, second)],
                axis=1,
            )
        )
    return jnp.concatenate(rows, axis=0)


HEAD = 4
LATE = 2


def exchange(x, offset):
    pairs = [(i, i ^ offset) for i in range(lax.axis_size("dev"))]
    return lax.ppermute(x, "dev", pairs)


def general(me, runs_field, spectral_filter, block_inverses, factor_panels):
    groups = lax.axis_size("dev")
    local, length, _ = runs_field.shape
    total = local * groups
    front = 2 * block_inverses.shape[1]
    rows, parts = length // groups, length // LANES
    (pieces,) = whiten(me, runs_field, spectral_filter, groups, 0, local, HEAD, False)
    runs = lax.all_to_all(pieces, "dev", 0, 0, tiled=True).reshape(total, parts, rows, LANES)
    panels = lax.all_gather(factor_panels, "dev", axis=1, tiled=True)
    tables = split_outside(mixing(block_inverses, panels, total))
    out = plain_solve(runs[:front].reshape(-1, LANES), *tables, rows, parts)
    if total > front:
        below = jnp.moveaxis(runs[front:], 1, 2).reshape(total - front, -1)
        out = jnp.concatenate([out[:front], out[front:] + below], axis=0)
    return out


def places(groups, local, early, late):
    top = groups // 2
    rest = range(HEAD, local)
    spots, masks = [], []
    for far in range(2):
        for source in range(top):
            spots += [(source + far * top) * local + r for r in range(HEAD)]
            masks += [top * local] * HEAD
        mine = [k for k in early + late if (2 * k >= top) == bool(far)]
        ways = [2 * k for k in mine]
        ways += [2 * k + 1 for k in mine]
        for way in ways:
            spots += [way * local + r for r in rest]
            masks += [-1] * len(rest)
    return np.array([spots], np.int32), np.array([masks], np.int32)


def per_device(runs_field, spectral_filter, block_inverses, factor_panels):
    groups = lax.axis_size("dev")
    place = lax.axis_index("dev")
    local, length, _ = runs_field.shape
    width = block_inverses.shape[1]
    rows, parts = length // groups, length // LANES
    chips, top = groups // 2, groups // 2
    me = place.astype(jnp.int32).reshape(1)
    if local * groups != 2 * width:
        return general(me, runs_field, spectral_filter, block_inverses, factor_panels)
    rest = local - HEAD
    near = list(range(1, chips // 2))
    far = list(range(chips // 2, chips))
    early, late = [0] + near + far[:-LATE], far[-LATE:]
    mine = factor_panels[0]
    mine = jnp.where(place < top, exchange(mine, top), mine)
    (head,) = whiten(me, runs_field, spectral_filter, groups, 0, HEAD, HEAD, False)
    head = lax.all_to_all(head, "dev", 0, 0, tiled=True)
    outs = whiten(me, runs_field, spectral_filter, groups, HEAD, rest, HEAD, True)
    outs = [o.reshape(2, -1, LANES) for o in outs]
    got = [outs[0]] + [None] * (chips - 1)
    papers = [mine]
    for k in near:
        papers.append(exchange(mine, 2 * k))
    for k in near + far:
        got[k] = exchange(outs[k], 2 * k)
    theirs = exchange(stack(me, papers), 1)
    spots, masks = places(groups, local, early, late)
    tables = mix(me, spots, masks, block_inverses, papers, theirs, top, local)
    load = bundle(me, [got[k] for k in early])
    load = exchange(load, 1)
    final = bundle(me, [got[k] for k in late])
    final = exchange(final, 1)
    return solve(me, head.reshape(-1, LANES), got, load, final, LATE, rest, tables, rows, parts, top)


def solution(mesh):
    return jax.shard_map(
        per_device,
        mesh=mesh,
        in_specs=(P("dev", None, None), P(), P(), P(None, "dev", None)),
        out_specs=P(None, "dev"),
        check_vma=False,
    )
```

```python
import functools, math
LANES = 128
import numpy as np
import jax, jax.numpy as jnp
from jax import lax
from jax.experimental import pallas as pl
from jax.experimental.pallas import tpu as pltpu
from jax.sharding import PartitionSpec as P


def basis(length):
    half = length // 2
    slot = np.arange(length)
    freq = np.where(slot <= half, slot, slot - half)
    phase = np.outer(np.arange(length), freq) % length
    angle = phase * (2.0 * math.pi / length)
    table = np.where(slot[None, :] <= half, np.cos(angle), np.sin(angle))
    hi = table.astype(jnp.bfloat16)
    lo = (table - hi.astype(np.float64)).astype(jnp.bfloat16)
    return hi, lo


def split(x):
    hi = x.astype(jnp.bfloat16)
    lo = (x - hi.astype(jnp.float32)).astype(jnp.bfloat16)
    return hi, lo


def mm(a, b):
    return lax.dot_general(a, b, (((1,), (0,)), ((), ())), preferred_element_type=jnp.float32)


def gains(filter_t, length):
    half = length // 2
    row = lax.broadcasted_iota(jnp.int32, (length, length), 0)
    col = lax.broadcasted_iota(jnp.int32, (length, length), 1)
    freq = jnp.where(row <= half, row, row - half)
    edge = (freq == 0) | (freq == half)
    plus = (col == freq).astype(jnp.float32)
    minus = (col == length - freq).astype(jnp.float32)
    minus = jnp.where(edge, 0.0, minus)
    plus_only = jnp.where(edge, 0.0, plus)
    sums = (plus + minus).astype(jnp.bfloat16)
    diffs = (plus_only - minus).astype(jnp.bfloat16)
    low = filter_t[:half]
    k = lax.broadcasted_iota(jnp.int32, (half, length), 0)
    high = jnp.where(k == 0, jnp.broadcast_to(filter_t[half:half + 1], (half, length)), low)

    def pick(sel, table):
        out = None
        rest = table
        for _ in range(3):
            piece = rest.astype(jnp.bfloat16)
            rest = rest - piece.astype(jnp.float32)
            part = lax.dot_general(sel, piece, (((1,), (1,)), ((), ())), preferred_element_type=jnp.float32)
            out = part if out is None else out + part
        return out

    tab = jnp.concatenate([low, high], axis=0)
    s = pick(sums, tab)
    d = pick(diffs, tab)
    kk = jnp.where(col <= half, col, col - half)
    kedge = (kk == 0) | (kk == half)
    scale = 1.0 / float(length * length)
    s = s * jnp.where(kedge, scale, 2.0 * scale)
    same = (row < half) == (col < half)
    d = d * jnp.where(kedge, 0.0, jnp.where(same, -2.0 * scale, 2.0 * scale))
    return s, d


def whiten_kernel(me_ref, x_ref, ft_ref, fh_ref, fl_ref, th_ref, tl_ref, *rest, rb, groups, outs):
    o_refs, (g1_ref, g2_ref), stage = rest[:outs], rest[outs:outs + 2], rest[outs + 2:]
    length = x_ref.shape[1]
    half = length // 2

    @pl.when(pl.program_id(0) == 0)
    def _():
        s, d = gains(ft_ref[...], length)
        g1_ref[...] = s
        g2_ref[...] = d

    fh, fl, th, tl = fh_ref[...], fl_ref[...], th_ref[...], tl_ref[...]

    def right(x, h, l):
        xh, xl = split(x)
        return mm(xh, h) + mm(xh, l) + mm(xl, h)

    def left(h, l, x):
        xh, xl = split(x)
        return mm(h, xh) + mm(l, xh) + mm(h, xl)

    z = right(x_ref[...].reshape(rb * length, length), fh, fl)
    vs = []
    for r in range(rb):
        t = left(th, tl, z[r * length:(r + 1) * length])
        sw = jnp.concatenate([
            jnp.concatenate([t[half:, half:], t[half:, :half]], axis=1),
            jnp.concatenate([t[:half, half:], t[:half, :half]], axis=1)], axis=0)
        t = g1_ref[...] * t + g2_ref[...] * sw
        vs.append(left(fh, fl, t))
    y = right(jnp.concatenate(vs, axis=0), th, tl)
    rows = length // groups
    target = stage[0] if stage else o_refs[0]
    for r in range(rb):
        for part in range(length // LANES):
            target[:, r, part] = y[r * length:(r + 1) * length, part * LANES:(part + 1) * LANES].reshape(groups, rows, LANES)
    if stage:
        chip = me_ref[0] // 2
        for k, o_ref in enumerate(o_refs[:groups // 4]):
            o_ref[...] = target[pl.ds(2 * (chip ^ k), 2)]
        for way, o_ref in enumerate(o_refs[groups // 4:], groups // 2):
            o_ref[...] = target[pl.ds(me_ref[0] ^ way, 1)]


def whiten(me, x, spectral_filter, groups, start, count, rb, spread):
    length = x.shape[1]
    rows, parts = length // groups, length // LANES
    fh, fl = basis(length)
    const = lambda shape: pl.BlockSpec(shape, lambda i, me: (0,) * len(shape), pipeline_mode=pl.Buffered(1))
    off = start // rb
    leads = [2] * (groups // 4) + [1] * (groups // 2) if spread else [groups]
    scratch = [pltpu.VMEM((length, length), jnp.float32)] * 2
    if spread:
        scratch.append(pltpu.VMEM((groups, rb, parts, rows, LANES), jnp.float32))
    return pl.pallas_call(
        functools.partial(whiten_kernel, rb=rb, groups=groups, outs=len(leads)),
        grid_spec=pltpu.PrefetchScalarGridSpec(
            num_scalar_prefetch=1,
            grid=(count // rb,),
            in_specs=[pl.BlockSpec((rb, length, length), lambda i, me: (i + off, 0, 0)),
                      const((spectral_filter.shape[1], length))] + [const((length, length))] * 4,
            out_specs=[pl.BlockSpec((lead, rb, parts, rows, LANES), lambda i, me: (0, i, 0, 0, 0)) for lead in leads],
            scratch_shapes=scratch,
        ),
        out_shape=[jax.ShapeDtypeStruct((lead, count, parts, rows, LANES), jnp.float32) for lead in leads],
        name="whiten",
    )(me, x, spectral_filter.T, fh, fl, fh.T, fl.T)


def plain_kernel(w_ref, mh_ref, ml_ref, o_ref, *, rows, parts):
    k = mh_ref.shape[1]
    i = pl.program_id(0)
    w = jnp.concatenate([w_ref[pl.ds(p * rows + i, k, stride=rows * parts), :] for p in range(parts)], axis=1)
    wh, wl = split(w)
    o_ref[...] = mm(mh_ref[...], wh) + mm(mh_ref[...], wl) + mm(ml_ref[...], wh)


def plain_solve(w, mh, ml, rows, parts):
    q = mh.shape[0]
    const = lambda a: pl.BlockSpec(a.shape, lambda i: (0,) * a.ndim, pipeline_mode=pl.Buffered(1))
    return pl.pallas_call(
        functools.partial(plain_kernel, rows=rows, parts=parts),
        grid=(rows,),
        in_specs=[const(w), const(mh), const(ml)],
        out_specs=pl.BlockSpec((q, parts * LANES), lambda i: (0, i)),
        out_shape=jax.ShapeDtypeStruct((q, rows * parts * LANES), jnp.float32),
        name="plain",
    )(w, mh, ml)


def whole(shape):
    return pl.BlockSpec(shape, lambda i, me: (0,) * len(shape), pipeline_mode=pl.Buffered(1))


def outside(arrays):
    return [pltpu.with_memory_space_constraint(a, pltpu.HBM) for a in arrays]


def parity(array, flip):
    pick = (lambda i, me: (1 - me[0] % 2, 0, 0)) if flip else (lambda i, me: (me[0] % 2, 0, 0))
    return pl.BlockSpec((None,) + array.shape[1:], pick, pipeline_mode=pl.Buffered(1))


def bundle_kernel(me_ref, *refs):
    size = refs[0].shape[0]
    for j, ref in enumerate(refs[:-1]):
        refs[-1][j * size:(j + 1) * size] = ref[...]


def bundle(me, arrays):
    size = arrays[0].shape[1]
    shape = (len(arrays) * size, LANES)
    return pl.pallas_call(
        bundle_kernel,
        grid_spec=pltpu.PrefetchScalarGridSpec(
            num_scalar_prefetch=1, grid=(1,), in_specs=[parity(a, True) for a in arrays], out_specs=whole(shape)),
        out_shape=jax.ShapeDtypeStruct(shape, jnp.float32),
        name="bundle",
    )(me, *arrays)


def stack(me, arrays):
    rows, lanes = arrays[0].shape
    shape = (len(arrays) * rows, lanes)
    return pl.pallas_call(
        bundle_kernel,
        grid_spec=pltpu.PrefetchScalarGridSpec(
            num_scalar_prefetch=1, grid=(1,), in_specs=[whole(a.shape) for a in arrays], out_specs=whole(shape)),
        out_shape=jax.ShapeDtypeStruct(shape, jnp.float32),
        name="stack",
    )(me, *arrays)


def mix_kernel(me_ref, spot_ref, mask_ref, inverse_ref, *refs, top, local):
    papers, theirs_ref = refs[:-6], refs[-6]
    th_ref, tl_ref, bh_ref, bl_ref, panel_ref = refs[-5:]
    me = me_ref[0]
    for k, ref in enumerate(papers):
        for c in range(2):
            at = pl.multiple_of(((me ^ (2 * k + c)) & (top - 1)) * local, local)
            panel_ref[pl.ds(at, local), :] = theirs_ref[k * local:(k + 1) * local] if c else ref[...]
    exact = functools.partial(jnp.dot, precision=lax.Precision.HIGHEST, preferred_element_type=jnp.float32)
    first, second = inverse_ref[0], inverse_ref[1]
    below = -exact(second, exact(panel_ref[...], first))
    width = first.shape[0]
    table = jnp.concatenate([
        jnp.concatenate([first, jnp.zeros_like(first)], axis=1),
        jnp.concatenate([below, second], axis=1)], axis=0)
    run = spot_ref[...] ^ ((me * local) & mask_ref[...])
    order = lax.broadcasted_iota(jnp.int32, table.shape, 0) == jnp.broadcast_to(run, table.shape)
    order = order.astype(jnp.float32).astype(jnp.bfloat16)
    left = me < top
    for piece, t_ref, b_ref in zip(split(table), (th_ref, tl_ref), (bh_ref, bl_ref)):
        moved = mm(piece, order)
        b_ref[...] = moved[width:].astype(jnp.bfloat16)
        t_ref[...] = jnp.where(left, moved[:width, :width], moved[:width, width:]).astype(jnp.bfloat16)


def mix(me, spots, masks, inverses, papers, theirs, top, local):
    width = inverses.shape[1]
    shapes = [(width, width)] * 2 + [(width, 2 * width)] * 2
    args = [spots, masks, inverses, *papers, theirs]
    return pl.pallas_call(
        functools.partial(mix_kernel, top=top, local=local),
        grid_spec=pltpu.PrefetchScalarGridSpec(
            num_scalar_prefetch=1, grid=(1,),
            in_specs=[whole(a.shape) for a in args],
            out_specs=[whole(shape) for shape in shapes],
            scratch_shapes=[pltpu.VMEM((width, width), jnp.float32)]),
        out_shape=[jax.ShapeDtypeStruct(shape, jnp.bfloat16) for shape in shapes],
        name="mix",
    )(me, *args)


def solve_kernel(me_ref, *refs, rows, parts, per, near, far, top):
    count = len(refs) - 6
    w_refs = refs[:count]
    th_ref, tl_ref, bh_ref, bl_ref, o_ref, held_ref = refs[count:]
    stride = rows * parts
    width = th_ref.shape[0]
    left = me_ref[0] // top
    for block, picks in enumerate((near, far)):
        columns = []
        for g in range(per):
            i = pl.program_id(0) * per + g
            for p in range(parts):
                at = p * rows + i
                column = []
                for n, start, size in picks:
                    if start is None:
                        start = (left ^ block) * (size * stride)
                    column.append(w_refs[n][pl.ds(start + at, size, stride=stride), :])
                columns.append(jnp.concatenate(column, axis=0))
        high, low = split(jnp.concatenate(columns, axis=1))
        held_ref[block, 0] = high
        held_ref[block, 1] = low
    th, tl = th_ref[...], tl_ref[...]
    o_ref[:width] = mm(th, held_ref[left, 0]) + mm(th, held_ref[left, 1]) + mm(tl, held_ref[left, 0])
    out = None
    for block in range(2):
        bh = bh_ref[:, block * width:(block + 1) * width]
        bl = bl_ref[:, block * width:(block + 1) * width]
        part = mm(bh, held_ref[block, 0]) + mm(bh, held_ref[block, 1]) + mm(bl, held_ref[block, 0])
        out = part if out is None else out + part
    o_ref[width:] = out


def solve(me, head, got, load, direct, rest, tables, rows, parts, top):
    each = rows * parts
    per = 2 if rows % 2 == 0 else 1
    args = [*outside([head]), *got, load, *outside([*direct, *tables])]
    specs = [parity(a, False) if a.ndim == 3 else whole(a.shape) for a in args]
    pair = lambda n, size: (n, 0, size)
    half_rows = head.shape[0] // each // 2
    near = [(0, None, half_rows)] + [pair(1 + k, rest) for k in range(len(got))]
    near += [pair(1 + len(got), len(got) * rest)]
    far = [(0, None, half_rows)] + [pair(2 + len(got) + k, rest) for k in range(len(direct))]
    width = tables[0].shape[0]
    return pl.pallas_call(
        functools.partial(solve_kernel, rows=rows, parts=parts, per=per, near=tuple(near), far=tuple(far), top=top),
        grid_spec=pltpu.PrefetchScalarGridSpec(
            num_scalar_prefetch=1, grid=(rows // per,), in_specs=specs,
            out_specs=pl.BlockSpec((2 * width, per * parts * LANES), lambda i, me: (0, i)),
            scratch_shapes=[pltpu.VMEM((2, 2, width, per * parts * LANES), jnp.bfloat16)]),
        out_shape=jax.ShapeDtypeStruct((2 * width, each * LANES), jnp.float32),
        name="solve",
    )(me, *args)


def precise_dot(a, b):
    return jnp.dot(a, b, precision=lax.Precision.HIGHEST, preferred_element_type=jnp.float32)


def split_outside(x):
    hi = lax.reduce_precision(x, 8, 7)
    return hi.astype(jnp.bfloat16), (x - hi).astype(jnp.bfloat16)


def mixing(block_inverses, panels, total):
    width = block_inverses.shape[1]
    first, second = block_inverses[0], block_inverses[1]
    below = -precise_dot(second, precise_dot(panels[0, width : 2 * width], first))
    top = jnp.concatenate([first, jnp.zeros_like(first)], axis=1)
    rows = [top, jnp.concatenate([below, second], axis=1)]
    if total > 2 * width:
        left, right = panels[0, 2 * width :], panels[1, 2 * width :]
        rows.append(
            -jnp.concatenate(
                [precise_dot(left, first) + precise_dot(right, below), precise_dot(right, second)],
                axis=1,
            )
        )
    return jnp.concatenate(rows, axis=0)


HEAD = 4


def exchange(x, offset):
    pairs = [(i, i ^ offset) for i in range(lax.axis_size("dev"))]
    return lax.ppermute(x, "dev", pairs)


def general(me, runs_field, spectral_filter, block_inverses, factor_panels):
    groups = lax.axis_size("dev")
    local, length, _ = runs_field.shape
    total = local * groups
    front = 2 * block_inverses.shape[1]
    rows, parts = length // groups, length // LANES
    (pieces,) = whiten(me, runs_field, spectral_filter, groups, 0, local, HEAD, False)
    runs = lax.all_to_all(pieces, "dev", 0, 0, tiled=True).reshape(total, parts, rows, LANES)
    panels = lax.all_gather(factor_panels, "dev", axis=1, tiled=True)
    tables = split_outside(mixing(block_inverses, panels, total))
    out = plain_solve(runs[:front].reshape(-1, LANES), *tables, rows, parts)
    if total > front:
        below = jnp.moveaxis(runs[front:], 1, 2).reshape(total - front, -1)
        out = jnp.concatenate([out[:front], out[front:] + below], axis=0)
    return out


def places(groups, local):
    top = groups // 2
    rest = range(HEAD, local)
    ways = list(range(0, top, 2)) + list(range(1, top, 2)) + list(range(top, groups))
    spots, masks = [], []
    for far in range(2):
        for source in range(top):
            spots += [(source + far * top) * local + r for r in range(HEAD)]
            masks += [top * local] * HEAD
        for way in ways[far * top : (far + 1) * top]:
            spots += [way * local + r for r in rest]
            masks += [-1] * len(rest)
    return np.array([spots], np.int32), np.array([masks], np.int32)


def per_device(runs_field, spectral_filter, block_inverses, factor_panels):
    groups = lax.axis_size("dev")
    place = lax.axis_index("dev")
    local, length, _ = runs_field.shape
    width = block_inverses.shape[1]
    rows, parts = length // groups, length // LANES
    chips, top = groups // 2, groups // 2
    me = place.astype(jnp.int32).reshape(1)
    if local * groups != 2 * width:
        return general(me, runs_field, spectral_filter, block_inverses, factor_panels)
    rest = local - HEAD
    near = list(range(1, chips // 2))
    mine = factor_panels[0]
    mine = jnp.where(place < top, exchange(mine, top), mine)
    (head,) = whiten(me, runs_field, spectral_filter, groups, 0, HEAD, HEAD, False)
    head = lax.all_to_all(head, "dev", 0, 0, tiled=True)
    outs = whiten(me, runs_field, spectral_filter, groups, HEAD, rest, HEAD, True)
    got = [outs[0].reshape(2, -1, LANES)]
    papers = [mine]
    for k in near:
        papers.append(exchange(mine, 2 * k))
    for k in near:
        got.append(exchange(outs[k].reshape(2, -1, LANES), 2 * k))
    direct = []
    for way in range(top, groups):
        direct.append(exchange(outs[way - chips // 2].reshape(-1, LANES), way))
    theirs = exchange(stack(me, papers), 1)
    tables = mix(me, *places(groups, local), block_inverses, papers, theirs, top, local)
    load = bundle(me, got)
    load = exchange(load, 1)
    return solve(me, head.reshape(-1, LANES), got, load, direct, rest, tables, rows, parts, top)


def solution(mesh):
    return jax.shard_map(
        per_device,
        mesh=mesh,
        in_specs=(P("dev", None, None), P(), P(), P(None, "dev", None)),
        out_specs=P(None, "dev"),
        check_vma=False,
    )
```

```python
import functools, math
LANES = 128
import numpy as np
import jax, jax.numpy as jnp
from jax import lax
from jax.experimental import pallas as pl
from jax.experimental.pallas import tpu as pltpu
from jax.sharding import PartitionSpec as P


def basis(length):
    half = length // 2
    slot = np.arange(length)
    freq = np.where(slot <= half, slot, slot - half)
    phase = np.outer(np.arange(length), freq) % length
    angle = phase * (2.0 * math.pi / length)
    table = np.where(slot[None, :] <= half, np.cos(angle), np.sin(angle))
    hi = table.astype(jnp.bfloat16)
    lo = (table - hi.astype(np.float64)).astype(jnp.bfloat16)
    return hi, lo


def split(x):
    hi = x.astype(jnp.bfloat16)
    lo = (x - hi.astype(jnp.float32)).astype(jnp.bfloat16)
    return hi, lo


def mm(a, b):
    return lax.dot_general(a, b, (((1,), (0,)), ((), ())), preferred_element_type=jnp.float32)


def gains(filter_t, length):
    half = length // 2
    row = lax.broadcasted_iota(jnp.int32, (length, length), 0)
    col = lax.broadcasted_iota(jnp.int32, (length, length), 1)
    freq = jnp.where(row <= half, row, row - half)
    edge = (freq == 0) | (freq == half)
    plus = (col == freq).astype(jnp.float32)
    minus = (col == length - freq).astype(jnp.float32)
    minus = jnp.where(edge, 0.0, minus)
    plus_only = jnp.where(edge, 0.0, plus)
    sums = (plus + minus).astype(jnp.bfloat16)
    diffs = (plus_only - minus).astype(jnp.bfloat16)
    low = filter_t[:half]
    k = lax.broadcasted_iota(jnp.int32, (half, length), 0)
    high = jnp.where(k == 0, jnp.broadcast_to(filter_t[half:half + 1], (half, length)), low)

    def pick(sel, table):
        out = None
        rest = table
        for _ in range(3):
            piece = rest.astype(jnp.bfloat16)
            rest = rest - piece.astype(jnp.float32)
            part = lax.dot_general(sel, piece, (((1,), (1,)), ((), ())), preferred_element_type=jnp.float32)
            out = part if out is None else out + part
        return out

    tab = jnp.concatenate([low, high], axis=0)
    s = pick(sums, tab)
    d = pick(diffs, tab)
    kk = jnp.where(col <= half, col, col - half)
    kedge = (kk == 0) | (kk == half)
    scale = 1.0 / float(length * length)
    s = s * jnp.where(kedge, scale, 2.0 * scale)
    same = (row < half) == (col < half)
    d = d * jnp.where(kedge, 0.0, jnp.where(same, -2.0 * scale, 2.0 * scale))
    return s, d


def whiten_kernel(me_ref, x_ref, ft_ref, fh_ref, fl_ref, th_ref, tl_ref, *rest, rb, groups, outs):
    o_refs, (g1_ref, g2_ref), stage = rest[:outs], rest[outs:outs + 2], rest[outs + 2:]
    length = x_ref.shape[1]
    half = length // 2

    @pl.when(pl.program_id(0) == 0)
    def _():
        s, d = gains(ft_ref[...], length)
        g1_ref[...] = s
        g2_ref[...] = d

    fh, fl, th, tl = fh_ref[...], fl_ref[...], th_ref[...], tl_ref[...]

    def right(x, h, l):
        xh, xl = split(x)
        return mm(xh, h) + mm(xh, l) + mm(xl, h)

    def left(h, l, x):
        xh, xl = split(x)
        return mm(h, xh) + mm(l, xh) + mm(h, xl)

    z = right(x_ref[...].reshape(rb * length, length), fh, fl)
    vs = []
    for r in range(rb):
        t = left(th, tl, z[r * length:(r + 1) * length])
        sw = jnp.concatenate([
            jnp.concatenate([t[half:, half:], t[half:, :half]], axis=1),
            jnp.concatenate([t[:half, half:], t[:half, :half]], axis=1)], axis=0)
        t = g1_ref[...] * t + g2_ref[...] * sw
        vs.append(left(fh, fl, t))
    y = right(jnp.concatenate(vs, axis=0), th, tl)
    rows = length // groups
    target = stage[0] if stage else o_refs[0]
    for r in range(rb):
        for part in range(length // LANES):
            target[:, r, part] = y[r * length:(r + 1) * length, part * LANES:(part + 1) * LANES].reshape(groups, rows, LANES)
    if stage:
        chip = me_ref[0] // 2
        for k, o_ref in enumerate(o_refs[:groups // 4]):
            o_ref[...] = target[pl.ds(2 * (chip ^ k), 2)]
        for way, o_ref in enumerate(o_refs[groups // 4:], groups // 2):
            o_ref[...] = target[pl.ds(me_ref[0] ^ way, 1)]


def whiten(me, x, spectral_filter, groups, start, count, rb, spread):
    length = x.shape[1]
    rows, parts = length // groups, length // LANES
    fh, fl = basis(length)
    const = lambda shape: pl.BlockSpec(shape, lambda i, me: (0,) * len(shape), pipeline_mode=pl.Buffered(1))
    off = start // rb
    leads = [2] * (groups // 4) + [1] * (groups // 2) if spread else [groups]
    scratch = [pltpu.VMEM((length, length), jnp.float32)] * 2
    if spread:
        scratch.append(pltpu.VMEM((groups, rb, parts, rows, LANES), jnp.float32))
    return pl.pallas_call(
        functools.partial(whiten_kernel, rb=rb, groups=groups, outs=len(leads)),
        grid_spec=pltpu.PrefetchScalarGridSpec(
            num_scalar_prefetch=1,
            grid=(count // rb,),
            in_specs=[pl.BlockSpec((rb, length, length), lambda i, me: (i + off, 0, 0)),
                      const((spectral_filter.shape[1], length))] + [const((length, length))] * 4,
            out_specs=[pl.BlockSpec((lead, rb, parts, rows, LANES), lambda i, me: (0, i, 0, 0, 0)) for lead in leads],
            scratch_shapes=scratch,
        ),
        out_shape=[jax.ShapeDtypeStruct((lead, count, parts, rows, LANES), jnp.float32) for lead in leads],
        name="whiten",
    )(me, x, spectral_filter.T, fh, fl, fh.T, fl.T)


def plain_kernel(w_ref, mh_ref, ml_ref, o_ref, *, rows, parts):
    k = mh_ref.shape[1]
    i = pl.program_id(0)
    w = jnp.concatenate([w_ref[pl.ds(p * rows + i, k, stride=rows * parts), :] for p in range(parts)], axis=1)
    wh, wl = split(w)
    o_ref[...] = mm(mh_ref[...], wh) + mm(mh_ref[...], wl) + mm(ml_ref[...], wh)


def plain_solve(w, mh, ml, rows, parts):
    q = mh.shape[0]
    const = lambda a: pl.BlockSpec(a.shape, lambda i: (0,) * a.ndim, pipeline_mode=pl.Buffered(1))
    return pl.pallas_call(
        functools.partial(plain_kernel, rows=rows, parts=parts),
        grid=(rows,),
        in_specs=[const(w), const(mh), const(ml)],
        out_specs=pl.BlockSpec((q, parts * LANES), lambda i: (0, i)),
        out_shape=jax.ShapeDtypeStruct((q, rows * parts * LANES), jnp.float32),
        name="plain",
    )(w, mh, ml)


def whole(shape):
    return pl.BlockSpec(shape, lambda i, me: (0,) * len(shape), pipeline_mode=pl.Buffered(1))


def outside(arrays):
    return [pltpu.with_memory_space_constraint(a, pltpu.HBM) for a in arrays]


def parity(array, flip):
    pick = (lambda i, me: (1 - me[0] % 2, 0, 0)) if flip else (lambda i, me: (me[0] % 2, 0, 0))
    return pl.BlockSpec((None,) + array.shape[1:], pick, pipeline_mode=pl.Buffered(1))


def bundle_kernel(me_ref, *refs):
    size = refs[0].shape[0]
    for j, ref in enumerate(refs[:-1]):
        refs[-1][j * size:(j + 1) * size] = ref[...]


def bundle(me, arrays):
    size = arrays[0].shape[1]
    shape = (len(arrays) * size, LANES)
    return pl.pallas_call(
        bundle_kernel,
        grid_spec=pltpu.PrefetchScalarGridSpec(
            num_scalar_prefetch=1, grid=(1,), in_specs=[parity(a, True) for a in arrays], out_specs=whole(shape)),
        out_shape=jax.ShapeDtypeStruct(shape, jnp.float32),
        name="bundle",
    )(me, *arrays)


def stack(me, arrays):
    rows, lanes = arrays[0].shape
    shape = (len(arrays) * rows, lanes)
    return pl.pallas_call(
        bundle_kernel,
        grid_spec=pltpu.PrefetchScalarGridSpec(
            num_scalar_prefetch=1, grid=(1,), in_specs=[whole(a.shape) for a in arrays], out_specs=whole(shape)),
        out_shape=jax.ShapeDtypeStruct(shape, jnp.float32),
        name="stack",
    )(me, *arrays)


def mix_kernel(me_ref, *refs, top, local, stages):
    orders, (inverse_ref, *papers, theirs_ref) = refs[:2 * stages], refs[2 * stages:-2 * stages - 1]
    o_refs, panel_ref = refs[-2 * stages - 1:-1], refs[-1]
    me = me_ref[0]
    for k, ref in enumerate(papers):
        for c in range(2):
            at = pl.multiple_of(((me ^ (2 * k + c)) & (top - 1)) * local, local)
            panel_ref[pl.ds(at, local), :] = theirs_ref[k * local:(k + 1) * local] if c else ref[...]
    exact = functools.partial(jnp.dot, precision=lax.Precision.HIGHEST, preferred_element_type=jnp.float32)
    first, second = inverse_ref[0], inverse_ref[1]
    below = -exact(second, exact(panel_ref[...], first))
    table = jnp.concatenate([
        jnp.concatenate([first, jnp.zeros_like(first)], axis=1),
        jnp.concatenate([below, second], axis=1)], axis=0)
    pieces = split(table)
    for n in range(stages):
        spot_ref, mask_ref = orders[2 * n:2 * n + 2]
        run = spot_ref[...] ^ ((me * local) & mask_ref[...])
        shape = (table.shape[0], run.shape[1])
        order = lax.broadcasted_iota(jnp.int32, shape, 0) == jnp.broadcast_to(run, shape)
        order = order.astype(jnp.float32).astype(jnp.bfloat16)
        for piece, o_ref in zip(pieces, o_refs[2 * n:2 * n + 2]):
            o_ref[...] = mm(piece, order).astype(jnp.bfloat16)


def mix(me, orders, inverses, papers, theirs, top, local):
    width = inverses.shape[1]
    flat = [table for order in orders for table in order]
    args = [*flat, inverses, *papers, theirs]
    shapes = [(2 * width, table.shape[1]) for table in flat]
    return pl.pallas_call(
        functools.partial(mix_kernel, top=top, local=local, stages=len(orders)),
        grid_spec=pltpu.PrefetchScalarGridSpec(
            num_scalar_prefetch=1, grid=(1,),
            in_specs=[whole(a.shape) for a in args],
            out_specs=[whole(shape) for shape in shapes],
            scratch_shapes=[pltpu.VMEM((width, width), jnp.float32)]),
        out_shape=[jax.ShapeDtypeStruct(shape, jnp.bfloat16) for shape in shapes],
        name="mix",
    )(me, *args)


def solve_kernel(me_ref, *refs, rows, parts, per, sizes, acc):
    n = len(sizes)
    mh_ref, ml_ref = refs[n:n + 2]
    o_ref = refs[-1]
    columns = []
    for g in range(per):
        i = pl.program_id(0) * per + g
        for p in range(parts):
            column = [ref[pl.ds(p * rows + i, k, stride=rows * parts), :] for ref, k in zip(refs, sizes)]
            columns.append(jnp.concatenate(column, axis=0))
    wh, wl = split(jnp.concatenate(columns, axis=1))
    mh, ml = mh_ref[...], ml_ref[...]
    out = mm(mh, wh) + mm(mh, wl) + mm(ml, wh)
    o_ref[...] = out + refs[n + 2][...] if acc else out


def solve(me, pieces, tables, rows, parts, acc=None):
    each = rows * parts
    per = max(d for d in (4, 2, 1) if rows % d == 0)
    width = tables[0].shape[0]
    sizes = [a.shape[-2] // each for a in pieces]
    args = [*pieces, *outside(tables)]
    specs = [parity(a, False) if a.ndim == 3 else whole(a.shape) for a in args]
    tile = pl.BlockSpec((width, per * parts * LANES), lambda i, me: (0, i))
    if acc is not None:
        args.append(acc)
        specs.append(tile)
    return pl.pallas_call(
        functools.partial(solve_kernel, rows=rows, parts=parts, per=per, sizes=tuple(sizes), acc=acc is not None),
        grid_spec=pltpu.PrefetchScalarGridSpec(
            num_scalar_prefetch=1, grid=(rows // per,), in_specs=specs, out_specs=tile),
        out_shape=jax.ShapeDtypeStruct((width, each * LANES), jnp.float32),
        input_output_aliases={} if acc is None else {len(args): 0},
        name="solve",
    )(me, *args)


def precise_dot(a, b):
    return jnp.dot(a, b, precision=lax.Precision.HIGHEST, preferred_element_type=jnp.float32)


def split_outside(x):
    hi = lax.reduce_precision(x, 8, 7)
    return hi.astype(jnp.bfloat16), (x - hi).astype(jnp.bfloat16)


def mixing(block_inverses, panels, total):
    width = block_inverses.shape[1]
    first, second = block_inverses[0], block_inverses[1]
    below = -precise_dot(second, precise_dot(panels[0, width : 2 * width], first))
    top = jnp.concatenate([first, jnp.zeros_like(first)], axis=1)
    rows = [top, jnp.concatenate([below, second], axis=1)]
    if total > 2 * width:
        left, right = panels[0, 2 * width :], panels[1, 2 * width :]
        rows.append(
            -jnp.concatenate(
                [precise_dot(left, first) + precise_dot(right, below), precise_dot(right, second)],
                axis=1,
            )
        )
    return jnp.concatenate(rows, axis=0)


HEAD = 4
SOON = 8


def exchange(x, offset):
    pairs = [(i, i ^ offset) for i in range(lax.axis_size("dev"))]
    return lax.ppermute(x, "dev", pairs)


def general(me, runs_field, spectral_filter, block_inverses, factor_panels):
    groups = lax.axis_size("dev")
    local, length, _ = runs_field.shape
    total = local * groups
    front = 2 * block_inverses.shape[1]
    rows, parts = length // groups, length // LANES
    (pieces,) = whiten(me, runs_field, spectral_filter, groups, 0, local, HEAD, False)
    runs = lax.all_to_all(pieces, "dev", 0, 0, tiled=True).reshape(total, parts, rows, LANES)
    panels = lax.all_gather(factor_panels, "dev", axis=1, tiled=True)
    tables = split_outside(mixing(block_inverses, panels, total))
    out = plain_solve(runs[:front].reshape(-1, LANES), *tables, rows, parts)
    if total > front:
        below = jnp.moveaxis(runs[front:], 1, 2).reshape(total - front, -1)
        out = jnp.concatenate([out[:front], out[front:] + below], axis=0)
    return out


def places(groups, local):
    top = groups // 2
    rest = range(HEAD, local)
    head = [(source * local + r, 0) for source in range(groups) for r in range(HEAD)]
    ways = lambda picks: [(way * local + r, -1) for way in picks for r in rest]
    soon = head + ways(range(0, top, 2)) + ways(range(top, top + SOON))
    last = ways(range(1, top, 2)) + ways(range(top + SOON, groups))
    return [np.array(stage, np.int32).T.reshape(2, 1, -1) for stage in (soon, last)]


def per_device(runs_field, spectral_filter, block_inverses, factor_panels):
    groups = lax.axis_size("dev")
    place = lax.axis_index("dev")
    local, length, _ = runs_field.shape
    width = block_inverses.shape[1]
    rows, parts = length // groups, length // LANES
    chips, top = groups // 2, groups // 2
    me = place.astype(jnp.int32).reshape(1)
    if local * groups != 2 * width:
        return general(me, runs_field, spectral_filter, block_inverses, factor_panels)
    rest = local - HEAD
    near = list(range(1, chips // 2))
    mine = factor_panels[0]
    mine = jnp.where(place < top, exchange(mine, top), mine)
    (head,) = whiten(me, runs_field, spectral_filter, groups, 0, HEAD, HEAD, False)
    head = lax.all_to_all(head, "dev", 0, 0, tiled=True)
    outs = whiten(me, runs_field, spectral_filter, groups, HEAD, rest, HEAD, True)
    got = [outs[0].reshape(2, -1, LANES)]
    papers = [mine]
    for k in near:
        papers.append(exchange(mine, 2 * k))
    for k in near:
        got.append(exchange(outs[k].reshape(2, -1, LANES), 2 * k))
    direct = []
    for way in range(top, groups):
        direct.append(exchange(outs[way - chips // 2].reshape(-1, LANES), way))
    theirs = exchange(stack(me, papers), 1)
    tables = mix(me, places(groups, local), block_inverses, papers, theirs, top, local)
    load = bundle(me, got)
    load = exchange(load, 1)
    out = solve(me, outside([head.reshape(-1, LANES), *got, *direct[:SOON]]), tables[:2], rows, parts)
    return solve(me, [load, *outside(direct[SOON:])], tables[2:], rows, parts, out)


def solution(mesh):
    return jax.shard_map(
        per_device,
        mesh=mesh,
        in_specs=(P("dev", None, None), P(), P(), P(None, "dev", None)),
        out_specs=P(None, "dev"),
        check_vma=False,
    )
```

```python
import functools, math
LANES = 128
import numpy as np
import jax, jax.numpy as jnp
from jax import lax
from jax.experimental import pallas as pl
from jax.experimental.pallas import tpu as pltpu
from jax.sharding import PartitionSpec as P


def basis(length):
    half = length // 2
    slot = np.arange(length)
    freq = np.where(slot <= half, slot, slot - half)
    phase = np.outer(np.arange(length), freq) % length
    angle = phase * (2.0 * math.pi / length)
    table = np.where(slot[None, :] <= half, np.cos(angle), np.sin(angle))
    hi = table.astype(jnp.bfloat16)
    lo = (table - hi.astype(np.float64)).astype(jnp.bfloat16)
    return hi, lo


def split(x):
    hi = x.astype(jnp.bfloat16)
    lo = (x - hi.astype(jnp.float32)).astype(jnp.bfloat16)
    return hi, lo


def mm(a, b):
    return lax.dot_general(a, b, (((1,), (0,)), ((), ())), preferred_element_type=jnp.float32)


def gains(filter_t, length):
    half = length // 2
    row = lax.broadcasted_iota(jnp.int32, (length, length), 0)
    col = lax.broadcasted_iota(jnp.int32, (length, length), 1)
    freq = jnp.where(row <= half, row, row - half)
    edge = (freq == 0) | (freq == half)
    plus = (col == freq).astype(jnp.float32)
    minus = (col == length - freq).astype(jnp.float32)
    minus = jnp.where(edge, 0.0, minus)
    plus_only = jnp.where(edge, 0.0, plus)
    sums = (plus + minus).astype(jnp.bfloat16)
    diffs = (plus_only - minus).astype(jnp.bfloat16)
    low = filter_t[:half]
    k = lax.broadcasted_iota(jnp.int32, (half, length), 0)
    high = jnp.where(k == 0, jnp.broadcast_to(filter_t[half:half + 1], (half, length)), low)

    def pick(sel, table):
        out = None
        rest = table
        for _ in range(3):
            piece = rest.astype(jnp.bfloat16)
            rest = rest - piece.astype(jnp.float32)
            part = lax.dot_general(sel, piece, (((1,), (1,)), ((), ())), preferred_element_type=jnp.float32)
            out = part if out is None else out + part
        return out

    tab = jnp.concatenate([low, high], axis=0)
    s = pick(sums, tab)
    d = pick(diffs, tab)
    kk = jnp.where(col <= half, col, col - half)
    kedge = (kk == 0) | (kk == half)
    scale = 1.0 / float(length * length)
    s = s * jnp.where(kedge, scale, 2.0 * scale)
    same = (row < half) == (col < half)
    d = d * jnp.where(kedge, 0.0, jnp.where(same, -2.0 * scale, 2.0 * scale))
    return s, d


def whiten_kernel(me_ref, x_ref, ft_ref, fh_ref, fl_ref, th_ref, tl_ref, *rest, rb, groups, outs):
    o_refs, (g1_ref, g2_ref), stage = rest[:outs], rest[outs:outs + 2], rest[outs + 2:]
    length = x_ref.shape[1]
    half = length // 2

    @pl.when(pl.program_id(0) == 0)
    def _():
        s, d = gains(ft_ref[...], length)
        g1_ref[...] = s
        g2_ref[...] = d

    fh, fl, th, tl = fh_ref[...], fl_ref[...], th_ref[...], tl_ref[...]

    def right(x, h, l):
        xh, xl = split(x)
        return mm(xh, h) + mm(xh, l) + mm(xl, h)

    def left(h, l, x):
        xh, xl = split(x)
        return mm(h, xh) + mm(l, xh) + mm(h, xl)

    z = right(x_ref[...].reshape(rb * length, length), fh, fl)
    vs = []
    for r in range(rb):
        t = left(th, tl, z[r * length:(r + 1) * length])
        sw = jnp.concatenate([
            jnp.concatenate([t[half:, half:], t[half:, :half]], axis=1),
            jnp.concatenate([t[:half, half:], t[:half, :half]], axis=1)], axis=0)
        t = g1_ref[...] * t + g2_ref[...] * sw
        vs.append(left(fh, fl, t))
    y = right(jnp.concatenate(vs, axis=0), th, tl)
    rows = length // groups
    target = stage[0] if stage else o_refs[0]
    for r in range(rb):
        for part in range(length // LANES):
            target[:, r, part] = y[r * length:(r + 1) * length, part * LANES:(part + 1) * LANES].reshape(groups, rows, LANES)
    if stage:
        chip = me_ref[0] // 2
        for k, o_ref in enumerate(o_refs[:groups // 4]):
            o_ref[...] = target[pl.ds(2 * (chip ^ k), 2)]
        for way, o_ref in enumerate(o_refs[groups // 4:], groups // 2):
            o_ref[...] = target[pl.ds(me_ref[0] ^ way, 1)]


def whiten(me, x, spectral_filter, groups, start, count, rb, spread):
    length = x.shape[1]
    rows, parts = length // groups, length // LANES
    fh, fl = basis(length)
    const = lambda shape: pl.BlockSpec(shape, lambda i, me: (0,) * len(shape), pipeline_mode=pl.Buffered(1))
    off = start // rb
    leads = [2] * (groups // 4) + [1] * (groups // 2) if spread else [groups]
    scratch = [pltpu.VMEM((length, length), jnp.float32)] * 2
    if spread:
        scratch.append(pltpu.VMEM((groups, rb, parts, rows, LANES), jnp.float32))
    return pl.pallas_call(
        functools.partial(whiten_kernel, rb=rb, groups=groups, outs=len(leads)),
        grid_spec=pltpu.PrefetchScalarGridSpec(
            num_scalar_prefetch=1,
            grid=(count // rb,),
            in_specs=[pl.BlockSpec((rb, length, length), lambda i, me: (i + off, 0, 0)),
                      const((spectral_filter.shape[1], length))] + [const((length, length))] * 4,
            out_specs=[pl.BlockSpec((lead, rb, parts, rows, LANES), lambda i, me: (0, i, 0, 0, 0)) for lead in leads],
            scratch_shapes=scratch,
        ),
        out_shape=[jax.ShapeDtypeStruct((lead, count, parts, rows, LANES), jnp.float32) for lead in leads],
        name="whiten",
    )(me, x, spectral_filter.T, fh, fl, fh.T, fl.T)


def plain_kernel(w_ref, mh_ref, ml_ref, o_ref, *, rows, parts):
    k = mh_ref.shape[1]
    i = pl.program_id(0)
    w = jnp.concatenate([w_ref[pl.ds(p * rows + i, k, stride=rows * parts), :] for p in range(parts)], axis=1)
    wh, wl = split(w)
    o_ref[...] = mm(mh_ref[...], wh) + mm(mh_ref[...], wl) + mm(ml_ref[...], wh)


def plain_solve(w, mh, ml, rows, parts):
    q = mh.shape[0]
    const = lambda a: pl.BlockSpec(a.shape, lambda i: (0,) * a.ndim, pipeline_mode=pl.Buffered(1))
    return pl.pallas_call(
        functools.partial(plain_kernel, rows=rows, parts=parts),
        grid=(rows,),
        in_specs=[const(w), const(mh), const(ml)],
        out_specs=pl.BlockSpec((q, parts * LANES), lambda i: (0, i)),
        out_shape=jax.ShapeDtypeStruct((q, rows * parts * LANES), jnp.float32),
        name="plain",
    )(w, mh, ml)


def whole(shape):
    return pl.BlockSpec(shape, lambda i, me: (0,) * len(shape), pipeline_mode=pl.Buffered(1))


def outside(arrays):
    return [pltpu.with_memory_space_constraint(a, pltpu.HBM) for a in arrays]


def parity(array, flip):
    pick = (lambda i, me: (1 - me[0] % 2, 0, 0)) if flip else (lambda i, me: (me[0] % 2, 0, 0))
    return pl.BlockSpec((None,) + array.shape[1:], pick, pipeline_mode=pl.Buffered(1))


def bundle_kernel(me_ref, *refs):
    size = refs[0].shape[0]
    for j, ref in enumerate(refs[:-1]):
        refs[-1][j * size:(j + 1) * size] = ref[...]


def bundle(me, arrays):
    size = arrays[0].shape[1]
    shape = (len(arrays) * size, LANES)
    return pl.pallas_call(
        bundle_kernel,
        grid_spec=pltpu.PrefetchScalarGridSpec(
            num_scalar_prefetch=1, grid=(1,), in_specs=[parity(a, True) for a in arrays], out_specs=whole(shape)),
        out_shape=jax.ShapeDtypeStruct(shape, jnp.float32),
        name="bundle",
    )(me, *arrays)


def stack(me, arrays):
    rows, lanes = arrays[0].shape
    shape = (len(arrays) * rows, lanes)
    return pl.pallas_call(
        bundle_kernel,
        grid_spec=pltpu.PrefetchScalarGridSpec(
            num_scalar_prefetch=1, grid=(1,), in_specs=[whole(a.shape) for a in arrays], out_specs=whole(shape)),
        out_shape=jax.ShapeDtypeStruct(shape, jnp.float32),
        name="stack",
    )(me, *arrays)


def mix_kernel(me_ref, *refs, top, local, stages):
    orders, (inverse_ref, *papers, theirs_ref) = refs[:2 * stages], refs[2 * stages:-2 * stages - 1]
    o_refs, panel_ref = refs[-2 * stages - 1:-1], refs[-1]
    me = me_ref[0]
    for k, ref in enumerate(papers):
        for c in range(2):
            at = pl.multiple_of(((me ^ (2 * k + c)) & (top - 1)) * local, local)
            panel_ref[pl.ds(at, local), :] = theirs_ref[k * local:(k + 1) * local] if c else ref[...]
    exact = functools.partial(jnp.dot, precision=lax.Precision.HIGHEST, preferred_element_type=jnp.float32)
    first, second = inverse_ref[0], inverse_ref[1]
    below = -exact(second, exact(panel_ref[...], first))
    table = jnp.concatenate([
        jnp.concatenate([first, jnp.zeros_like(first)], axis=1),
        jnp.concatenate([below, second], axis=1)], axis=0)
    pieces = split(table)
    for n in range(stages):
        spot_ref, mask_ref = orders[2 * n:2 * n + 2]
        run = spot_ref[...] ^ ((me * local) & mask_ref[...])
        shape = (table.shape[0], run.shape[1])
        order = lax.broadcasted_iota(jnp.int32, shape, 0) == jnp.broadcast_to(run, shape)
        order = order.astype(jnp.float32).astype(jnp.bfloat16)
        for piece, o_ref in zip(pieces, o_refs[2 * n:2 * n + 2]):
            o_ref[...] = mm(piece, order).astype(jnp.bfloat16)


def mix(me, orders, inverses, papers, theirs, top, local):
    width = inverses.shape[1]
    flat = [table for order in orders for table in order]
    args = [*flat, inverses, *papers, theirs]
    shapes = [(2 * width, table.shape[1]) for table in flat]
    return pl.pallas_call(
        functools.partial(mix_kernel, top=top, local=local, stages=len(orders)),
        grid_spec=pltpu.PrefetchScalarGridSpec(
            num_scalar_prefetch=1, grid=(1,),
            in_specs=[whole(a.shape) for a in args],
            out_specs=[whole(shape) for shape in shapes],
            scratch_shapes=[pltpu.VMEM((width, width), jnp.float32)]),
        out_shape=[jax.ShapeDtypeStruct(shape, jnp.bfloat16) for shape in shapes],
        name="mix",
    )(me, *args)


def solve_kernel(me_ref, *refs, rows, parts, per, sizes, acc):
    n = len(sizes)
    mh_ref, ml_ref = refs[n:n + 2]
    o_ref = refs[-1]
    columns = []
    for g in range(per):
        i = pl.program_id(0) * per + g
        for p in range(parts):
            column = [ref[pl.ds(p * rows + i, k, stride=rows * parts), :] for ref, k in zip(refs, sizes)]
            columns.append(jnp.concatenate(column, axis=0))
    wh, wl = split(jnp.concatenate(columns, axis=1))
    mh, ml = mh_ref[...], ml_ref[...]
    out = mm(mh, wh) + mm(mh, wl) + mm(ml, wh)
    o_ref[...] = out + refs[n + 2][...] if acc else out


def solve(me, pieces, tables, rows, parts, acc=None):
    each = rows * parts
    per = max(d for d in (4, 2, 1) if rows % d == 0)
    width = tables[0].shape[0]
    sizes = [a.shape[-2] // each for a in pieces]
    args = [*pieces, *outside(tables)]
    specs = [parity(a, False) if a.ndim == 3 else whole(a.shape) for a in args]
    tile = pl.BlockSpec((width, per * parts * LANES), lambda i, me: (0, i))
    if acc is not None:
        args.append(acc)
        specs.append(tile)
    return pl.pallas_call(
        functools.partial(solve_kernel, rows=rows, parts=parts, per=per, sizes=tuple(sizes), acc=acc is not None),
        grid_spec=pltpu.PrefetchScalarGridSpec(
            num_scalar_prefetch=1, grid=(rows // per,), in_specs=specs, out_specs=tile),
        out_shape=jax.ShapeDtypeStruct((width, each * LANES), jnp.float32),
        input_output_aliases={} if acc is None else {len(args): 0},
        compiler_params=None if acc is None else pltpu.CompilerParams(vmem_limit_bytes=24 << 20),
        name="solve",
    )(me, *args)


def precise_dot(a, b):
    return jnp.dot(a, b, precision=lax.Precision.HIGHEST, preferred_element_type=jnp.float32)


def split_outside(x):
    hi = lax.reduce_precision(x, 8, 7)
    return hi.astype(jnp.bfloat16), (x - hi).astype(jnp.bfloat16)


def mixing(block_inverses, panels, total):
    width = block_inverses.shape[1]
    first, second = block_inverses[0], block_inverses[1]
    below = -precise_dot(second, precise_dot(panels[0, width : 2 * width], first))
    top = jnp.concatenate([first, jnp.zeros_like(first)], axis=1)
    rows = [top, jnp.concatenate([below, second], axis=1)]
    if total > 2 * width:
        left, right = panels[0, 2 * width :], panels[1, 2 * width :]
        rows.append(
            -jnp.concatenate(
                [precise_dot(left, first) + precise_dot(right, below), precise_dot(right, second)],
                axis=1,
            )
        )
    return jnp.concatenate(rows, axis=0)


HEAD = 4
SOON = 6
NEAR_SOON = 5


def exchange(x, offset):
    pairs = [(i, i ^ offset) for i in range(lax.axis_size("dev"))]
    return lax.ppermute(x, "dev", pairs)


def general(me, runs_field, spectral_filter, block_inverses, factor_panels):
    groups = lax.axis_size("dev")
    local, length, _ = runs_field.shape
    total = local * groups
    front = 2 * block_inverses.shape[1]
    rows, parts = length // groups, length // LANES
    (pieces,) = whiten(me, runs_field, spectral_filter, groups, 0, local, HEAD, False)
    runs = lax.all_to_all(pieces, "dev", 0, 0, tiled=True).reshape(total, parts, rows, LANES)
    panels = lax.all_gather(factor_panels, "dev", axis=1, tiled=True)
    tables = split_outside(mixing(block_inverses, panels, total))
    out = plain_solve(runs[:front].reshape(-1, LANES), *tables, rows, parts)
    if total > front:
        below = jnp.moveaxis(runs[front:], 1, 2).reshape(total - front, -1)
        out = jnp.concatenate([out[:front], out[front:] + below], axis=0)
    return out


def places(groups, local):
    top = groups // 2
    rest = range(HEAD, local)
    head = [(source * local + r, 0) for source in range(groups) for r in range(HEAD)]
    ways = lambda picks: [(way * local + r, -1) for way in picks for r in rest]
    near, far = list(range(0, top, 2)), list(range(top, groups))
    soon = head + ways(near[:NEAR_SOON]) + ways(far[:SOON])
    last = ways(range(1, top, 2)) + ways(near[NEAR_SOON:]) + ways(far[SOON:])
    return [np.array(stage, np.int32).T.reshape(2, 1, -1) for stage in (soon, last)]


def per_device(runs_field, spectral_filter, block_inverses, factor_panels):
    groups = lax.axis_size("dev")
    place = lax.axis_index("dev")
    local, length, _ = runs_field.shape
    width = block_inverses.shape[1]
    rows, parts = length // groups, length // LANES
    chips, top = groups // 2, groups // 2
    me = place.astype(jnp.int32).reshape(1)
    if local * groups != 2 * width:
        return general(me, runs_field, spectral_filter, block_inverses, factor_panels)
    rest = local - HEAD
    near = list(range(1, chips // 2))
    mine = factor_panels[0]
    mine = jnp.where(place < top, exchange(mine, top), mine)
    (head,) = whiten(me, runs_field, spectral_filter, groups, 0, HEAD, HEAD, False)
    head = lax.all_to_all(head, "dev", 0, 0, tiled=True)
    outs = whiten(me, runs_field, spectral_filter, groups, HEAD, rest, HEAD, True)
    got = [outs[0].reshape(2, -1, LANES)]
    papers = [mine]
    for k in near:
        papers.append(exchange(mine, 2 * k))
    for k in near:
        got.append(exchange(outs[k].reshape(2, -1, LANES), 2 * k))
    direct = []
    for way in range(top, groups):
        direct.append(exchange(outs[way - chips // 2].reshape(-1, LANES), way))
    theirs = exchange(stack(me, papers), 1)
    tables = mix(me, places(groups, local), block_inverses, papers, theirs, top, local)
    load = bundle(me, got)
    load = exchange(load, 1)
    out = solve(me, outside([head.reshape(-1, LANES), *got[:NEAR_SOON], *direct[:SOON]]), tables[:2], rows, parts)
    return solve(me, [load, *outside(got[NEAR_SOON:]), *direct[SOON:]], tables[2:], rows, parts, out)


def solution(mesh):
    return jax.shard_map(
        per_device,
        mesh=mesh,
        in_specs=(P("dev", None, None), P(), P(), P(None, "dev", None)),
        out_specs=P(None, "dev"),
        check_vma=False,
    )
```

```python
import functools, math
LANES = 128
import numpy as np
import jax, jax.numpy as jnp
from jax import lax
from jax.experimental import pallas as pl
from jax.experimental.pallas import tpu as pltpu
from jax.sharding import PartitionSpec as P


def basis(length):
    half, quarter = length // 2, length // 4
    slot = np.arange(half)
    tables = []
    for freq, cosine in (
        (np.where(slot <= quarter, 2 * slot, 2 * slot - half), slot <= quarter),
        (2 * (slot % quarter) + 1, slot < quarter),
    ):
        angle = (np.outer(np.arange(half), freq) % length) * (2.0 * math.pi / length)
        table = np.where(cosine[None, :], np.cos(angle), np.sin(angle))
        hi = table.astype(jnp.bfloat16)
        lo = (table - hi.astype(np.float64)).astype(jnp.bfloat16)
        ahead = np.block([[hi, lo], [hi, lo]])
        back = np.block([[hi.T, lo.T], [hi.T, lo.T]])
        tables += [ahead, ahead.T, back, back.T]
    return tables


def split(x):
    hi = x.astype(jnp.bfloat16)
    lo = (x - hi.astype(jnp.float32)).astype(jnp.bfloat16)
    return hi, lo


def mm(a, b):
    return lax.dot_general(a, b, (((1,), (0,)), ((), ())), preferred_element_type=jnp.float32)


def exact_pick(sel, table, dims):
    out, rest = None, table
    for _ in range(3):
        piece = rest.astype(jnp.bfloat16)
        rest = rest - piece.astype(jnp.float32)
        part = lax.dot_general(sel, piece, (dims, ((), ())), preferred_element_type=jnp.float32)
        out = part if out is None else out + part
    return out


def frequency(slot, length):
    half, quarter = length // 2, length // 4
    within = slot & (half - 1)
    even = jnp.where(within <= quarter, 2 * within, 2 * within - half)
    odd = 2 * (slot & (quarter - 1)) + 1
    return jnp.where(slot < half, even, odd), within < quarter


def gains(filter_t, length):
    half = length // 2
    row = lax.broadcasted_iota(jnp.int32, (length, length), 0)
    col = lax.broadcasted_iota(jnp.int32, (length, length), 1)
    freq, kind = frequency(row, length)
    edge = (freq == 0) | (freq == half)
    plus = (col == freq).astype(jnp.float32)
    minus = jnp.where(edge, 0.0, (col == length - freq).astype(jnp.float32))
    sums = (plus + minus).astype(jnp.bfloat16)
    diffs = (jnp.where(edge, 0.0, plus) - minus).astype(jnp.bfloat16)
    table = exact_pick(plus[:, :half].astype(jnp.bfloat16), filter_t[:half], ((1,), (0,)))
    table = jnp.where(freq == half, jnp.broadcast_to(filter_t[half:half + 1], table.shape), table)
    s = exact_pick(sums, table, ((1,), (1,)))
    d = exact_pick(diffs, table, ((1,), (1,)))
    across, other = frequency(col, length)
    border = (across == 0) | (across == half)
    scale = 1.0 / float(length * length)
    s = s * jnp.where(border, scale, 2.0 * scale)
    d = d * jnp.where(border, 0.0, jnp.where(kind == other, -2.0 * scale, 2.0 * scale))
    return s, d


def whiten_kernel(me_ref, x_ref, ft_ref, *rest, rb, groups, outs):
    tables, rest = rest[:8], rest[8:]
    o_refs, (g1_ref, g2_ref), stage = rest[:outs], rest[outs:outs + 2], rest[outs + 2:]
    length = x_ref.shape[1]
    half, quarter = length // 2, length // 4

    @pl.when(pl.program_id(0) == 0)
    def _():
        s, d = gains(ft_ref[...], length)
        g1_ref[...] = s
        g2_ref[...] = d

    even, even_t, even_back, even_back_t, odd, odd_t, odd_back, odd_back_t = (ref[...] for ref in tables)

    def right(x, table):
        out = mm(jnp.concatenate(split(x), axis=1), table)
        return out[:, :half] + out[:, half:]

    def left(table, x):
        out = mm(table, jnp.concatenate(split(x), axis=0))
        return out[:half] + out[half:]

    x = x_ref[...].reshape(rb * length, length)
    x0, x1 = x[:, :half], x[:, half:]
    z = jnp.concatenate([right(x0 + x1, even), right(x0 - x1, odd)], axis=1)
    vs = []
    for r in range(rb):
        z0, z1 = z[r * length:r * length + half], z[r * length + half:(r + 1) * length]
        t = jnp.concatenate([left(even_t, z0 + z1), left(odd_t, z0 - z1)], axis=0)
        sw = jnp.concatenate([t[q * quarter:(q + 1) * quarter] for q in (1, 0, 3, 2)], axis=0)
        sw = jnp.concatenate([pltpu.roll(sw[:, :half], quarter, 1), pltpu.roll(sw[:, half:], quarter, 1)], axis=1)
        t = g1_ref[...] * t + g2_ref[...] * sw
        e, o = left(even_back_t, t[:half]), left(odd_back_t, t[half:])
        vs += [e + o, e - o]
    v = jnp.concatenate(vs, axis=0)
    e, o = right(v[:, :half], even_back), right(v[:, half:], odd_back)
    y = jnp.concatenate([e + o, e - o], axis=1)
    rows = length // groups
    target = stage[0] if stage else o_refs[0]
    for r in range(rb):
        for part in range(length // LANES):
            target[:, r, part] = y[r * length:(r + 1) * length, part * LANES:(part + 1) * LANES].reshape(groups, rows, LANES)
    if stage:
        chip = me_ref[0] // 2
        for k, o_ref in enumerate(o_refs[:groups // 4]):
            o_ref[...] = target[pl.ds(2 * (chip ^ k), 2)]
        for way, o_ref in enumerate(o_refs[groups // 4:], groups // 2):
            o_ref[...] = target[pl.ds(me_ref[0] ^ way, 1)]


def whiten(me, x, spectral_filter, groups, start, count, rb, spread):
    length = x.shape[1]
    rows, parts = length // groups, length // LANES
    tables = basis(length)
    const = lambda shape: pl.BlockSpec(shape, lambda i, me: (0,) * len(shape), pipeline_mode=pl.Buffered(1))
    off = start // rb
    leads = [2] * (groups // 4) + [1] * (groups // 2) if spread else [groups]
    scratch = [pltpu.VMEM((length, length), jnp.float32)] * 2
    if spread:
        scratch.append(pltpu.VMEM((groups, rb, parts, rows, LANES), jnp.float32))
    return pl.pallas_call(
        functools.partial(whiten_kernel, rb=rb, groups=groups, outs=len(leads)),
        grid_spec=pltpu.PrefetchScalarGridSpec(
            num_scalar_prefetch=1,
            grid=(count // rb,),
            in_specs=[pl.BlockSpec((rb, length, length), lambda i, me: (i + off, 0, 0)),
                      const((spectral_filter.shape[1], length))] + [const((length, length))] * 8,
            out_specs=[pl.BlockSpec((lead, rb, parts, rows, LANES), lambda i, me: (0, i, 0, 0, 0)) for lead in leads],
            scratch_shapes=scratch,
        ),
        out_shape=[jax.ShapeDtypeStruct((lead, count, parts, rows, LANES), jnp.float32) for lead in leads],
        name="whiten",
    )(me, x, spectral_filter.T, *tables)


def plain_kernel(w_ref, mh_ref, ml_ref, o_ref, *, rows, parts):
    k = mh_ref.shape[1]
    i = pl.program_id(0)
    w = jnp.concatenate([w_ref[pl.ds(p * rows + i, k, stride=rows * parts), :] for p in range(parts)], axis=1)
    wh, wl = split(w)
    o_ref[...] = mm(mh_ref[...], wh) + mm(mh_ref[...], wl) + mm(ml_ref[...], wh)


def plain_solve(w, mh, ml, rows, parts):
    q = mh.shape[0]
    const = lambda a: pl.BlockSpec(a.shape, lambda i: (0,) * a.ndim, pipeline_mode=pl.Buffered(1))
    return pl.pallas_call(
        functools.partial(plain_kernel, rows=rows, parts=parts),
        grid=(rows,),
        in_specs=[const(w), const(mh), const(ml)],
        out_specs=pl.BlockSpec((q, parts * LANES), lambda i: (0, i)),
        out_shape=jax.ShapeDtypeStruct((q, rows * parts * LANES), jnp.float32),
        name="plain",
    )(w, mh, ml)


def whole(shape):
    return pl.BlockSpec(shape, lambda i, me: (0,) * len(shape), pipeline_mode=pl.Buffered(1))


def outside(arrays):
    return [pltpu.with_memory_space_constraint(a, pltpu.HBM) for a in arrays]


def parity(array, flip):
    pick = (lambda i, me: (1 - me[0] % 2, 0, 0)) if flip else (lambda i, me: (me[0] % 2, 0, 0))
    return pl.BlockSpec((None,) + array.shape[1:], pick, pipeline_mode=pl.Buffered(1))


def bundle_kernel(me_ref, *refs):
    size = refs[0].shape[0]
    for j, ref in enumerate(refs[:-1]):
        refs[-1][j * size:(j + 1) * size] = ref[...]


def bundle(me, arrays):
    size = arrays[0].shape[1]
    shape = (len(arrays) * size, LANES)
    return pl.pallas_call(
        bundle_kernel,
        grid_spec=pltpu.PrefetchScalarGridSpec(
            num_scalar_prefetch=1, grid=(1,), in_specs=[parity(a, True) for a in arrays], out_specs=whole(shape)),
        out_shape=jax.ShapeDtypeStruct(shape, jnp.float32),
        name="bundle",
    )(me, *arrays)


def stack(me, arrays):
    rows, lanes = arrays[0].shape
    shape = (len(arrays) * rows, lanes)
    return pl.pallas_call(
        bundle_kernel,
        grid_spec=pltpu.PrefetchScalarGridSpec(
            num_scalar_prefetch=1, grid=(1,), in_specs=[whole(a.shape) for a in arrays], out_specs=whole(shape)),
        out_shape=jax.ShapeDtypeStruct(shape, jnp.float32),
        name="stack",
    )(me, *arrays)


def mix_kernel(me_ref, *refs, top, local, stages):
    orders, (inverse_ref, *papers, theirs_ref) = refs[:2 * stages], refs[2 * stages:-2 * stages - 1]
    o_refs, panel_ref = refs[-2 * stages - 1:-1], refs[-1]
    me = me_ref[0]
    for k, ref in enumerate(papers):
        for c in range(2):
            at = pl.multiple_of(((me ^ (2 * k + c)) & (top - 1)) * local, local)
            panel_ref[pl.ds(at, local), :] = theirs_ref[k * local:(k + 1) * local] if c else ref[...]
    exact = functools.partial(jnp.dot, precision=lax.Precision.HIGHEST, preferred_element_type=jnp.float32)
    first, second = inverse_ref[0], inverse_ref[1]
    below = -exact(second, exact(panel_ref[...], first))
    table = jnp.concatenate([
        jnp.concatenate([first, jnp.zeros_like(first)], axis=1),
        jnp.concatenate([below, second], axis=1)], axis=0)
    pieces = split(table)
    for n in range(stages):
        spot_ref, mask_ref = orders[2 * n:2 * n + 2]
        run = spot_ref[...] ^ ((me * local) & mask_ref[...])
        shape = (table.shape[0], run.shape[1])
        order = lax.broadcasted_iota(jnp.int32, shape, 0) == jnp.broadcast_to(run, shape)
        order = order.astype(jnp.float32).astype(jnp.bfloat16)
        for piece, o_ref in zip(pieces, o_refs[2 * n:2 * n + 2]):
            o_ref[...] = mm(piece, order).astype(jnp.bfloat16)


def mix(me, orders, inverses, papers, theirs, top, local):
    width = inverses.shape[1]
    flat = [table for order in orders for table in order]
    args = [*flat, inverses, *papers, theirs]
    shapes = [(2 * width, table.shape[1]) for table in flat]
    return pl.pallas_call(
        functools.partial(mix_kernel, top=top, local=local, stages=len(orders)),
        grid_spec=pltpu.PrefetchScalarGridSpec(
            num_scalar_prefetch=1, grid=(1,),
            in_specs=[whole(a.shape) for a in args],
            out_specs=[whole(shape) for shape in shapes],
            scratch_shapes=[pltpu.VMEM((width, width), jnp.float32)]),
        out_shape=[jax.ShapeDtypeStruct(shape, jnp.bfloat16) for shape in shapes],
        name="mix",
    )(me, *args)


def solve_kernel(me_ref, *refs, rows, parts, per, sizes, acc):
    n = len(sizes)
    mh_ref, ml_ref = refs[n:n + 2]
    o_ref = refs[-1]
    columns = []
    for g in range(per):
        i = pl.program_id(0) * per + g
        for p in range(parts):
            column = [ref[pl.ds(p * rows + i, k, stride=rows * parts), :] for ref, k in zip(refs, sizes)]
            columns.append(jnp.concatenate(column, axis=0))
    wh, wl = split(jnp.concatenate(columns, axis=1))
    mh, ml = mh_ref[...], ml_ref[...]
    out = mm(mh, wh) + mm(mh, wl) + mm(ml, wh)
    o_ref[...] = out + refs[n + 2][...] if acc else out


def solve(me, pieces, tables, rows, parts, acc=None):
    each = rows * parts
    per = max(d for d in (4, 2, 1) if rows % d == 0)
    width = tables[0].shape[0]
    sizes = [a.shape[-2] // each for a in pieces]
    args = [*pieces, *outside(tables)]
    specs = [parity(a, False) if a.ndim == 3 else whole(a.shape) for a in args]
    tile = pl.BlockSpec((width, per * parts * LANES), lambda i, me: (0, i))
    if acc is not None:
        args.append(acc)
        specs.append(tile)
    return pl.pallas_call(
        functools.partial(solve_kernel, rows=rows, parts=parts, per=per, sizes=tuple(sizes), acc=acc is not None),
        grid_spec=pltpu.PrefetchScalarGridSpec(
            num_scalar_prefetch=1, grid=(rows // per,), in_specs=specs, out_specs=tile),
        out_shape=jax.ShapeDtypeStruct((width, each * LANES), jnp.float32),
        input_output_aliases={} if acc is None else {len(args): 0},
        compiler_params=None if acc is None else pltpu.CompilerParams(vmem_limit_bytes=24 << 20),
        name="solve",
    )(me, *args)


def finish_kernel(me_ref, *refs, rows, parts, sizes):
    n = len(sizes)
    mh_ref, ml_ref, acc_ref, o_ref, held_ref, in_sems, out_sems = refs[n:]
    span = parts * LANES
    mh, ml = mh_ref[...], ml_ref[...]

    def tile(ref, i):
        return ref.at[:, i * span:(i + 1) * span]

    def fetch(i):
        return pltpu.make_async_copy(tile(acc_ref, i), held_ref.at[i], in_sems.at[i])

    def store(i):
        return pltpu.make_async_copy(held_ref.at[i], tile(o_ref, i), out_sems.at[i])

    for i in range(rows):
        fetch(i).start()
    for i in range(rows):
        columns = []
        for p in range(parts):
            column = [ref[pl.ds(p * rows + i, k, stride=rows * parts), :] for ref, k in zip(refs, sizes)]
            columns.append(jnp.concatenate(column, axis=0))
        wh, wl = split(jnp.concatenate(columns, axis=1))
        out = mm(mh, wh) + mm(mh, wl) + mm(ml, wh)
        fetch(i).wait()
        held_ref[i] = held_ref[i] + out
        store(i).start()
    for i in range(rows):
        store(i).wait()


def finish(me, pieces, tables, rows, parts, acc):
    each = rows * parts
    width = tables[0].shape[0]
    sizes = [a.shape[-2] // each for a in pieces]
    args = [*pieces, *outside(tables)]
    specs = [parity(a, False) if a.ndim == 3 else whole(a.shape) for a in args]
    return pl.pallas_call(
        functools.partial(finish_kernel, rows=rows, parts=parts, sizes=tuple(sizes)),
        grid_spec=pltpu.PrefetchScalarGridSpec(
            num_scalar_prefetch=1, grid=(1,), in_specs=[*specs, pl.BlockSpec(memory_space=pl.ANY)],
            out_specs=pl.BlockSpec(memory_space=pl.ANY),
            scratch_shapes=[pltpu.VMEM((rows, width, parts * LANES), jnp.float32),
                            pltpu.SemaphoreType.DMA((rows,)), pltpu.SemaphoreType.DMA((rows,))]),
        out_shape=jax.ShapeDtypeStruct((width, each * LANES), jnp.float32),
        input_output_aliases={len(args) + 1: 0},
        compiler_params=pltpu.CompilerParams(vmem_limit_bytes=24 << 20),
        name="finish",
    )(me, *args, acc)


def precise_dot(a, b):
    return jnp.dot(a, b, precision=lax.Precision.HIGHEST, preferred_element_type=jnp.float32)


def split_outside(x):
    hi = lax.reduce_precision(x, 8, 7)
    return hi.astype(jnp.bfloat16), (x - hi).astype(jnp.bfloat16)


def mixing(block_inverses, panels, total):
    width = block_inverses.shape[1]
    first, second = block_inverses[0], block_inverses[1]
    below = -precise_dot(second, precise_dot(panels[0, width : 2 * width], first))
    top = jnp.concatenate([first, jnp.zeros_like(first)], axis=1)
    rows = [top, jnp.concatenate([below, second], axis=1)]
    if total > 2 * width:
        left, right = panels[0, 2 * width :], panels[1, 2 * width :]
        rows.append(
            -jnp.concatenate(
                [precise_dot(left, first) + precise_dot(right, below), precise_dot(right, second)],
                axis=1,
            )
        )
    return jnp.concatenate(rows, axis=0)


HEAD = 4
SOON = 6
NEAR_SOON = 5


def exchange(x, offset):
    pairs = [(i, i ^ offset) for i in range(lax.axis_size("dev"))]
    return lax.ppermute(x, "dev", pairs)


def general(me, runs_field, spectral_filter, block_inverses, factor_panels):
    groups = lax.axis_size("dev")
    local, length, _ = runs_field.shape
    total = local * groups
    front = 2 * block_inverses.shape[1]
    rows, parts = length // groups, length // LANES
    (pieces,) = whiten(me, runs_field, spectral_filter, groups, 0, local, HEAD, False)
    runs = lax.all_to_all(pieces, "dev", 0, 0, tiled=True).reshape(total, parts, rows, LANES)
    panels = lax.all_gather(factor_panels, "dev", axis=1, tiled=True)
    tables = split_outside(mixing(block_inverses, panels, total))
    out = plain_solve(runs[:front].reshape(-1, LANES), *tables, rows, parts)
    if total > front:
        below = jnp.moveaxis(runs[front:], 1, 2).reshape(total - front, -1)
        out = jnp.concatenate([out[:front], out[front:] + below], axis=0)
    return out


def places(groups, local):
    top = groups // 2
    rest = range(HEAD, local)
    head = [(source * local + r, 0) for source in range(groups) for r in range(HEAD)]
    ways = lambda picks: [(way * local + r, -1) for way in picks for r in rest]
    near, far = list(range(0, top, 2)), list(range(top, groups))
    soon = head + ways(near[:NEAR_SOON]) + ways(far[:SOON])
    last = ways(range(1, top, 2)) + ways(near[NEAR_SOON:]) + ways(far[SOON:])
    return [np.array(stage, np.int32).T.reshape(2, 1, -1) for stage in (soon, last)]


def per_device(runs_field, spectral_filter, block_inverses, factor_panels):
    groups = lax.axis_size("dev")
    place = lax.axis_index("dev")
    local, length, _ = runs_field.shape
    width = block_inverses.shape[1]
    rows, parts = length // groups, length // LANES
    chips, top = groups // 2, groups // 2
    me = place.astype(jnp.int32).reshape(1)
    if local * groups != 2 * width:
        return general(me, runs_field, spectral_filter, block_inverses, factor_panels)
    rest = local - HEAD
    near = list(range(1, chips // 2))
    mine = factor_panels[0]
    mine = jnp.where(place < top, exchange(mine, top), mine)
    (head,) = whiten(me, runs_field, spectral_filter, groups, 0, HEAD, HEAD // 2, False)
    head = lax.all_to_all(head, "dev", 0, 0, tiled=True)
    outs = whiten(me, runs_field, spectral_filter, groups, HEAD, rest, HEAD, True)
    got = [outs[0].reshape(2, -1, LANES)]
    papers = [mine]
    for k in near:
        papers.append(exchange(mine, 2 * k))
    for k in near:
        got.append(exchange(outs[k].reshape(2, -1, LANES), 2 * k))
    direct = []
    for way in range(top, groups):
        direct.append(exchange(outs[way - chips // 2].reshape(-1, LANES), way))
    theirs = exchange(stack(me, papers), 1)
    tables = mix(me, places(groups, local), block_inverses, papers, theirs, top, local)
    load = bundle(me, got)
    load = exchange(load, 1)
    out = solve(me, outside([head.reshape(-1, LANES), *got[:NEAR_SOON], *direct[:SOON]]), tables[:2], rows, parts)
    return finish(me, [load, *outside(got[NEAR_SOON:]), *direct[SOON:]], tables[2:], rows, parts, out)


def solution(mesh):
    return jax.shard_map(
        per_device,
        mesh=mesh,
        in_specs=(P("dev", None, None), P(), P(), P(None, "dev", None)),
        out_specs=P(None, "dev"),
        check_vma=False,
    )
```

```python
import functools, math
LANES = 128
import numpy as np
import jax, jax.numpy as jnp
from jax import lax
from jax.experimental import pallas as pl
from jax.experimental.pallas import tpu as pltpu
from jax.sharding import PartitionSpec as P


def basis(length):
    half, quarter = length // 2, length // 4
    slot = np.arange(half)
    tables = []
    for freq, cosine in (
        (np.where(slot <= quarter, 2 * slot, 2 * slot - half), slot <= quarter),
        (2 * (slot % quarter) + 1, slot < quarter),
    ):
        angle = (np.outer(np.arange(half), freq) % length) * (2.0 * math.pi / length)
        table = np.where(cosine[None, :], np.cos(angle), np.sin(angle))
        hi = table.astype(jnp.bfloat16)
        lo = (table - hi.astype(np.float64)).astype(jnp.bfloat16)
        ahead = np.block([[hi, lo], [hi, lo]])
        back = np.block([[hi.T, lo.T], [hi.T, lo.T]])
        tables += [ahead, ahead.T, back, back.T]
    return tables


def split(x):
    hi = x.astype(jnp.bfloat16)
    lo = (x - hi.astype(jnp.float32)).astype(jnp.bfloat16)
    return hi, lo


def mm(a, b):
    return lax.dot_general(a, b, (((1,), (0,)), ((), ())), preferred_element_type=jnp.float32)


def exact_pick(sel, table, dims):
    out, rest = None, table
    for _ in range(3):
        piece = rest.astype(jnp.bfloat16)
        rest = rest - piece.astype(jnp.float32)
        part = lax.dot_general(sel, piece, (dims, ((), ())), preferred_element_type=jnp.float32)
        out = part if out is None else out + part
    return out


def frequency(slot, length):
    half, quarter = length // 2, length // 4
    within = slot & (half - 1)
    even = jnp.where(within <= quarter, 2 * within, 2 * within - half)
    odd = 2 * (slot & (quarter - 1)) + 1
    return jnp.where(slot < half, even, odd), within < quarter


def gains(filter_t, length):
    half = length // 2
    row = lax.broadcasted_iota(jnp.int32, (length, length), 0)
    col = lax.broadcasted_iota(jnp.int32, (length, length), 1)
    freq, kind = frequency(row, length)
    edge = (freq == 0) | (freq == half)
    plus = (col == freq).astype(jnp.float32)
    minus = jnp.where(edge, 0.0, (col == length - freq).astype(jnp.float32))
    sums = (plus + minus).astype(jnp.bfloat16)
    diffs = (jnp.where(edge, 0.0, plus) - minus).astype(jnp.bfloat16)
    table = exact_pick(plus[:, :half].astype(jnp.bfloat16), filter_t[:half], ((1,), (0,)))
    table = jnp.where(freq == half, jnp.broadcast_to(filter_t[half:half + 1], table.shape), table)
    s = exact_pick(sums, table, ((1,), (1,)))
    d = exact_pick(diffs, table, ((1,), (1,)))
    across, other = frequency(col, length)
    border = (across == 0) | (across == half)
    scale = 1.0 / float(length * length)
    s = s * jnp.where(border, scale, 2.0 * scale)
    d = d * jnp.where(border, 0.0, jnp.where(kind == other, -2.0 * scale, 2.0 * scale))
    return s, d


def whiten_kernel(me_ref, x_ref, ft_ref, *rest, rb, groups, outs):
    tables, rest = rest[:8], rest[8:]
    o_refs, (g1_ref, g2_ref), stage = rest[:outs], rest[outs:outs + 2], rest[outs + 2:]
    length = x_ref.shape[1]
    half, quarter = length // 2, length // 4

    @pl.when(pl.program_id(0) == 0)
    def _():
        s, d = gains(ft_ref[...], length)
        g1_ref[...] = s
        g2_ref[...] = d

    even, even_t, even_back, even_back_t, odd, odd_t, odd_back, odd_back_t = (ref[...] for ref in tables)

    def right(x, table):
        out = mm(jnp.concatenate(split(x), axis=1), table)
        return out[:, :half] + out[:, half:]

    def left(table, x):
        out = mm(table, jnp.concatenate(split(x), axis=0))
        return out[:half] + out[half:]

    x = x_ref[...].reshape(rb * length, length)
    x0, x1 = x[:, :half], x[:, half:]
    z = jnp.concatenate([right(x0 + x1, even), right(x0 - x1, odd)], axis=1)
    vs = []
    for r in range(rb):
        z0, z1 = z[r * length:r * length + half], z[r * length + half:(r + 1) * length]
        t = jnp.concatenate([left(even_t, z0 + z1), left(odd_t, z0 - z1)], axis=0)
        sw = jnp.concatenate([t[q * quarter:(q + 1) * quarter] for q in (1, 0, 3, 2)], axis=0)
        sw = jnp.concatenate([pltpu.roll(sw[:, :half], quarter, 1), pltpu.roll(sw[:, half:], quarter, 1)], axis=1)
        t = g1_ref[...] * t + g2_ref[...] * sw
        e, o = left(even_back_t, t[:half]), left(odd_back_t, t[half:])
        vs += [e + o, e - o]
    v = jnp.concatenate(vs, axis=0)
    e, o = right(v[:, :half], even_back), right(v[:, half:], odd_back)
    y = jnp.concatenate([e + o, e - o], axis=1)
    rows = length // groups
    target = stage[0] if stage else o_refs[0]
    for r in range(rb):
        for part in range(length // LANES):
            target[:, r, part] = y[r * length:(r + 1) * length, part * LANES:(part + 1) * LANES].reshape(groups, rows, LANES)
    if stage:
        chip = me_ref[0] // 2
        for k, o_ref in enumerate(o_refs[:groups // 4]):
            o_ref[...] = target[pl.ds(2 * (chip ^ k), 2)]
        for way, o_ref in enumerate(o_refs[groups // 4:], groups // 2):
            o_ref[...] = target[pl.ds(me_ref[0] ^ way, 1)]


def whiten(me, x, spectral_filter, groups, start, count, rb, spread):
    length = x.shape[1]
    rows, parts = length // groups, length // LANES
    tables = basis(length)
    const = lambda shape: pl.BlockSpec(shape, lambda i, me: (0,) * len(shape), pipeline_mode=pl.Buffered(1))
    off = start // rb
    leads = [2] * (groups // 4) + [1] * (groups // 2) if spread else [groups]
    scratch = [pltpu.VMEM((length, length), jnp.float32)] * 2
    if spread:
        scratch.append(pltpu.VMEM((groups, rb, parts, rows, LANES), jnp.float32))
    return pl.pallas_call(
        functools.partial(whiten_kernel, rb=rb, groups=groups, outs=len(leads)),
        grid_spec=pltpu.PrefetchScalarGridSpec(
            num_scalar_prefetch=1,
            grid=(count // rb,),
            in_specs=[pl.BlockSpec((rb, length, length), lambda i, me: (i + off, 0, 0)),
                      const((spectral_filter.shape[1], length))] + [const((length, length))] * 8,
            out_specs=[pl.BlockSpec((lead, rb, parts, rows, LANES), lambda i, me: (0, i, 0, 0, 0)) for lead in leads],
            scratch_shapes=scratch,
        ),
        out_shape=[jax.ShapeDtypeStruct((lead, count, parts, rows, LANES), jnp.float32) for lead in leads],
        name="whiten",
    )(me, x, spectral_filter.T, *tables)


def plain_kernel(w_ref, mh_ref, ml_ref, o_ref, *, rows, parts):
    k = mh_ref.shape[1]
    i = pl.program_id(0)
    w = jnp.concatenate([w_ref[pl.ds(p * rows + i, k, stride=rows * parts), :] for p in range(parts)], axis=1)
    wh, wl = split(w)
    o_ref[...] = mm(mh_ref[...], wh) + mm(mh_ref[...], wl) + mm(ml_ref[...], wh)


def plain_solve(w, mh, ml, rows, parts):
    q = mh.shape[0]
    const = lambda a: pl.BlockSpec(a.shape, lambda i: (0,) * a.ndim, pipeline_mode=pl.Buffered(1))
    return pl.pallas_call(
        functools.partial(plain_kernel, rows=rows, parts=parts),
        grid=(rows,),
        in_specs=[const(w), const(mh), const(ml)],
        out_specs=pl.BlockSpec((q, parts * LANES), lambda i: (0, i)),
        out_shape=jax.ShapeDtypeStruct((q, rows * parts * LANES), jnp.float32),
        name="plain",
    )(w, mh, ml)


def whole(shape):
    return pl.BlockSpec(shape, lambda i, me: (0,) * len(shape), pipeline_mode=pl.Buffered(1))


def outside(arrays):
    return [pltpu.with_memory_space_constraint(a, pltpu.HBM) for a in arrays]


def parity(array, flip):
    pick = (lambda i, me: (1 - me[0] % 2, 0, 0)) if flip else (lambda i, me: (me[0] % 2, 0, 0))
    return pl.BlockSpec((None,) + array.shape[1:], pick, pipeline_mode=pl.Buffered(1))


def bundle_kernel(me_ref, *refs):
    size = refs[0].shape[0]
    for j, ref in enumerate(refs[:-1]):
        refs[-1][j * size:(j + 1) * size] = ref[...]


def bundle(me, arrays):
    size = arrays[0].shape[1]
    shape = (len(arrays) * size, LANES)
    return pl.pallas_call(
        bundle_kernel,
        grid_spec=pltpu.PrefetchScalarGridSpec(
            num_scalar_prefetch=1, grid=(1,), in_specs=[parity(a, True) for a in arrays], out_specs=whole(shape)),
        out_shape=jax.ShapeDtypeStruct(shape, jnp.float32),
        name="bundle",
    )(me, *arrays)


def stack(me, arrays):
    rows, lanes = arrays[0].shape
    shape = (len(arrays) * rows, lanes)
    return pl.pallas_call(
        bundle_kernel,
        grid_spec=pltpu.PrefetchScalarGridSpec(
            num_scalar_prefetch=1, grid=(1,), in_specs=[whole(a.shape) for a in arrays], out_specs=whole(shape)),
        out_shape=jax.ShapeDtypeStruct(shape, jnp.float32),
        name="stack",
    )(me, *arrays)


def mix_kernel(me_ref, *refs, top, local, stages):
    orders, (inverse_ref, *papers, theirs_ref) = refs[:2 * stages], refs[2 * stages:-2 * stages - 1]
    o_refs, panel_ref = refs[-2 * stages - 1:-1], refs[-1]
    me = me_ref[0]
    for k, ref in enumerate(papers):
        for c in range(2):
            at = pl.multiple_of(((me ^ (2 * k + c)) & (top - 1)) * local, local)
            panel_ref[pl.ds(at, local), :] = theirs_ref[k * local:(k + 1) * local] if c else ref[...]
    exact = functools.partial(jnp.dot, precision=lax.Precision.HIGHEST, preferred_element_type=jnp.float32)
    first, second = inverse_ref[0], inverse_ref[1]
    below = -exact(second, exact(panel_ref[...], first))
    table = jnp.concatenate([
        jnp.concatenate([first, jnp.zeros_like(first)], axis=1),
        jnp.concatenate([below, second], axis=1)], axis=0)
    pieces = split(table)
    for n in range(stages):
        spot_ref, mask_ref = orders[2 * n:2 * n + 2]
        run = spot_ref[...] ^ ((me * local) & mask_ref[...])
        shape = (table.shape[0], run.shape[1])
        order = lax.broadcasted_iota(jnp.int32, shape, 0) == jnp.broadcast_to(run, shape)
        order = order.astype(jnp.float32).astype(jnp.bfloat16)
        for piece, o_ref in zip(pieces, o_refs[2 * n:2 * n + 2]):
            o_ref[...] = mm(piece, order).astype(jnp.bfloat16)


def mix(me, orders, inverses, papers, theirs, top, local):
    width = inverses.shape[1]
    flat = [table for order in orders for table in order]
    args = [*flat, inverses, *papers, theirs]
    shapes = [(2 * width, table.shape[1]) for table in flat]
    return pl.pallas_call(
        functools.partial(mix_kernel, top=top, local=local, stages=len(orders)),
        grid_spec=pltpu.PrefetchScalarGridSpec(
            num_scalar_prefetch=1, grid=(1,),
            in_specs=[whole(a.shape) for a in args],
            out_specs=[whole(shape) for shape in shapes],
            scratch_shapes=[pltpu.VMEM((width, width), jnp.float32)]),
        out_shape=[jax.ShapeDtypeStruct(shape, jnp.bfloat16) for shape in shapes],
        name="mix",
    )(me, *args)


def solve_kernel(me_ref, *refs, rows, parts, per, sizes, acc):
    n = len(sizes)
    mh_ref, ml_ref = refs[n:n + 2]
    o_ref = refs[-1]
    columns = []
    for g in range(per):
        i = pl.program_id(0) * per + g
        for p in range(parts):
            column = [ref[pl.ds(p * rows + i, k, stride=rows * parts), :] for ref, k in zip(refs, sizes)]
            columns.append(jnp.concatenate(column, axis=0))
    wh, wl = split(jnp.concatenate(columns, axis=1))
    mh, ml = mh_ref[...], ml_ref[...]
    out = mm(mh, wh) + mm(mh, wl) + mm(ml, wh)
    o_ref[...] = out + refs[n + 2][...] if acc else out


def solve(me, pieces, tables, rows, parts, acc=None):
    each = rows * parts
    per = max(d for d in (4, 2, 1) if rows % d == 0)
    width = tables[0].shape[0]
    sizes = [a.shape[-2] // each for a in pieces]
    args = [*pieces, *outside(tables)]
    specs = [parity(a, False) if a.ndim == 3 else whole(a.shape) for a in args]
    tile = pl.BlockSpec((width, per * parts * LANES), lambda i, me: (0, i))
    if acc is not None:
        args.append(acc)
        specs.append(tile)
    return pl.pallas_call(
        functools.partial(solve_kernel, rows=rows, parts=parts, per=per, sizes=tuple(sizes), acc=acc is not None),
        grid_spec=pltpu.PrefetchScalarGridSpec(
            num_scalar_prefetch=1, grid=(rows // per,), in_specs=specs, out_specs=tile),
        out_shape=jax.ShapeDtypeStruct((width, each * LANES), jnp.float32),
        input_output_aliases={} if acc is None else {len(args): 0},
        compiler_params=None if acc is None else pltpu.CompilerParams(vmem_limit_bytes=24 << 20),
        name="solve",
    )(me, *args)


def precise_dot(a, b):
    return jnp.dot(a, b, precision=lax.Precision.HIGHEST, preferred_element_type=jnp.float32)


def split_outside(x):
    hi = lax.reduce_precision(x, 8, 7)
    return hi.astype(jnp.bfloat16), (x - hi).astype(jnp.bfloat16)


def mixing(block_inverses, panels, total):
    width = block_inverses.shape[1]
    first, second = block_inverses[0], block_inverses[1]
    below = -precise_dot(second, precise_dot(panels[0, width : 2 * width], first))
    top = jnp.concatenate([first, jnp.zeros_like(first)], axis=1)
    rows = [top, jnp.concatenate([below, second], axis=1)]
    if total > 2 * width:
        left, right = panels[0, 2 * width :], panels[1, 2 * width :]
        rows.append(
            -jnp.concatenate(
                [precise_dot(left, first) + precise_dot(right, below), precise_dot(right, second)],
                axis=1,
            )
        )
    return jnp.concatenate(rows, axis=0)


HEAD = 4
SOON = 6
NEAR_SOON = 5


def exchange(x, offset):
    pairs = [(i, i ^ offset) for i in range(lax.axis_size("dev"))]
    return lax.ppermute(x, "dev", pairs)


def general(me, runs_field, spectral_filter, block_inverses, factor_panels):
    groups = lax.axis_size("dev")
    local, length, _ = runs_field.shape
    total = local * groups
    front = 2 * block_inverses.shape[1]
    rows, parts = length // groups, length // LANES
    (pieces,) = whiten(me, runs_field, spectral_filter, groups, 0, local, HEAD, False)
    runs = lax.all_to_all(pieces, "dev", 0, 0, tiled=True).reshape(total, parts, rows, LANES)
    panels = lax.all_gather(factor_panels, "dev", axis=1, tiled=True)
    tables = split_outside(mixing(block_inverses, panels, total))
    out = plain_solve(runs[:front].reshape(-1, LANES), *tables, rows, parts)
    if total > front:
        below = jnp.moveaxis(runs[front:], 1, 2).reshape(total - front, -1)
        out = jnp.concatenate([out[:front], out[front:] + below], axis=0)
    return out


def places(groups, local):
    top = groups // 2
    rest = range(HEAD, local)
    head = [(source * local + r, 0) for source in range(groups) for r in range(HEAD)]
    ways = lambda picks: [(way * local + r, -1) for way in picks for r in rest]
    near, far = list(range(0, top, 2)), list(range(top, groups))
    soon = head + ways(near[:NEAR_SOON]) + ways(far[:SOON])
    last = ways(range(1, top, 2)) + ways(near[NEAR_SOON:]) + ways(far[SOON:])
    return [np.array(stage, np.int32).T.reshape(2, 1, -1) for stage in (soon, last)]


def per_device(runs_field, spectral_filter, block_inverses, factor_panels):
    groups = lax.axis_size("dev")
    place = lax.axis_index("dev")
    local, length, _ = runs_field.shape
    width = block_inverses.shape[1]
    rows, parts = length // groups, length // LANES
    chips, top = groups // 2, groups // 2
    me = place.astype(jnp.int32).reshape(1)
    if local * groups != 2 * width:
        return general(me, runs_field, spectral_filter, block_inverses, factor_panels)
    rest = local - HEAD
    near = list(range(1, chips // 2))
    mine = factor_panels[0]
    mine = jnp.where(place < top, exchange(mine, top), mine)
    (head,) = whiten(me, runs_field, spectral_filter, groups, 0, HEAD, HEAD, False)
    head = lax.all_to_all(head, "dev", 0, 0, tiled=True)
    outs = whiten(me, runs_field, spectral_filter, groups, HEAD, rest, HEAD, True)
    got = [outs[0].reshape(2, -1, LANES)]
    papers = [mine]
    for k in near:
        papers.append(exchange(mine, 2 * k))
    for k in near:
        got.append(exchange(outs[k].reshape(2, -1, LANES), 2 * k))
    direct = []
    for way in range(top, groups):
        direct.append(exchange(outs[way - chips // 2].reshape(-1, LANES), way))
    theirs = exchange(stack(me, papers), 1)
    tables = mix(me, places(groups, local), block_inverses, papers, theirs, top, local)
    load = bundle(me, got)
    load = exchange(load, 1)
    out = solve(me, outside([head.reshape(-1, LANES), *got[:NEAR_SOON], *direct[:SOON]]), tables[:2], rows, parts)
    return solve(me, [load, *outside(got[NEAR_SOON:]), *direct[SOON:]], tables[2:], rows, parts, out)


def solution(mesh):
    return jax.shard_map(
        per_device,
        mesh=mesh,
        in_specs=(P("dev", None, None), P(), P(), P(None, "dev", None)),
        out_specs=P(None, "dev"),
        check_vma=False,
    )
```

```python
import functools, math
LANES = 128
import numpy as np
import jax, jax.numpy as jnp
from jax import lax
from jax.experimental import pallas as pl
from jax.experimental.pallas import tpu as pltpu
from jax.sharding import PartitionSpec as P


def basis(length):
    half, quarter = length // 2, length // 4
    slot = np.arange(half)
    tables = []
    for freq, cosine in (
        (np.where(slot <= quarter, 2 * slot, 2 * slot - half), slot <= quarter),
        (2 * (slot % quarter) + 1, slot < quarter),
    ):
        angle = (np.outer(np.arange(half), freq) % length) * (2.0 * math.pi / length)
        table = np.where(cosine[None, :], np.cos(angle), np.sin(angle))
        hi = table.astype(jnp.bfloat16)
        lo = (table - hi.astype(np.float64)).astype(jnp.bfloat16)
        ahead = np.block([[hi, lo], [hi, lo]])
        back = np.block([[hi.T, lo.T], [hi.T, lo.T]])
        tables += [ahead, ahead.T, back, back.T]
    return tables


def split(x):
    hi = x.astype(jnp.bfloat16)
    lo = (x - hi.astype(jnp.float32)).astype(jnp.bfloat16)
    return hi, lo


def mm(a, b):
    return lax.dot_general(a, b, (((1,), (0,)), ((), ())), preferred_element_type=jnp.float32)


def exact_pick(sel, table, dims):
    out, rest = None, table
    for _ in range(3):
        piece = rest.astype(jnp.bfloat16)
        rest = rest - piece.astype(jnp.float32)
        part = lax.dot_general(sel, piece, (dims, ((), ())), preferred_element_type=jnp.float32)
        out = part if out is None else out + part
    return out


def frequency(slot, length):
    half, quarter = length // 2, length // 4
    within = slot & (half - 1)
    even = jnp.where(within <= quarter, 2 * within, 2 * within - half)
    odd = 2 * (slot & (quarter - 1)) + 1
    return jnp.where(slot < half, even, odd), within < quarter


def gains(filter_t, length):
    half = length // 2
    row = lax.broadcasted_iota(jnp.int32, (length, length), 0)
    col = lax.broadcasted_iota(jnp.int32, (length, length), 1)
    freq, kind = frequency(row, length)
    edge = (freq == 0) | (freq == half)
    plus = (col == freq).astype(jnp.float32)
    minus = jnp.where(edge, 0.0, (col == length - freq).astype(jnp.float32))
    sums = (plus + minus).astype(jnp.bfloat16)
    diffs = (jnp.where(edge, 0.0, plus) - minus).astype(jnp.bfloat16)
    table = exact_pick(plus[:, :half].astype(jnp.bfloat16), filter_t[:half], ((1,), (0,)))
    table = jnp.where(freq == half, jnp.broadcast_to(filter_t[half:half + 1], table.shape), table)
    s = exact_pick(sums, table, ((1,), (1,)))
    d = exact_pick(diffs, table, ((1,), (1,)))
    across, other = frequency(col, length)
    border = (across == 0) | (across == half)
    scale = 1.0 / float(length * length)
    s = s * jnp.where(border, scale, 2.0 * scale)
    d = d * jnp.where(border, 0.0, jnp.where(kind == other, -2.0 * scale, 2.0 * scale))
    return s, d


def whiten_kernel(me_ref, x_ref, ft_ref, *rest, rb, groups, outs):
    tables, rest = rest[:8], rest[8:]
    o_refs, (g1_ref, g2_ref), stage = rest[:outs], rest[outs:outs + 2], rest[outs + 2:]
    length = x_ref.shape[1]
    half, quarter = length // 2, length // 4

    @pl.when(pl.program_id(0) == 0)
    def _():
        s, d = gains(ft_ref[...], length)
        g1_ref[...] = s
        g2_ref[...] = d

    even, even_t, even_back, even_back_t, odd, odd_t, odd_back, odd_back_t = (ref[...] for ref in tables)

    def right(x, table):
        out = mm(jnp.concatenate(split(x), axis=1), table)
        return out[:, :half] + out[:, half:]

    def left(table, x):
        out = mm(table, jnp.concatenate(split(x), axis=0))
        return out[:half] + out[half:]

    x = x_ref[...].reshape(rb * length, length)
    x0, x1 = x[:, :half], x[:, half:]
    z = jnp.concatenate([right(x0 + x1, even), right(x0 - x1, odd)], axis=1)
    vs = []
    for r in range(rb):
        z0, z1 = z[r * length:r * length + half], z[r * length + half:(r + 1) * length]
        t = jnp.concatenate([left(even_t, z0 + z1), left(odd_t, z0 - z1)], axis=0)
        sw = jnp.concatenate([t[q * quarter:(q + 1) * quarter] for q in (1, 0, 3, 2)], axis=0)
        sw = jnp.concatenate([pltpu.roll(sw[:, :half], quarter, 1), pltpu.roll(sw[:, half:], quarter, 1)], axis=1)
        t = g1_ref[...] * t + g2_ref[...] * sw
        e, o = left(even_back_t, t[:half]), left(odd_back_t, t[half:])
        vs += [e + o, e - o]
    v = jnp.concatenate(vs, axis=0)
    e, o = right(v[:, :half], even_back), right(v[:, half:], odd_back)
    y = jnp.concatenate([e + o, e - o], axis=1)
    rows = length // groups
    target = stage[0] if stage else o_refs[0]
    for r in range(rb):
        for part in range(length // LANES):
            target[:, r, part] = y[r * length:(r + 1) * length, part * LANES:(part + 1) * LANES].reshape(groups, rows, LANES)
    if stage:
        chip = me_ref[0] // 2
        for k, o_ref in enumerate(o_refs[:groups // 4]):
            o_ref[...] = target[pl.ds(2 * (chip ^ k), 2)]
        for way, o_ref in enumerate(o_refs[groups // 4:], groups // 2):
            o_ref[...] = target[pl.ds(me_ref[0] ^ way, 1)]


def whiten(me, x, spectral_filter, groups, start, count, rb, spread):
    length = x.shape[1]
    rows, parts = length // groups, length // LANES
    tables = basis(length)
    const = lambda shape: pl.BlockSpec(shape, lambda i, me: (0,) * len(shape), pipeline_mode=pl.Buffered(1))
    off = start // rb
    leads = [2] * (groups // 4) + [1] * (groups // 2) if spread else [groups]
    scratch = [pltpu.VMEM((length, length), jnp.float32)] * 2
    if spread:
        scratch.append(pltpu.VMEM((groups, rb, parts, rows, LANES), jnp.float32))
    return pl.pallas_call(
        functools.partial(whiten_kernel, rb=rb, groups=groups, outs=len(leads)),
        grid_spec=pltpu.PrefetchScalarGridSpec(
            num_scalar_prefetch=1,
            grid=(count // rb,),
            in_specs=[pl.BlockSpec((rb, length, length), lambda i, me: (i + off, 0, 0)),
                      const((spectral_filter.shape[1], length))] + [const((length, length))] * 8,
            out_specs=[pl.BlockSpec((lead, rb, parts, rows, LANES), lambda i, me: (0, i, 0, 0, 0)) for lead in leads],
            scratch_shapes=scratch,
        ),
        out_shape=[jax.ShapeDtypeStruct((lead, count, parts, rows, LANES), jnp.float32) for lead in leads],
        name="whiten",
    )(me, x, spectral_filter.T, *tables)


def plain_kernel(w_ref, mh_ref, ml_ref, o_ref, *, rows, parts):
    k = mh_ref.shape[1]
    i = pl.program_id(0)
    w = jnp.concatenate([w_ref[pl.ds(p * rows + i, k, stride=rows * parts), :] for p in range(parts)], axis=1)
    wh, wl = split(w)
    o_ref[...] = mm(mh_ref[...], wh) + mm(mh_ref[...], wl) + mm(ml_ref[...], wh)


def plain_solve(w, mh, ml, rows, parts):
    q = mh.shape[0]
    const = lambda a: pl.BlockSpec(a.shape, lambda i: (0,) * a.ndim, pipeline_mode=pl.Buffered(1))
    return pl.pallas_call(
        functools.partial(plain_kernel, rows=rows, parts=parts),
        grid=(rows,),
        in_specs=[const(w), const(mh), const(ml)],
        out_specs=pl.BlockSpec((q, parts * LANES), lambda i: (0, i)),
        out_shape=jax.ShapeDtypeStruct((q, rows * parts * LANES), jnp.float32),
        name="plain",
    )(w, mh, ml)


def whole(shape):
    return pl.BlockSpec(shape, lambda i, me: (0,) * len(shape), pipeline_mode=pl.Buffered(1))


def outside(arrays):
    return [pltpu.with_memory_space_constraint(a, pltpu.HBM) for a in arrays]


def parity(array, flip):
    pick = (lambda i, me: (1 - me[0] % 2, 0, 0)) if flip else (lambda i, me: (me[0] % 2, 0, 0))
    return pl.BlockSpec((None,) + array.shape[1:], pick, pipeline_mode=pl.Buffered(1))


def bundle_kernel(me_ref, *refs):
    size = refs[0].shape[0]
    for j, ref in enumerate(refs[:-1]):
        refs[-1][j * size:(j + 1) * size] = ref[...]


def bundle(me, arrays):
    size = arrays[0].shape[1]
    shape = (len(arrays) * size, LANES)
    return pl.pallas_call(
        bundle_kernel,
        grid_spec=pltpu.PrefetchScalarGridSpec(
            num_scalar_prefetch=1, grid=(1,), in_specs=[parity(a, True) for a in arrays], out_specs=whole(shape)),
        out_shape=jax.ShapeDtypeStruct(shape, jnp.float32),
        name="bundle",
    )(me, *arrays)


def stack(me, arrays):
    rows, lanes = arrays[0].shape
    shape = (len(arrays) * rows, lanes)
    return pl.pallas_call(
        bundle_kernel,
        grid_spec=pltpu.PrefetchScalarGridSpec(
            num_scalar_prefetch=1, grid=(1,), in_specs=[whole(a.shape) for a in arrays], out_specs=whole(shape)),
        out_shape=jax.ShapeDtypeStruct(shape, jnp.float32),
        name="stack",
    )(me, *arrays)


def mix_kernel(me_ref, *refs, top, local, stages):
    orders, (inverse_ref, *papers, theirs_ref) = refs[:2 * stages], refs[2 * stages:-2 * stages - 1]
    o_refs, panel_ref = refs[-2 * stages - 1:-1], refs[-1]
    me = me_ref[0]
    for k, ref in enumerate(papers):
        for c in range(2):
            at = pl.multiple_of(((me ^ (2 * k + c)) & (top - 1)) * local, local)
            panel_ref[pl.ds(at, local), :] = theirs_ref[k * local:(k + 1) * local] if c else ref[...]
    exact = functools.partial(jnp.dot, precision=lax.Precision.HIGHEST, preferred_element_type=jnp.float32)
    first, second = inverse_ref[0], inverse_ref[1]
    below = -exact(second, exact(panel_ref[...], first))
    table = jnp.concatenate([
        jnp.concatenate([first, jnp.zeros_like(first)], axis=1),
        jnp.concatenate([below, second], axis=1)], axis=0)
    pieces = split(table)
    for n in range(stages):
        spot_ref, mask_ref = orders[2 * n:2 * n + 2]
        run = spot_ref[...] ^ ((me * local) & mask_ref[...])
        shape = (table.shape[0], run.shape[1])
        order = lax.broadcasted_iota(jnp.int32, shape, 0) == jnp.broadcast_to(run, shape)
        order = order.astype(jnp.float32).astype(jnp.bfloat16)
        for piece, o_ref in zip(pieces, o_refs[2 * n:2 * n + 2]):
            o_ref[...] = mm(piece, order).astype(jnp.bfloat16)


def mix(me, orders, inverses, papers, theirs, top, local):
    width = inverses.shape[1]
    flat = [table for order in orders for table in order]
    args = [*flat, inverses, *papers, theirs]
    shapes = [(2 * width, table.shape[1]) for table in flat]
    return pl.pallas_call(
        functools.partial(mix_kernel, top=top, local=local, stages=len(orders)),
        grid_spec=pltpu.PrefetchScalarGridSpec(
            num_scalar_prefetch=1, grid=(1,),
            in_specs=[whole(a.shape) for a in args],
            out_specs=[whole(shape) for shape in shapes],
            scratch_shapes=[pltpu.VMEM((width, width), jnp.float32)]),
        out_shape=[jax.ShapeDtypeStruct(shape, jnp.bfloat16) for shape in shapes],
        name="mix",
    )(me, *args)


def solve_kernel(me_ref, *refs, rows, parts, per, sizes, acc):
    n = len(sizes)
    mh_ref, ml_ref = refs[n:n + 2]
    o_ref = refs[-1]
    columns = []
    for g in range(per):
        i = pl.program_id(0) * per + g
        for p in range(parts):
            column = [ref[pl.ds(p * rows + i, k, stride=rows * parts), :] for ref, k in zip(refs, sizes)]
            columns.append(jnp.concatenate(column, axis=0))
    wh, wl = split(jnp.concatenate(columns, axis=1))
    mh = mh_ref[...]
    both = mm(jnp.concatenate([mh, ml_ref[...]], axis=0), wh)
    out = both[:mh.shape[0]] + both[mh.shape[0]:] + mm(mh, wl)
    o_ref[...] = out + refs[n + 2][...] if acc else out


def solve(me, pieces, tables, rows, parts, acc=None):
    each = rows * parts
    per = max(d for d in (4, 2, 1) if rows % d == 0)
    width = tables[0].shape[0]
    sizes = [a.shape[-2] // each for a in pieces]
    args = [*pieces, *outside(tables)]
    specs = [parity(a, False) if a.ndim == 3 else whole(a.shape) for a in args]
    tile = pl.BlockSpec((width, per * parts * LANES), lambda i, me: (0, i))
    if acc is not None:
        args.append(acc)
        specs.append(tile)
    return pl.pallas_call(
        functools.partial(solve_kernel, rows=rows, parts=parts, per=per, sizes=tuple(sizes), acc=acc is not None),
        grid_spec=pltpu.PrefetchScalarGridSpec(
            num_scalar_prefetch=1, grid=(rows // per,), in_specs=specs, out_specs=tile),
        out_shape=jax.ShapeDtypeStruct((width, each * LANES), jnp.float32),
        input_output_aliases={} if acc is None else {len(args): 0},
        compiler_params=None if acc is None else pltpu.CompilerParams(vmem_limit_bytes=24 << 20),
        name="solve",
    )(me, *args)


def precise_dot(a, b):
    return jnp.dot(a, b, precision=lax.Precision.HIGHEST, preferred_element_type=jnp.float32)


def split_outside(x):
    hi = lax.reduce_precision(x, 8, 7)
    return hi.astype(jnp.bfloat16), (x - hi).astype(jnp.bfloat16)


def mixing(block_inverses, panels, total):
    width = block_inverses.shape[1]
    first, second = block_inverses[0], block_inverses[1]
    below = -precise_dot(second, precise_dot(panels[0, width : 2 * width], first))
    top = jnp.concatenate([first, jnp.zeros_like(first)], axis=1)
    rows = [top, jnp.concatenate([below, second], axis=1)]
    if total > 2 * width:
        left, right = panels[0, 2 * width :], panels[1, 2 * width :]
        rows.append(
            -jnp.concatenate(
                [precise_dot(left, first) + precise_dot(right, below), precise_dot(right, second)],
                axis=1,
            )
        )
    return jnp.concatenate(rows, axis=0)


HEAD = 4
SOON = 6
NEAR_SOON = 5


def exchange(x, offset):
    pairs = [(i, i ^ offset) for i in range(lax.axis_size("dev"))]
    return lax.ppermute(x, "dev", pairs)


def general(me, runs_field, spectral_filter, block_inverses, factor_panels):
    groups = lax.axis_size("dev")
    local, length, _ = runs_field.shape
    total = local * groups
    front = 2 * block_inverses.shape[1]
    rows, parts = length // groups, length // LANES
    (pieces,) = whiten(me, runs_field, spectral_filter, groups, 0, local, HEAD, False)
    runs = lax.all_to_all(pieces, "dev", 0, 0, tiled=True).reshape(total, parts, rows, LANES)
    panels = lax.all_gather(factor_panels, "dev", axis=1, tiled=True)
    tables = split_outside(mixing(block_inverses, panels, total))
    out = plain_solve(runs[:front].reshape(-1, LANES), *tables, rows, parts)
    if total > front:
        below = jnp.moveaxis(runs[front:], 1, 2).reshape(total - front, -1)
        out = jnp.concatenate([out[:front], out[front:] + below], axis=0)
    return out


def places(groups, local):
    top = groups // 2
    rest = range(HEAD, local)
    head = [(source * local + r, 0) for source in range(groups) for r in range(HEAD)]
    ways = lambda picks: [(way * local + r, -1) for way in picks for r in rest]
    near, far = list(range(0, top, 2)), list(range(top, groups))
    soon = head + ways(near[:NEAR_SOON]) + ways(far[:SOON])
    last = ways(range(1, top, 2)) + ways(near[NEAR_SOON:]) + ways(far[SOON:])
    return [np.array(stage, np.int32).T.reshape(2, 1, -1) for stage in (soon, last)]


def per_device(runs_field, spectral_filter, block_inverses, factor_panels):
    groups = lax.axis_size("dev")
    place = lax.axis_index("dev")
    local, length, _ = runs_field.shape
    width = block_inverses.shape[1]
    rows, parts = length // groups, length // LANES
    chips, top = groups // 2, groups // 2
    me = place.astype(jnp.int32).reshape(1)
    if local * groups != 2 * width:
        return general(me, runs_field, spectral_filter, block_inverses, factor_panels)
    rest = local - HEAD
    near = list(range(1, chips // 2))
    mine = jnp.where(place < top, exchange(factor_panels, top)[0], factor_panels[0])
    (head,) = whiten(me, runs_field, spectral_filter, groups, 0, HEAD, HEAD, False)
    head = lax.all_to_all(head, "dev", 0, 0, tiled=True)
    outs = whiten(me, runs_field, spectral_filter, groups, HEAD, rest, HEAD, True)
    got = [outs[0].reshape(2, -1, LANES)]
    papers = [mine]
    for k in near:
        papers.append(exchange(mine, 2 * k))
    for k in near:
        got.append(exchange(outs[k].reshape(2, -1, LANES), 2 * k))
    direct = []
    for way in range(top, groups):
        direct.append(exchange(outs[way - chips // 2].reshape(-1, LANES), way))
    theirs = exchange(stack(me, papers), 1)
    tables = mix(me, places(groups, local), block_inverses, papers, theirs, top, local)
    load = bundle(me, got)
    load = exchange(load, 1)
    out = solve(me, outside([head.reshape(-1, LANES), *got[:NEAR_SOON], *direct[:SOON]]), tables[:2], rows, parts)
    return solve(me, [load, *outside(got[NEAR_SOON:]), *direct[SOON:]], tables[2:], rows, parts, out)


def solution(mesh):
    return jax.shard_map(
        per_device,
        mesh=mesh,
        in_specs=(P("dev", None, None), P(), P(), P(None, "dev", None)),
        out_specs=P(None, "dev"),
        check_vma=False,
    )
```

```python
import functools, math
LANES = 128
import numpy as np
import jax, jax.numpy as jnp
from jax import lax
from jax.experimental import pallas as pl
from jax.experimental.pallas import tpu as pltpu
from jax.sharding import PartitionSpec as P


def basis(length):
    half, quarter = length // 2, length // 4
    slot = np.arange(half)
    tables = []
    for freq, cosine in (
        (np.where(slot <= quarter, 2 * slot, 2 * slot - half), slot <= quarter),
        (2 * (slot % quarter) + 1, slot < quarter),
    ):
        angle = (np.outer(np.arange(half), freq) % length) * (2.0 * math.pi / length)
        table = np.where(cosine[None, :], np.cos(angle), np.sin(angle))
        hi = table.astype(jnp.bfloat16)
        lo = (table - hi.astype(np.float64)).astype(jnp.bfloat16)
        ahead = np.block([[hi, lo], [hi, lo]])
        back = np.block([[hi.T, lo.T], [hi.T, lo.T]])
        tables += [ahead, ahead.T, back, back.T]
    return tables


def split(x):
    hi = x.astype(jnp.bfloat16)
    lo = (x - hi.astype(jnp.float32)).astype(jnp.bfloat16)
    return hi, lo


def mm(a, b):
    return lax.dot_general(a, b, (((1,), (0,)), ((), ())), preferred_element_type=jnp.float32)


def exact_pick(sel, table, dims):
    out, rest = None, table
    for _ in range(3):
        piece = rest.astype(jnp.bfloat16)
        rest = rest - piece.astype(jnp.float32)
        part = lax.dot_general(sel, piece, (dims, ((), ())), preferred_element_type=jnp.float32)
        out = part if out is None else out + part
    return out


def frequency(slot, length):
    half, quarter = length // 2, length // 4
    within = slot & (half - 1)
    even = jnp.where(within <= quarter, 2 * within, 2 * within - half)
    odd = 2 * (slot & (quarter - 1)) + 1
    return jnp.where(slot < half, even, odd), within < quarter


def gains(filter_t, length):
    half = length // 2
    row = lax.broadcasted_iota(jnp.int32, (length, length), 0)
    col = lax.broadcasted_iota(jnp.int32, (length, length), 1)
    freq, kind = frequency(row, length)
    edge = (freq == 0) | (freq == half)
    plus = (col == freq).astype(jnp.float32)
    minus = jnp.where(edge, 0.0, (col == length - freq).astype(jnp.float32))
    sums = (plus + minus).astype(jnp.bfloat16)
    diffs = (jnp.where(edge, 0.0, plus) - minus).astype(jnp.bfloat16)
    table = exact_pick(plus[:, :half].astype(jnp.bfloat16), filter_t[:half], ((1,), (0,)))
    table = jnp.where(freq == half, jnp.broadcast_to(filter_t[half:half + 1], table.shape), table)
    both = exact_pick(jnp.concatenate([sums, diffs], axis=0), table, ((1,), (1,)))
    s, d = both[:length], both[length:]
    across, other = frequency(col, length)
    border = (across == 0) | (across == half)
    scale = 1.0 / float(length * length)
    s = s * jnp.where(border, scale, 2.0 * scale)
    d = d * jnp.where(border, 0.0, jnp.where(kind == other, -2.0 * scale, 2.0 * scale))
    return s, d


def whiten_kernel(me_ref, x_ref, ft_ref, *rest, rb, groups, outs):
    tables, rest = rest[:8], rest[8:]
    o_refs, (g1_ref, g2_ref), stage = rest[:outs], rest[outs:outs + 2], rest[outs + 2:]
    length = x_ref.shape[1]
    half, quarter = length // 2, length // 4

    @pl.when(pl.program_id(0) == 0)
    def _():
        s, d = gains(ft_ref[...], length)
        g1_ref[...] = s
        g2_ref[...] = d

    even, even_t, even_back, even_back_t, odd, odd_t, odd_back, odd_back_t = (ref[...] for ref in tables)

    def right(x, table):
        out = mm(jnp.concatenate(split(x), axis=1), table)
        return out[:, :half] + out[:, half:]

    def left(table, x):
        out = mm(table, jnp.concatenate(split(x), axis=0))
        return out[:half] + out[half:]

    x = x_ref[...].reshape(rb * length, length)
    x0, x1 = x[:, :half], x[:, half:]
    z = jnp.concatenate([right(x0 + x1, even), right(x0 - x1, odd)], axis=1)
    vs = []
    for r in range(rb):
        z0, z1 = z[r * length:r * length + half], z[r * length + half:(r + 1) * length]
        t = jnp.concatenate([left(even_t, z0 + z1), left(odd_t, z0 - z1)], axis=0)
        sw = jnp.concatenate([t[q * quarter:(q + 1) * quarter] for q in (1, 0, 3, 2)], axis=0)
        sw = jnp.concatenate([pltpu.roll(sw[:, :half], quarter, 1), pltpu.roll(sw[:, half:], quarter, 1)], axis=1)
        t = g1_ref[...] * t + g2_ref[...] * sw
        e, o = left(even_back_t, t[:half]), left(odd_back_t, t[half:])
        vs += [e + o, e - o]
    v = jnp.concatenate(vs, axis=0)
    e, o = right(v[:, :half], even_back), right(v[:, half:], odd_back)
    y = jnp.concatenate([e + o, e - o], axis=1)
    rows = length // groups
    target = stage[0] if stage else o_refs[0]
    for r in range(rb):
        for part in range(length // LANES):
            target[:, r, part] = y[r * length:(r + 1) * length, part * LANES:(part + 1) * LANES].reshape(groups, rows, LANES)
    if stage:
        chip = me_ref[0] // 2
        for k, o_ref in enumerate(o_refs[:groups // 4]):
            o_ref[...] = target[pl.ds(2 * (chip ^ k), 2)]
        for way, o_ref in enumerate(o_refs[groups // 4:], groups // 2):
            o_ref[...] = target[pl.ds(me_ref[0] ^ way, 1)]


def whiten(me, x, spectral_filter, groups, start, count, rb, spread):
    length = x.shape[1]
    rows, parts = length // groups, length // LANES
    tables = basis(length)
    const = lambda shape: pl.BlockSpec(shape, lambda i, me: (0,) * len(shape), pipeline_mode=pl.Buffered(1))
    off = start // rb
    leads = [2] * (groups // 4) + [1] * (groups // 2) if spread else [groups]
    scratch = [pltpu.VMEM((length, length), jnp.float32)] * 2
    if spread:
        scratch.append(pltpu.VMEM((groups, rb, parts, rows, LANES), jnp.float32))
    return pl.pallas_call(
        functools.partial(whiten_kernel, rb=rb, groups=groups, outs=len(leads)),
        grid_spec=pltpu.PrefetchScalarGridSpec(
            num_scalar_prefetch=1,
            grid=(count // rb,),
            in_specs=[pl.BlockSpec((rb, length, length), lambda i, me: (i + off, 0, 0)),
                      const((spectral_filter.shape[1], length))] + [const((length, length))] * 8,
            out_specs=[pl.BlockSpec((lead, rb, parts, rows, LANES), lambda i, me: (0, i, 0, 0, 0)) for lead in leads],
            scratch_shapes=scratch,
        ),
        out_shape=[jax.ShapeDtypeStruct((lead, count, parts, rows, LANES), jnp.float32) for lead in leads],
        name="whiten",
    )(me, x, spectral_filter.T, *tables)


def plain_kernel(w_ref, mh_ref, ml_ref, o_ref, *, rows, parts):
    k = mh_ref.shape[1]
    i = pl.program_id(0)
    w = jnp.concatenate([w_ref[pl.ds(p * rows + i, k, stride=rows * parts), :] for p in range(parts)], axis=1)
    wh, wl = split(w)
    o_ref[...] = mm(mh_ref[...], wh) + mm(mh_ref[...], wl) + mm(ml_ref[...], wh)


def plain_solve(w, mh, ml, rows, parts):
    q = mh.shape[0]
    const = lambda a: pl.BlockSpec(a.shape, lambda i: (0,) * a.ndim, pipeline_mode=pl.Buffered(1))
    return pl.pallas_call(
        functools.partial(plain_kernel, rows=rows, parts=parts),
        grid=(rows,),
        in_specs=[const(w), const(mh), const(ml)],
        out_specs=pl.BlockSpec((q, parts * LANES), lambda i: (0, i)),
        out_shape=jax.ShapeDtypeStruct((q, rows * parts * LANES), jnp.float32),
        name="plain",
    )(w, mh, ml)


def whole(shape):
    return pl.BlockSpec(shape, lambda i, me: (0,) * len(shape), pipeline_mode=pl.Buffered(1))


def outside(arrays):
    return [pltpu.with_memory_space_constraint(a, pltpu.HBM) for a in arrays]


def parity(array, flip):
    pick = (lambda i, me: (1 - me[0] % 2, 0, 0)) if flip else (lambda i, me: (me[0] % 2, 0, 0))
    return pl.BlockSpec((None,) + array.shape[1:], pick, pipeline_mode=pl.Buffered(1))


def bundle_kernel(me_ref, *refs):
    size = refs[0].shape[0]
    for j, ref in enumerate(refs[:-1]):
        refs[-1][j * size:(j + 1) * size] = ref[...]


def bundle(me, arrays):
    size = arrays[0].shape[1]
    shape = (len(arrays) * size, LANES)
    return pl.pallas_call(
        bundle_kernel,
        grid_spec=pltpu.PrefetchScalarGridSpec(
            num_scalar_prefetch=1, grid=(1,), in_specs=[parity(a, True) for a in arrays], out_specs=whole(shape)),
        out_shape=jax.ShapeDtypeStruct(shape, jnp.float32),
        name="bundle",
    )(me, *arrays)


def stack(me, arrays):
    rows, lanes = arrays[0].shape
    shape = (len(arrays) * rows, lanes)
    return pl.pallas_call(
        bundle_kernel,
        grid_spec=pltpu.PrefetchScalarGridSpec(
            num_scalar_prefetch=1, grid=(1,), in_specs=[whole(a.shape) for a in arrays], out_specs=whole(shape)),
        out_shape=jax.ShapeDtypeStruct(shape, jnp.float32),
        name="stack",
    )(me, *arrays)


def mix_kernel(me_ref, *refs, top, local, stages):
    orders, (inverse_ref, *papers, theirs_ref) = refs[:2 * stages], refs[2 * stages:-2 * stages - 1]
    o_refs, panel_ref = refs[-2 * stages - 1:-1], refs[-1]
    me = me_ref[0]
    for k, ref in enumerate(papers):
        for c in range(2):
            at = pl.multiple_of(((me ^ (2 * k + c)) & (top - 1)) * local, local)
            panel_ref[pl.ds(at, local), :] = theirs_ref[k * local:(k + 1) * local] if c else ref[...]
    exact = functools.partial(jnp.dot, precision=lax.Precision.HIGHEST, preferred_element_type=jnp.float32)
    first, second = inverse_ref[0], inverse_ref[1]
    below = -exact(second, exact(panel_ref[...], first))
    table = jnp.concatenate([
        jnp.concatenate([first, jnp.zeros_like(first)], axis=1),
        jnp.concatenate([below, second], axis=1)], axis=0)
    pieces = split(table)
    for n in range(stages):
        spot_ref, mask_ref = orders[2 * n:2 * n + 2]
        run = spot_ref[...] ^ ((me * local) & mask_ref[...])
        shape = (table.shape[0], run.shape[1])
        order = lax.broadcasted_iota(jnp.int32, shape, 0) == jnp.broadcast_to(run, shape)
        order = order.astype(jnp.float32).astype(jnp.bfloat16)
        for piece, o_ref in zip(pieces, o_refs[2 * n:2 * n + 2]):
            o_ref[...] = mm(piece, order).astype(jnp.bfloat16)


def mix(me, orders, inverses, papers, theirs, top, local):
    width = inverses.shape[1]
    flat = [table for order in orders for table in order]
    args = [*flat, inverses, *papers, theirs]
    shapes = [(2 * width, table.shape[1]) for table in flat]
    return pl.pallas_call(
        functools.partial(mix_kernel, top=top, local=local, stages=len(orders)),
        grid_spec=pltpu.PrefetchScalarGridSpec(
            num_scalar_prefetch=1, grid=(1,),
            in_specs=[whole(a.shape) for a in args],
            out_specs=[whole(shape) for shape in shapes],
            scratch_shapes=[pltpu.VMEM((width, width), jnp.float32)]),
        out_shape=[jax.ShapeDtypeStruct(shape, jnp.bfloat16) for shape in shapes],
        name="mix",
    )(me, *args)


def solve_kernel(me_ref, *refs, rows, parts, per, sizes, acc):
    n = len(sizes)
    mh_ref, ml_ref = refs[n:n + 2]
    o_ref = refs[-1]
    columns = []
    for g in range(per):
        i = pl.program_id(0) * per + g
        for p in range(parts):
            column = [ref[pl.ds(p * rows + i, k, stride=rows * parts), :] for ref, k in zip(refs, sizes)]
            columns.append(jnp.concatenate(column, axis=0))
    wh, wl = split(jnp.concatenate(columns, axis=1))
    mh, ml = mh_ref[...], ml_ref[...]
    out = mm(mh, wh) + mm(mh, wl) + mm(ml, wh)
    o_ref[...] = out + refs[n + 2][...] if acc else out


def solve(me, pieces, tables, rows, parts, acc=None):
    each = rows * parts
    per = max(d for d in (4, 2, 1) if rows % d == 0)
    width = tables[0].shape[0]
    sizes = [a.shape[-2] // each for a in pieces]
    args = [*pieces, *outside(tables)]
    specs = [parity(a, False) if a.ndim == 3 else whole(a.shape) for a in args]
    tile = pl.BlockSpec((width, per * parts * LANES), lambda i, me: (0, i))
    if acc is not None:
        args.append(acc)
        specs.append(tile)
    return pl.pallas_call(
        functools.partial(solve_kernel, rows=rows, parts=parts, per=per, sizes=tuple(sizes), acc=acc is not None),
        grid_spec=pltpu.PrefetchScalarGridSpec(
            num_scalar_prefetch=1, grid=(rows // per,), in_specs=specs, out_specs=tile),
        out_shape=jax.ShapeDtypeStruct((width, each * LANES), jnp.float32),
        input_output_aliases={} if acc is None else {len(args): 0},
        compiler_params=None if acc is None else pltpu.CompilerParams(vmem_limit_bytes=24 << 20),
        name="solve",
    )(me, *args)


def precise_dot(a, b):
    return jnp.dot(a, b, precision=lax.Precision.HIGHEST, preferred_element_type=jnp.float32)


def split_outside(x):
    hi = lax.reduce_precision(x, 8, 7)
    return hi.astype(jnp.bfloat16), (x - hi).astype(jnp.bfloat16)


def mixing(block_inverses, panels, total):
    width = block_inverses.shape[1]
    first, second = block_inverses[0], block_inverses[1]
    below = -precise_dot(second, precise_dot(panels[0, width : 2 * width], first))
    top = jnp.concatenate([first, jnp.zeros_like(first)], axis=1)
    rows = [top, jnp.concatenate([below, second], axis=1)]
    if total > 2 * width:
        left, right = panels[0, 2 * width :], panels[1, 2 * width :]
        rows.append(
            -jnp.concatenate(
                [precise_dot(left, first) + precise_dot(right, below), precise_dot(right, second)],
                axis=1,
            )
        )
    return jnp.concatenate(rows, axis=0)


HEAD = 4
SOON = 6
NEAR_SOON = 5


def exchange(x, offset):
    pairs = [(i, i ^ offset) for i in range(lax.axis_size("dev"))]
    return lax.ppermute(x, "dev", pairs)


def general(me, runs_field, spectral_filter, block_inverses, factor_panels):
    groups = lax.axis_size("dev")
    local, length, _ = runs_field.shape
    total = local * groups
    front = 2 * block_inverses.shape[1]
    rows, parts = length // groups, length // LANES
    (pieces,) = whiten(me, runs_field, spectral_filter, groups, 0, local, HEAD, False)
    runs = lax.all_to_all(pieces, "dev", 0, 0, tiled=True).reshape(total, parts, rows, LANES)
    panels = lax.all_gather(factor_panels, "dev", axis=1, tiled=True)
    tables = split_outside(mixing(block_inverses, panels, total))
    out = plain_solve(runs[:front].reshape(-1, LANES), *tables, rows, parts)
    if total > front:
        below = jnp.moveaxis(runs[front:], 1, 2).reshape(total - front, -1)
        out = jnp.concatenate([out[:front], out[front:] + below], axis=0)
    return out


def places(groups, local):
    top = groups // 2
    rest = range(HEAD, local)
    head = [(source * local + r, 0) for source in range(groups) for r in range(HEAD)]
    ways = lambda picks: [(way * local + r, -1) for way in picks for r in rest]
    near, far = list(range(0, top, 2)), list(range(top, groups))
    soon = head + ways(near[:NEAR_SOON]) + ways(far[:SOON])
    last = ways(range(1, top, 2)) + ways(near[NEAR_SOON:]) + ways(far[SOON:])
    return [np.array(stage, np.int32).T.reshape(2, 1, -1) for stage in (soon, last)]


def per_device(runs_field, spectral_filter, block_inverses, factor_panels):
    groups = lax.axis_size("dev")
    place = lax.axis_index("dev")
    local, length, _ = runs_field.shape
    width = block_inverses.shape[1]
    rows, parts = length // groups, length // LANES
    chips, top = groups // 2, groups // 2
    me = place.astype(jnp.int32).reshape(1)
    if local * groups != 2 * width:
        return general(me, runs_field, spectral_filter, block_inverses, factor_panels)
    rest = local - HEAD
    near = list(range(1, chips // 2))
    mine = jnp.where(place < top, exchange(factor_panels, top)[0], factor_panels[0])
    (head,) = whiten(me, runs_field, spectral_filter, groups, 0, HEAD, HEAD, False)
    head = lax.all_to_all(head, "dev", 0, 0, tiled=True)
    outs = whiten(me, runs_field, spectral_filter, groups, HEAD, rest, HEAD, True)
    got = [outs[0].reshape(2, -1, LANES)]
    papers = [mine]
    for k in near:
        papers.append(exchange(mine, 2 * k))
    for k in near:
        got.append(exchange(outs[k].reshape(2, -1, LANES), 2 * k))
    direct = []
    for way in range(top, groups):
        direct.append(exchange(outs[way - chips // 2].reshape(-1, LANES), way))
    theirs = exchange(stack(me, papers), 1)
    tables = mix(me, places(groups, local), block_inverses, papers, theirs, top, local)
    load = bundle(me, got)
    load = exchange(load, 1)
    out = solve(me, outside([head.reshape(-1, LANES), *got[:NEAR_SOON], *direct[:SOON]]), tables[:2], rows, parts)
    return solve(me, [load, *outside(got[NEAR_SOON:]), *direct[SOON:]], tables[2:], rows, parts, out)


def solution(mesh):
    return jax.shard_map(
        per_device,
        mesh=mesh,
        in_specs=(P("dev", None, None), P(), P(), P(None, "dev", None)),
        out_specs=P(None, "dev"),
        check_vma=False,
    )
```
